32 devices in a mesh: dp: 8 (over z, x), tensor: 4 (over y, core).
Axes of the slice: x: 2, y: 2, z: 4, core: 2. Of those that a mesh axis runs over, the one named last changes fastest.
Arguments:
- hidden: bfloat16 [2048, 2048], P('dp'), may hold values from -200 to 200
- norm_gain: float32 [2048], replicated, may hold values from 0.5 to 2
- expert_ids: int32 [2048, 8], P(('dp', 'tensor')), may hold values from 0 to 31, all different within a row; in each aligned block of 64 rows (0 to 63, 64 to 127, ...) at most 32 rows name the same one
- gate_probs: float32 [2048, 8], P(('dp', 'tensor')), may hold values from 0.05 to 0.5
- out_grad: bfloat16 [2048, 2048], P(('dp', 'tensor')), may hold values from -8 to 8
- gate_weight: bfloat16 [32, 2048, 768], P(('dp', 'tensor')), may hold values from -0.125 to 0.125
- up_weight: bfloat16 [32, 2048, 768], P(('dp', 'tensor')), may hold values from -0.125 to 0.125
- down_weight: bfloat16 [32, 768, 2048], P(('dp', 'tensor')), may hold values from -0.21875 to 0.21875
Outputs:
- layer_out: bfloat16 [2048, 2048], P(('dp', 'tensor'))
- input_grad: bfloat16 [2048, 2048], P('dp')
- gate_grad: float32 [2048, 8], P(('dp', 'tensor'))
- gain_grad: float32 [2048], replicated
- gate_weight_grad: bfloat16 [32, 2048, 768], P(('dp', 'tensor'))
- up_weight_grad: bfloat16 [32, 2048, 768], P(('dp', 'tensor'))
- down_weight_grad: bfloat16 [32, 768, 2048], P(('dp', 'tensor'))
The draws below stay inside these ranges and needn't reach their ends.
Inputs may be any that keep to these rules, and one draw needn't show every extreme that they name: `expert_ids`: within the rows of one device no expert is named by more than 32 rows, a bound that some block reaches.
All inputs are finite; a program needn't handle non-finite values.
Results may differ from the reference program's by a relative error of at most 0.0072.
Values may be sent and summed in bfloat16 or wider, within the bound.
A program may use at most 128 MiB of HBM per device.

```python
import math
import jax
import jax.numpy as jnp
import numpy as np
from jax import lax

D = 2048
FF = 768
TOPK = 8
EXPERTS = 32
TOKENS = 2048
ROWS_DEV = 64
CAP = 32
SLOTS = 1024


def draw_hidden(key, part):
    first, second, third = jax.random.split(key, 3)
    row_scale = jnp.exp(jax.random.uniform(first, (TOKENS, 1), jnp.float32, 0.0, math.log(10.0)))
    col_scale = jnp.exp(jax.random.uniform(second, (1, D), jnp.float32, 0.0, math.log(10.0)))
    base = jnp.clip(jax.random.normal(third, (TOKENS, D), jnp.float32), -6.0, 6.0)
    return (0.3 * base * row_scale * col_scale).astype(jnp.bfloat16)


def draw_out_grad(key, part):
    first = jax.random.fold_in(key, 0)
    ramp = jnp.arange(TOKENS, dtype=jnp.float32)[:, None] / float(max(TOKENS - 1, 1))
    rising = jnp.exp(math.log(3.0) * ramp)
    base = jnp.clip(jax.random.normal(first, (TOKENS, D), jnp.float32), -6.0, 6.0)
    return (0.3 * base * rising).astype(jnp.bfloat16)


def block_scale(own_key, dims, cuts, smallest, top_value):
    def one(dim, parts):
        steps = jax.random.uniform(jax.random.fold_in(jax.random.fold_in(own_key, 6), dim), (parts,), jnp.float32, smallest / len(cuts), top_value / len(cuts))
        return jnp.repeat(jnp.exp(steps), dims[dim] // parts).reshape((-1,) + (1,) * (len(dims) - dim - 1))

    gain = one(*cuts[0])
    for cut in cuts[1:]:
        gain = gain * one(*cut)
    return gain


def shared_out(own_key, own, number, rows, number_of, top, limit, lean):
    ranking = jax.random.permutation(own_key, number_of)
    heavy_load, usual = portions_of(number_of, rows * top, limit, lean, True), portions_of(number_of, rows * top, limit, lean, False)
    places = jnp.arange(number_of)

    def named(tallies, offset_by):
        used = int((tallies > 0).sum())
        fixed = max(1, used // 4)
        passed = fixed + (places - fixed + offset_by * (used - fixed)) % max(1, number_of - fixed)
        return jnp.zeros((number_of,), jnp.int32).at[ranking[jnp.where(places < fixed, places, passed)]].set(jnp.asarray(tallies, jnp.int32))

    tallies = jnp.where(number % 4 == 0, named(heavy_load, number // 4), named(usual, number - number // 4 - 1))
    mixed = jax.random.permutation(jax.random.fold_in(own, 3), number_of)
    source_of, receiver = mixed[0:number_of // 2 * 2:2], mixed[1:number_of // 2 * 2:2]
    slack = jnp.minimum(tallies[source_of] - 1, limit - tallies[receiver]) // 2
    slack = jnp.where((source_of == ranking[0]) | (receiver == ranking[0]) | (tallies[receiver] == 0), 0, jnp.maximum(slack, 0))
    passed = jax.random.randint(jax.random.fold_in(own, 4), (number_of // 2,), 0, 1 << 20) % (slack + 1)
    tallies = tallies.at[source_of].add(-passed).at[receiver].add(passed)
    labels = jnp.searchsorted(jnp.cumsum(tallies), jnp.arange(rows * top), side="right").astype(jnp.int32)
    listing = labels.reshape(top, rows).T
    listing = listing[jax.random.permutation(jax.random.fold_in(own, 1), rows)]
    offset_by = jax.random.randint(jax.random.fold_in(own, 2), (rows, 1), 0, top)
    return jnp.take_along_axis(listing, (jnp.arange(top)[None, :] + offset_by) % top, axis=1)


def portions_of(amount, total, reach, lean, full):
    portions = [(1 << 20) // math.isqrt(grade ** lean) + 1 for grade in range(1, amount + 1)]
    largest = reach if full else min(reach, max(-(-total // amount), total * portions[0] // sum(portions)))
    least = 1 if total - largest >= amount - 1 else 0
    counts, surplus = [largest] + [least] * (amount - 1), total - largest - least * (amount - 1)
    while surplus > 0:
        free = [i for i in range(1, amount) if counts[i] < largest] or [i for i in range(1, amount) if counts[i] < reach]
        whole, remaining = sum([portions[i] for i in free]), surplus
        for i in free:
            more = min(reach - counts[i], max(1, remaining * portions[i] // whole), surplus)
            counts[i] = counts[i] + more
            surplus = surplus - more
    return np.array(counts)


def scatter_about(key, extent, width, most, shards=(), kind=jnp.bfloat16):
    values = width * jax.random.normal(key, extent, jnp.float32)
    if shards:
        values = values * block_scale(key, extent, shards, -0.22, 0.18)
    return jnp.clip(values, -most, most).astype(kind)


def setup_inputs(seed: int = 0) -> dict:
    key_list = jax.random.split(jax.random.key(seed), 9)
    hidden = draw_hidden(jax.random.fold_in(key_list[8], 71), 0)
    norm_gain = jnp.clip(jnp.exp(jax.random.uniform(key_list[1], (D,), jnp.float32, math.log(0.5), math.log(2.0))), 0.5, 2.0)
    expert_ids_keys = jax.random.split(jax.random.fold_in(key_list[2], 1), TOKENS // ROWS_DEV)
    expert_ids_turns = jax.random.permutation(jax.random.fold_in(key_list[2], 3), TOKENS // ROWS_DEV)
    expert_ids = jax.vmap(lambda own, number: shared_out(jax.random.fold_in(key_list[2], 2), own, number, ROWS_DEV, EXPERTS, TOPK, CAP, 2))(expert_ids_keys, expert_ids_turns).reshape((TOKENS, TOPK))
    gate_probs = jnp.clip(jnp.exp(math.log(0.5) - 2.3025851 * jax.random.uniform(key_list[3], (TOKENS, TOPK), jnp.float32) ** block_scale(key_list[3], (TOKENS, TOPK), ((0, 32),), -0.2, 0.2)), 0.05, 0.5)
    out_grad = draw_out_grad(jax.random.fold_in(key_list[8], 71), 0)
    gate_weight = scatter_about(key_list[5], (EXPERTS, D, FF), D ** -0.5, 0.125, ((0, 32),))
    up_weight = scatter_about(key_list[6], (EXPERTS, D, FF), D ** -0.5, 0.125, ((0, 32),))
    down_weight = scatter_about(key_list[7], (EXPERTS, FF, D), FF ** -0.5, 0.21875, ((0, 32),))
    return {"hidden": hidden, "norm_gain": norm_gain, "expert_ids": expert_ids, "gate_probs": gate_probs, "out_grad": out_grad, "gate_weight": gate_weight, "up_weight": up_weight, "down_weight": down_weight}


epsilon = 1e-06

def reference(hidden, norm_gain, expert_ids, gate_probs, out_grad, gate_weight, up_weight, down_weight):
    values = hidden.astype(jnp.float32)
    inverse = lax.rsqrt(lax.optimization_barrier(jnp.mean(values * values, axis=-1, keepdims=True)) + epsilon)
    unit_rows = values * inverse
    normed = (unit_rows * norm_gain).astype(jnp.bfloat16)
    grad_rows = out_grad.astype(jnp.float32)
    scaled = (gate_probs[:, :, None] * grad_rows[:, None, :]).astype(jnp.bfloat16)
    total_pairs = TOKENS * TOPK
    flat_ids = expert_ids.reshape(-1).astype(jnp.int32)
    normed_pad = jnp.concatenate([normed, jnp.zeros((1, D), jnp.bfloat16)], axis=0)
    scaled_pad = jnp.concatenate([scaled.reshape(total_pairs, D), jnp.zeros((1, D), jnp.bfloat16)], axis=0)

    def single(operands):
        expert, w_gate, w_up, w_down = operands
        found = jnp.nonzero(flat_ids == expert, size=SLOTS, fill_value=total_pairs)[0].astype(jnp.int32)
        token = jnp.where(found < total_pairs, found // TOPK, TOKENS).astype(jnp.int32)
        inputs = normed_pad[token]
        cotan = scaled_pad[found]
        gate_pre = jnp.dot(inputs, w_gate, preferred_element_type=jnp.float32)
        up_pre = jnp.dot(inputs, w_up, preferred_element_type=jnp.float32)
        sigma = jax.nn.sigmoid(gate_pre)
        silu_vals = gate_pre * sigma
        act = (silu_vals * up_pre).astype(jnp.bfloat16)
        result = jnp.dot(act, w_down, preferred_element_type=jnp.float32).astype(jnp.bfloat16)
        act_grad = jnp.dot(cotan, w_down.T, preferred_element_type=jnp.float32)
        gate_pgrad = (act_grad * up_pre * sigma * (1.0 + gate_pre * (1.0 - sigma))).astype(jnp.bfloat16)
        up_pgrad = (act_grad * silu_vals).astype(jnp.bfloat16)
        down_g = jnp.dot(act.T, cotan, preferred_element_type=jnp.float32).astype(jnp.bfloat16)
        gate_g = jnp.dot(inputs.T, gate_pgrad, preferred_element_type=jnp.float32).astype(jnp.bfloat16)
        up_g = jnp.dot(inputs.T, up_pgrad, preferred_element_type=jnp.float32).astype(jnp.bfloat16)
        back = jnp.dot(gate_pgrad, w_gate.T, preferred_element_type=jnp.float32)
        back = back + jnp.dot(up_pgrad, w_up.T, preferred_element_type=jnp.float32)
        return (result, back.astype(jnp.bfloat16), found, gate_g, up_g, down_g)
    numbers = jnp.arange(EXPERTS, dtype=jnp.int32)
    results, backs, founds, gate_g, up_g, down_g = lax.map(single, (numbers, gate_weight, up_weight, down_weight))
    where_all = founds.reshape(-1).astype(jnp.int32)
    out_rows = jnp.zeros((total_pairs + 1, D), jnp.bfloat16).at[where_all].set(results.reshape(-1, D))
    out_rows = out_rows[:total_pairs].reshape(TOKENS, TOPK, D)
    back_rows = jnp.zeros((total_pairs + 1, D), jnp.bfloat16).at[where_all].set(backs.reshape(-1, D))
    back_rows = back_rows[:total_pairs].reshape(TOKENS, TOPK, D)
    out_f = out_rows.astype(jnp.float32)
    layer_out = (values + lax.optimization_barrier(jnp.sum(gate_probs[:, :, None] * out_f, axis=1))).astype(jnp.bfloat16)
    gate_grad = lax.optimization_barrier(jnp.sum(grad_rows[:, None, :] * out_f, axis=2))
    normed_total = lax.optimization_barrier(jnp.sum(back_rows.astype(jnp.float32), axis=1))
    gain_grad = lax.optimization_barrier(jnp.sum(normed_total * unit_rows, axis=0))
    upstream = normed_total * norm_gain
    input_grad = grad_rows + inverse * (upstream - unit_rows * lax.optimization_barrier(jnp.mean(upstream * unit_rows, axis=-1, keepdims=True)))
    return (layer_out, input_grad.astype(jnp.bfloat16), gate_grad, gain_grad, gate_g, up_g, down_g)
```

```python
import functools

import jax
import jax.numpy as jnp
from jax import lax
from jax.experimental import pallas as pl
from jax.experimental.pallas import tpu as pltpu
from jax.sharding import PartitionSpec as P

epsilon = 1e-06
AXES = ("dp", "tensor")
MESH = pl.DeviceIdType.MESH
f32, bf16 = jnp.float32, jnp.bfloat16


class Place:
    def __init__(self, line):
        self.line = line
        dp, tensor = lax.axis_index("dp"), lax.axis_index("tensor")
        self.z, self.x = dp // 2, dp % 2
        self.y, self.c = tensor // 2, tensor % 2

    def block(self, z, flip):
        x = 1 - self.x if flip in (1, 3) else self.x
        y = 1 - self.y if flip in (2, 3) else self.y
        return x, y

    def index(self, z, flip, c):
        x, y = self.block(z, flip)
        return (z * 2 + x) * 4 + y * 2 + c

    def device(self, z, flip, c):
        x, y = self.block(z, flip)
        return (z * 2 + x, y * 2 + c)

    def order(self, step, farthest_first):
        result = jnp.int32(0)
        for own in range(self.line):
            listed = sorted(range(self.line), key=lambda p: (abs(p - own), p))
            if farthest_first:
                listed = listed[::-1]
            result = jnp.where(self.z == own, jnp.int32(listed[step]), result)
        return result

    def greet(self):
        barrier = pltpu.get_barrier_semaphore()

        def tell(device):
            pl.semaphore_signal(barrier, inc=1, device_id=device, device_id_type=MESH)

        for flip, c in ((1, self.c), (2, self.c), (0, 1 - self.c)):
            tell(self.device(self.z, flip, c))
        below, above = self.z > 0, self.z < self.line - 1
        pl.when(below)(lambda: tell(self.device(self.z - 1, 0, self.c)))
        pl.when(above)(lambda: tell(self.device(self.z + 1, 0, self.c)))
        pl.semaphore_wait(barrier, 3 + below.astype(jnp.int32) + above.astype(jnp.int32))


UP, DOWN, SIDE, FACE, HALF0, HALF1, CORE = 0, 1, 2, 3, 4, 5, 6


class Gather:
    def __init__(self, place, own, held, send, recv, keep):
        self.p, self.own, self.held = place, own, held
        self.send, self.recv, self.keep = send, recv, keep
        self.half = own.shape[0] // 2

    def copy(self, kind, zz, flip, part, device, own=False):
        where = self.p.index(zz, flip, self.p.c)
        dst = self.held.at[where]
        src = self.own if own else dst
        if part is not None:
            rows = pl.ds(part * self.half, self.half)
            src, dst = src.at[rows], dst.at[rows]
        return pltpu.make_async_remote_copy(
            src_ref=src, dst_ref=dst, send_sem=self.send.at[kind, zz],
            recv_sem=self.recv.at[kind, zz], device_id=device, device_id_type=MESH,
        )

    def up(self, zz, own=False):
        return self.copy(UP, zz, 0, None, self.p.device(self.p.z + 1, 0, self.p.c), own)

    def down(self, zz, own=False):
        return self.copy(DOWN, zz, 0, None, self.p.device(self.p.z - 1, 0, self.p.c), own)

    def side(self, zz, own=False):
        return self.copy(SIDE, zz, 0, None, self.p.device(self.p.z, 1, self.p.c), own)

    def face(self, zz, own=False):
        return self.copy(FACE, zz, 0, None, self.p.device(self.p.z, 2, self.p.c), own)

    def half0(self, zz):
        return self.copy(HALF0, zz, 1, 0, self.p.device(self.p.z, 2, self.p.c))

    def half1(self, zz):
        return self.copy(HALF1, zz, 2, 1, self.p.device(self.p.z, 1, self.p.c))

    def core(self, zz, flip, own=False):
        return self.copy(CORE + flip, zz, flip, None, self.p.device(self.p.z, 0, 1 - self.p.c), own)

    def arrived(self, kind, zz, flip, part, c=None):
        where = self.p.index(zz, flip, self.p.c if c is None else c)
        dst = self.held.at[where]
        if part is not None:
            dst = dst.at[pl.ds(part * self.half, self.half)]
        pltpu.make_async_remote_copy(
            src_ref=dst, dst_ref=dst, send_sem=self.send.at[kind, zz],
            recv_sem=self.recv.at[kind, zz],
            device_id=self.p.device(self.p.z, 0, 1 - self.p.c), device_id_type=MESH,
        ).wait_recv()

    def first(self):
        p = self.p
        pltpu.make_async_copy(self.own, self.held.at[p.index(p.z, 0, p.c)], self.keep).start()
        pl.when(p.z < p.line - 1)(lambda: self.up(p.z, True).start())
        pl.when(p.z > 0)(lambda: self.down(p.z, True).start())
        self.side(p.z, True).start()
        self.face(p.z, True).start()
        self.core(p.z, 0, True).start()

    def column(self, step):
        p, zz = self.p, self.p.order(step, False)

        @pl.when(zz < p.z)
        def _():
            self.arrived(UP, zz, 0, None)
            pl.when(p.z < p.line - 1)(lambda: self.up(zz).start())

        @pl.when(zz > p.z)
        def _():
            self.arrived(DOWN, zz, 0, None)
            pl.when(p.z > 0)(lambda: self.down(zz).start())

        self.side(zz).start()
        self.face(zz).start()
        self.core(zz, 0).start()

    def plane(self, step):
        zz = self.p.order(step, False)
        self.arrived(SIDE, zz, 1, None)
        self.half0(zz).start()
        self.core(zz, 1).start()
        self.arrived(FACE, zz, 2, None)
        self.half1(zz).start()
        self.core(zz, 2).start()

    def corner(self, step):
        zz = self.p.order(step, False)
        self.arrived(HALF0, zz, 3, 0)
        self.arrived(HALF1, zz, 3, 1)
        self.core(zz, 3).start()

    def slot(self, step):
        line = self.p.line
        if step == 0:
            self.first()
        elif 0 < step < line:
            self.column(step)
        if 0 <= step - 1 < line:
            self.plane(step - 1)
        if 0 <= step - 2 < line:
            self.corner(step - 2)

    def finish(self):
        p = self.p
        for zz in range(p.line):
            for flip in range(4):
                self.arrived(CORE + flip, zz, flip, None, 1 - p.c)
        for zz in range(p.line):
            pl.when((zz <= p.z) & (p.z < p.line - 1))(lambda zz=zz: self.up(zz).wait_send())
            pl.when((zz >= p.z) & (p.z > 0))(lambda zz=zz: self.down(zz).wait_send())
            for one in (self.side(zz), self.face(zz), self.half0(zz), self.half1(zz)):
                one.wait_send()
            for flip in range(4):
                self.core(zz, flip).wait_send()
        pltpu.make_async_copy(self.own, self.held.at[p.index(p.z, 0, p.c)], self.keep).wait()


def gather_kernel(line, offsets, *refs):
    count = len(offsets)
    owns, helds = refs[:count], refs[count:2 * count]
    send, recv, keep = refs[2 * count:]
    place = Place(line)
    place.greet()
    arrays = [
        Gather(place, owns[i], helds[i], send.at[i], recv.at[i], keep.at[i]) for i in range(count)
    ]
    for step in range(max(offsets) + line + 2):
        for one, offset in zip(arrays, offsets):
            one.slot(step - offset)
    for one in arrays:
        one.finish()


def gather_all(arrays, offsets, number):
    line = lax.axis_size("dp") // 2
    devices = lax.axis_size(AXES)
    count = len(arrays)
    return pl.pallas_call(
        functools.partial(gather_kernel, line, offsets),
        out_shape=[jax.ShapeDtypeStruct((devices,) + a.shape, a.dtype) for a in arrays],
        in_specs=[pl.BlockSpec(memory_space=pltpu.VMEM)] * count,
        out_specs=[pl.BlockSpec(memory_space=pl.ANY)] * count,
        scratch_shapes=[
            pltpu.SemaphoreType.DMA((count, 10, line)),
            pltpu.SemaphoreType.DMA((count, 10, line)),
            pltpu.SemaphoreType.DMA((count,)),
        ],
        compiler_params=pltpu.CompilerParams(collective_id=number, has_side_effects=True),
        name=f"gather{number}",
    )(*arrays)


def add_rows(start, count, store, *loads):
    chunk = 16

    @pl.loop(0, count // chunk)
    def _(i):
        rows = pl.ds(pl.multiple_of(start + i * chunk, chunk), chunk)
        total = loads[0](rows).astype(f32)
        for load in loads[1:]:
            total = total + load(rows).astype(f32)
        store(rows, total)


def dot(a, b, ca, cb):
    return lax.dot_general(a, b, (((ca,), (cb,)), ((), ())), preferred_element_type=f32)


def row_grads(act_grad, gate_pre, up_pre):
    sigma = jax.nn.sigmoid(gate_pre)
    gate_pgrad = act_grad * up_pre * sigma * (1.0 + gate_pre * (1.0 - sigma))
    return gate_pgrad.astype(bf16), (act_grad * (gate_pre * sigma)).astype(bf16)


def backward_plain(cotan, gate_pre, up_pre, w_down, w_gate, w_up):
    gate_pgrad, up_pgrad = row_grads(dot(cotan, w_down, 1, 1), gate_pre, up_pre)
    back = dot(gate_pgrad, w_gate, 1, 1) + dot(up_pgrad, w_up, 1, 1)
    return gate_pgrad, up_pgrad, back.astype(bf16)


def backward_tile(step, ready, ins, outs):
    cotan, gate_pre, up_pre, w_down, w_gate, w_up = ins
    gate_pgrad, up_pgrad, back = outs
    if step == 0:
        ready(0, 1, 2, 3)
    count = cotan.shape[0] // 4
    rows = pl.ds(step * count, count)
    one, two = row_grads(dot(cotan[rows], w_down[...], 1, 1), gate_pre[rows], up_pre[rows])
    gate_pgrad[rows] = one
    up_pgrad[rows] = two
    if step == 0:
        ready(4, 5)
    wide = 512

    @pl.loop(0, back.shape[1] // wide)
    def _(i):
        cols = pl.ds(pl.multiple_of(i * wide, wide), wide)
        total = dot(gate_pgrad[rows], w_gate[cols], 1, 1) + dot(up_pgrad[rows], w_up[cols], 1, 1)
        back[rows, cols] = total.astype(bf16)


def weights_plain(inputs, gate_pgrad, up_pgrad, act, cotan):
    return tuple(
        dot(a, b, 0, 0).astype(bf16)
        for a, b in ((inputs, gate_pgrad), (inputs, up_pgrad), (act, cotan))
    )


def weights_tile(step, ready, ins, outs):
    inputs, gate_pgrad, up_pgrad, act, cotan = ins
    gate_wgrad, up_wgrad, down_grad = outs
    if step == 0:
        ready(0, 1, 2)
    deep, wide = 256, 512
    share = inputs.shape[1] // deep // 4

    @pl.loop(step * share, (step + 1) * share)
    def _(i):
        cols = pl.ds(pl.multiple_of(i * deep, deep), deep)
        block = inputs[:, cols]
        gate_wgrad[cols] = dot(block, gate_pgrad[...], 0, 0).astype(bf16)
        up_wgrad[cols] = dot(block, up_pgrad[...], 0, 0).astype(bf16)

    if step == 0:
        ready(3, 4)
    if step * deep < act.shape[1]:
        rows = pl.ds(step * deep, deep)

        @pl.loop(0, cotan.shape[1] // wide)
        def _(i):
            cols = pl.ds(pl.multiple_of(i * wide, wide), wide)
            down_grad[rows, cols] = dot(act[:, rows], cotan[:, cols], 0, 0).astype(bf16)


def scatter_kernel(line, job, n_in, n_out, *refs):
    part, refs = refs[0], refs[1:]
    job_in, refs = refs[:n_in], refs[n_in:]
    out, refs = refs[0], refs[1:]
    job_out, refs = refs[:n_out], refs[n_out:]
    mine, theirs, half_in, side_in, face_in, up_in, down_in, send, recv, keep = refs[:10]
    held_in, held_out = refs[10:10 + n_in], refs[10 + n_in:10 + n_in + n_out]
    if job is not None:
        in_sem, out_sem = refs[10 + n_in + n_out:]
        arriving = [
            pltpu.make_async_copy(job_in[i], held_in[i], in_sem.at[i]) for i in range(n_in)
        ]
        leaving = [
            pltpu.make_async_copy(held_out[i], job_out[i], out_sem.at[i]) for i in range(n_out)
        ]

    def ready(*which):
        for i in which:
            arriving[i].wait()

    p = Place(line)
    p.greet()
    count = out.shape[0]
    half = count // 2
    z = p.z

    def put(ref, index):
        def store(rows, value):
            ref[index + (rows,)] = value.astype(ref.dtype)
        return store

    def get(ref, index):
        return lambda rows: ref[index + (rows,)]

    def remote(src, dst, kind, zz, device):
        return pltpu.make_async_remote_copy(
            src_ref=src, dst_ref=dst, send_sem=send.at[kind, zz], recv_sem=recv.at[kind, zz],
            device_id=device, device_id_type=MESH,
        )

    def core(zz, flip):
        return remote(
            part.at[p.index(zz, flip, 1 - p.c)], theirs.at[zz, flip], CORE + flip, zz,
            p.device(z, 0, 1 - p.c),
        )

    def load(zz, flip):
        return pltpu.make_async_copy(
            part.at[p.index(zz, flip, p.c)], mine.at[zz, flip], keep.at[flip, zz]
        )

    def half0(zz):
        return remote(
            theirs.at[zz, 3, pl.ds(0, half)], half_in.at[zz, 0], HALF0, zz, p.device(z, 2, p.c)
        )

    def half1(zz):
        return remote(
            theirs.at[zz, 3, pl.ds(half, half)], half_in.at[zz, 1], HALF1, zz, p.device(z, 1, p.c)
        )

    def side(zz):
        return remote(theirs.at[zz, 1], side_in.at[zz], SIDE, zz, p.device(z, 1, p.c))

    def face(zz):
        return remote(theirs.at[zz, 2], face_in.at[zz], FACE, zz, p.device(z, 2, p.c))

    def up(zz):
        return remote(theirs.at[zz, 0], up_in.at[zz], UP, zz, p.device(z + 1, 0, p.c))

    def down(zz):
        return remote(theirs.at[zz, 0], down_in.at[zz], DOWN, zz, p.device(z - 1, 0, p.c))

    def joined(zz, flip):
        core(zz, flip).wait_recv()
        load(zz, flip).wait()
        add_rows(
            0, count, put(theirs, (zz, flip)), get(theirs, (zz, flip)), get(mine, (zz, flip))
        )

    for step in range(line):
        zz = p.order(step, True)
        for flip in (3, 1, 2, 0):
            core(zz, flip).start()
            load(zz, flip).start()

    if job is not None:
        for copy in arriving:
            copy.start()

    def corner(step):
        zz = p.order(step, True)
        joined(zz, 3)
        half0(zz).start()
        half1(zz).start()
        for flip in (1, 2, 0):
            joined(zz, flip)

    def plane(step):
        zz = p.order(step, True)
        half0(zz).wait_recv()
        here = (zz, 1)
        add_rows(
            0, half, put(theirs, here), get(theirs, here), get(half_in, (zz, 0))
        )
        side(zz).start()
        half1(zz).wait_recv()

        @pl.loop(0, half // 16)
        def _(i):
            low = pl.ds(pl.multiple_of(i * 16, 16), 16)
            high = pl.ds(pl.multiple_of(half + i * 16, 16), 16)
            total = theirs[zz, 2, high].astype(f32) + half_in[zz, 1, low].astype(f32)
            theirs[zz, 2, high] = total.astype(bf16)

        face(zz).start()

    def column(step):
        zz = p.order(step, True)
        side(zz).wait_recv()
        face(zz).wait_recv()
        base = (get(theirs, (zz, 0)), get(side_in, (zz,)), get(face_in, (zz,)))
        if step == line - 1:
            add_rows(0, count, put(out, ()), *base)

            @pl.when(z > 0)
            def _():
                up(zz).wait_recv()
                add_rows(0, count, put(out, ()), get(out, ()), get(up_in, (zz,)))

            @pl.when(z < line - 1)
            def _():
                down(zz).wait_recv()
                add_rows(0, count, put(out, ()), get(out, ()), get(down_in, (zz,)))

            return

        def onward(copy, source, more):
            @pl.when(more)
            def _():
                copy(zz).wait_recv()
                add_rows(0, count, put(theirs, (zz, 0)), *base, get(source, (zz,)))

            @pl.when(jnp.logical_not(more))
            def _():
                add_rows(0, count, put(theirs, (zz, 0)), *base)

            copy(zz).start()

        pl.when(zz > z)(lambda: onward(up, up_in, z > 0))
        pl.when(zz < z)(lambda: onward(down, down_in, z < line - 1))

    for step in range(line + 2):
        if step < line:
            corner(step)
        if 0 <= step - 1 < line:
            plane(step - 1)
        if 0 <= step - 2 < line:
            column(step - 2)
        if job is not None and step < 4:
            job(step, ready, held_in, held_out)
            if step == 3:
                for copy in leaving:
                    copy.start()

    for zz in range(line):
        for flip in range(4):
            core(zz, flip).wait_send()
        for one in (half0, half1, side, face):
            one(zz).wait_send()
        pl.when(zz > z)(lambda zz=zz: up(zz).wait_send())
        pl.when(zz < z)(lambda zz=zz: down(zz).wait_send())
    if job is not None:
        for copy in leaving:
            copy.wait()


def scatter_sum(part, number, job, plain, arrays):
    line = lax.axis_size("dp") // 2
    _, rows, width = part.shape
    results = jax.eval_shape(plain, *arrays)
    size = sum(a.size * a.dtype.itemsize for a in list(arrays) + list(results))
    extra = None
    if size + 13 * line * rows * width * 2 > 52 * 2**20:
        extra, job, arrays, results = plain(*arrays), None, (), ()
    anywhere = pl.BlockSpec(memory_space=pl.ANY)
    more = []
    if job is not None:
        more = [pltpu.VMEM(a.shape, a.dtype) for a in list(arrays) + list(results)] + [
            pltpu.SemaphoreType.DMA((len(arrays),)),
            pltpu.SemaphoreType.DMA((len(results),)),
        ]
    total, *done = pl.pallas_call(
        functools.partial(scatter_kernel, line, job, len(arrays), len(results)),
        out_shape=[jax.ShapeDtypeStruct((rows, width), f32)]
        + [jax.ShapeDtypeStruct(r.shape, r.dtype) for r in results],
        in_specs=[anywhere] * (1 + len(arrays)),
        out_specs=[pl.BlockSpec(memory_space=pltpu.VMEM)] + [anywhere] * len(results),
        scratch_shapes=[
            pltpu.VMEM((line, 4, rows, width), bf16),
            pltpu.VMEM((line, 4, rows, width), bf16),
            pltpu.VMEM((line, 2, rows // 2, width), bf16),
            pltpu.VMEM((line, rows, width), bf16),
            pltpu.VMEM((line, rows, width), bf16),
            pltpu.VMEM((line, rows, width), bf16),
            pltpu.VMEM((line, rows, width), bf16),
            pltpu.SemaphoreType.DMA((10, line)),
            pltpu.SemaphoreType.DMA((10, line)),
            pltpu.SemaphoreType.DMA((4, line)),
        ] + more,
        compiler_params=pltpu.CompilerParams(
            collective_id=number, has_side_effects=True, vmem_limit_bytes=62 * 2**20
        ),
        name=f"scatter{number}",
    )(part, *arrays)
    return total, tuple(done) if extra is None else extra


def last_kernel(line, small, grad, held, rows_out, send, recv, keep, tsend, trecv, tkeep):
    p = Place(line)
    p.greet()
    here = p.y * 2 + p.c
    other = (1 - p.y) * 2 + p.c

    def tremote(src, where, i, device):
        return pltpu.make_async_remote_copy(
            src_ref=src, dst_ref=rows_out.at[where], send_sem=tsend.at[i], recv_sem=trecv.at[i],
            device_id=device, device_id_type=MESH,
        )

    partner = p.device(p.z, 0, 1 - p.c)
    keeping = pltpu.make_async_copy(grad, rows_out.at[here], tkeep)
    keeping.start()
    across = tremote(grad, here, 0, p.device(p.z, 2, p.c))
    beside = tremote(grad, here, 1, partner)
    relay = tremote(rows_out.at[other], other, 2, partner)
    across.start()
    beside.start()
    one = Gather(p, small, held, send, recv, keep)
    for step in range(line + 2):
        one.slot(step)
        if step == 1:
            across.wait_recv()
            relay.start()
    one.finish()
    beside.wait_recv()
    relay.wait_recv()
    for copy in (across, beside, relay):
        copy.wait_send()
    keeping.wait()


def gather_last(small, grad, number):
    line = lax.axis_size("dp") // 2
    devices, quarters = lax.axis_size(AXES), lax.axis_size("tensor")
    anywhere = pl.BlockSpec(memory_space=pl.ANY)
    return pl.pallas_call(
        functools.partial(last_kernel, line),
        out_shape=[
            jax.ShapeDtypeStruct((devices,) + small.shape, small.dtype),
            jax.ShapeDtypeStruct((quarters,) + grad.shape, grad.dtype),
        ],
        in_specs=[pl.BlockSpec(memory_space=pltpu.VMEM)] * 2,
        out_specs=[anywhere, anywhere],
        scratch_shapes=[
            pltpu.SemaphoreType.DMA((10, line)),
            pltpu.SemaphoreType.DMA((10, line)),
            pltpu.SemaphoreType.DMA,
            pltpu.SemaphoreType.DMA((3,)),
            pltpu.SemaphoreType.DMA((3,)),
            pltpu.SemaphoreType.DMA,
        ],
        compiler_params=pltpu.CompilerParams(collective_id=number, has_side_effects=True),
        name=f"last{number}",
    )(small, grad)


def per_device(
    hidden, norm_gain, expert_ids, gate_probs, out_grad, gate_weight, up_weight, down_weight
):
    quarters = lax.axis_size("tensor")
    quarter = lax.axis_index("tensor")
    own_count = hidden.shape[0] // quarters
    width = hidden.shape[1]
    top_count = expert_ids.shape[1]
    devices = lax.axis_size(AXES)
    experts = gate_weight.shape[0] * devices
    capacity = 2 * own_count * top_count // experts
    tokens = own_count * devices
    blocks_in = min(4, devices)
    groups = devices // blocks_in
    gtok = own_count * blocks_in
    gslots = capacity * blocks_in
    slots = groups * gslots
    me = lax.axis_index(AXES)

    own_rows = lax.dynamic_slice_in_dim(hidden, quarter * own_count, own_count, 0)
    values = own_rows.astype(f32)
    inverse = lax.rsqrt(jnp.mean(values * values, axis=-1, keepdims=True) + epsilon)
    unit_rows = values * inverse
    normed = (unit_rows * norm_gain).astype(bf16)
    grad_rows = out_grad.astype(f32)

    meta = jnp.concatenate(
        [
            expert_ids.astype(f32),
            gate_probs,
            jnp.zeros((own_count, 128 - 2 * top_count), f32),
        ],
        axis=1,
    )
    meta_all, normed_all, grads_all = gather_all(
        [meta, normed, out_grad], (0, 0, lax.axis_size("dp") // 2 - 1), 0
    )
    meta_all = meta_all.reshape(tokens, 128)
    ids_all = meta_all[:, :top_count].astype(jnp.int32)
    probs_all = meta_all[:, top_count:2 * top_count]

    hits = ids_all == me
    member = jnp.any(hits, axis=1).reshape(devices, own_count)
    prob = jnp.sum(jnp.where(hits, probs_all, 0.0), axis=1)
    earlier = jnp.arange(own_count)[:, None] < jnp.arange(own_count)[None, :]
    place = jnp.dot(member.astype(bf16), earlier.astype(bf16), preferred_element_type=f32)
    place = place.astype(jnp.int32)
    block = jnp.arange(devices, dtype=jnp.int32)[:, None] % blocks_in
    slot = jnp.where(member, block * capacity + place, -1).reshape(groups, gtok)
    picks = slot[:, None, :] == jnp.arange(gslots, dtype=jnp.int32)[None, :, None]
    choose = picks.astype(bf16)
    slot_prob = jnp.sum(
        jnp.where(picks, prob.reshape(groups, 1, gtok), 0.0), axis=2
    ).reshape(slots, 1)

    def pack(rows):
        return jnp.einsum(
            "gst,gtd->gsd", choose, rows.reshape(groups, gtok, width), preferred_element_type=f32
        ).astype(bf16).reshape(slots, width)

    def spread(rows):
        return jnp.einsum(
            "gst,gsd->gtd", choose, rows.reshape(groups, gslots, width), preferred_element_type=f32
        ).astype(bf16).reshape(devices, own_count, width)

    w_gate, w_up, w_down = gate_weight[0], up_weight[0], down_weight[0]
    inputs = pack(normed_all)
    gate_pre = dot(inputs, w_gate, 1, 0)
    up_pre = dot(inputs, w_up, 1, 0)
    sigma = jax.nn.sigmoid(gate_pre)
    silu_vals = gate_pre * sigma
    act = (silu_vals * up_pre).astype(bf16)
    results = dot(act, w_down, 1, 0).astype(bf16)
    results_f = results.astype(f32)
    grads = pack(grads_all).astype(f32)
    cotan = (slot_prob * grads).astype(bf16)
    slot_gg = jnp.sum(grads * results_f, axis=1)
    layer_part, (gate_pgrad, up_pgrad, back) = scatter_sum(
        spread((slot_prob * results_f).astype(bf16)), 1, backward_tile, backward_plain,
        (cotan, gate_pre, up_pre, w_down, w_gate, w_up),
    )
    normed_total, (gate_wgrad, up_wgrad, down_grad) = scatter_sum(
        spread(back), 2, weights_tile, weights_plain,
        (inputs, gate_pgrad, up_pgrad, act, cotan),
    )
    gate_wgrad, up_wgrad, down_grad = gate_wgrad[None], up_wgrad[None], down_grad[None]
    token_gg = jnp.sum(jnp.where(picks, slot_gg.reshape(groups, gslots, 1), 0.0), axis=1)

    layer_out = (values + layer_part).astype(bf16)
    gain_part = jnp.sum(normed_total * unit_rows, axis=0)
    upstream = normed_total * norm_gain
    own_grad = grad_rows + inverse * (
        upstream - unit_rows * jnp.mean(upstream * unit_rows, axis=-1, keepdims=True)
    )
    small = jnp.concatenate([token_gg.reshape(-1, 128), gain_part.reshape(-1, 128)], axis=0)
    small_all, input_grad = gather_last(small, own_grad.astype(bf16), 3)
    input_grad = input_grad.reshape(hidden.shape)
    tiles = tokens // 128
    gain_grad = jnp.sum(small_all[:, tiles:, :], axis=0).reshape(width)
    mine = lax.dynamic_slice_in_dim(
        small_all[:, :tiles, :].reshape(devices, tokens), me * own_count, own_count, 1
    )
    named = expert_ids[:, :, None] == jnp.arange(devices, dtype=jnp.int32)[None, None, :]
    gate_grad = jnp.sum(jnp.where(named, mine.T[:, None, :], 0.0), axis=2)
    return (layer_out, input_grad, gate_grad, gain_grad, gate_wgrad, up_wgrad, down_grad)


def solution(mesh):
    rows, wide = P(AXES, None), P(AXES, None, None)
    in_specs = (P("dp", None), P(), rows, rows, rows, wide, wide, wide)
    out_specs = (rows, P("dp", None), rows, P(), wide, wide, wide)
    return jax.shard_map(
        per_device, mesh=mesh, in_specs=in_specs, out_specs=out_specs, check_vma=False
    )
```

```python
import functools

import jax
import jax.numpy as jnp
from jax import lax
from jax.experimental import pallas as pl
from jax.experimental.pallas import tpu as pltpu
from jax.sharding import PartitionSpec as P

epsilon = 1e-06
AXES = ("dp", "tensor")
MESH = pl.DeviceIdType.MESH
f32, bf16 = jnp.float32, jnp.bfloat16


class Place:
    def __init__(self, line):
        self.line = line
        dp, tensor = lax.axis_index("dp"), lax.axis_index("tensor")
        self.z, self.x = dp // 2, dp % 2
        self.y, self.c = tensor // 2, tensor % 2

    def block(self, z, flip):
        x = 1 - self.x if flip in (1, 3) else self.x
        y = 1 - self.y if flip in (2, 3) else self.y
        return x, y

    def index(self, z, flip, c):
        x, y = self.block(z, flip)
        return (z * 2 + x) * 4 + y * 2 + c

    def device(self, z, flip, c):
        x, y = self.block(z, flip)
        return (z * 2 + x, y * 2 + c)

    def order(self, step, farthest_first):
        result = jnp.int32(0)
        for own in range(self.line):
            listed = sorted(range(self.line), key=lambda p: (abs(p - own), p))
            if farthest_first:
                listed = listed[::-1]
            result = jnp.where(self.z == own, jnp.int32(listed[step]), result)
        return result

    def greet(self):
        barrier = pltpu.get_barrier_semaphore()

        def tell(device):
            pl.semaphore_signal(barrier, inc=1, device_id=device, device_id_type=MESH)

        for flip, c in ((1, self.c), (2, self.c), (0, 1 - self.c)):
            tell(self.device(self.z, flip, c))
        below, above = self.z > 0, self.z < self.line - 1
        pl.when(below)(lambda: tell(self.device(self.z - 1, 0, self.c)))
        pl.when(above)(lambda: tell(self.device(self.z + 1, 0, self.c)))
        pl.semaphore_wait(barrier, 3 + below.astype(jnp.int32) + above.astype(jnp.int32))


UP, DOWN, SIDE, FACE, HALF0, HALF1, CORE = 0, 1, 2, 3, 4, 5, 6


class Gather:
    def __init__(self, place, own, held, send, recv, keep):
        self.p, self.own, self.held = place, own, held
        self.send, self.recv, self.keep = send, recv, keep
        self.half = own.shape[0] // 2

    def copy(self, kind, zz, flip, part, device, own=False):
        where = self.p.index(zz, flip, self.p.c)
        dst = self.held.at[where]
        src = self.own if own else dst
        if part is not None:
            rows = pl.ds(part * self.half, self.half)
            src, dst = src.at[rows], dst.at[rows]
        return pltpu.make_async_remote_copy(
            src_ref=src, dst_ref=dst, send_sem=self.send.at[kind, zz],
            recv_sem=self.recv.at[kind, zz], device_id=device, device_id_type=MESH,
        )

    def up(self, zz, own=False):
        return self.copy(UP, zz, 0, None, self.p.device(self.p.z + 1, 0, self.p.c), own)

    def down(self, zz, own=False):
        return self.copy(DOWN, zz, 0, None, self.p.device(self.p.z - 1, 0, self.p.c), own)

    def side(self, zz, own=False):
        return self.copy(SIDE, zz, 0, None, self.p.device(self.p.z, 1, self.p.c), own)

    def face(self, zz, own=False):
        return self.copy(FACE, zz, 0, None, self.p.device(self.p.z, 2, self.p.c), own)

    def half0(self, zz):
        return self.copy(HALF0, zz, 1, 0, self.p.device(self.p.z, 2, self.p.c))

    def half1(self, zz):
        return self.copy(HALF1, zz, 2, 1, self.p.device(self.p.z, 1, self.p.c))

    def core(self, zz, flip, own=False):
        return self.copy(CORE + flip, zz, flip, None, self.p.device(self.p.z, 0, 1 - self.p.c), own)

    def arrived(self, kind, zz, flip, part, c=None):
        where = self.p.index(zz, flip, self.p.c if c is None else c)
        dst = self.held.at[where]
        if part is not None:
            dst = dst.at[pl.ds(part * self.half, self.half)]
        pltpu.make_async_remote_copy(
            src_ref=dst, dst_ref=dst, send_sem=self.send.at[kind, zz],
            recv_sem=self.recv.at[kind, zz],
            device_id=self.p.device(self.p.z, 0, 1 - self.p.c), device_id_type=MESH,
        ).wait_recv()

    def first(self):
        p = self.p
        pltpu.make_async_copy(self.own, self.held.at[p.index(p.z, 0, p.c)], self.keep).start()
        pl.when(p.z < p.line - 1)(lambda: self.up(p.z, True).start())
        pl.when(p.z > 0)(lambda: self.down(p.z, True).start())
        self.side(p.z, True).start()
        self.face(p.z, True).start()
        self.core(p.z, 0, True).start()

    def column(self, step):
        p, zz = self.p, self.p.order(step, False)

        @pl.when(zz < p.z)
        def _():
            self.arrived(UP, zz, 0, None)
            pl.when(p.z < p.line - 1)(lambda: self.up(zz).start())

        @pl.when(zz > p.z)
        def _():
            self.arrived(DOWN, zz, 0, None)
            pl.when(p.z > 0)(lambda: self.down(zz).start())

        self.side(zz).start()
        self.face(zz).start()
        self.core(zz, 0).start()

    def plane(self, step):
        zz = self.p.order(step, False)
        self.arrived(SIDE, zz, 1, None)
        self.half0(zz).start()
        self.core(zz, 1).start()
        self.arrived(FACE, zz, 2, None)
        self.half1(zz).start()
        self.core(zz, 2).start()

    def corner(self, step):
        zz = self.p.order(step, False)
        self.arrived(HALF0, zz, 3, 0)
        self.arrived(HALF1, zz, 3, 1)
        self.core(zz, 3).start()

    def slot(self, step):
        line = self.p.line
        if step == 0:
            self.first()
        elif 0 < step < line:
            self.column(step)
        if 0 <= step - 1 < line:
            self.plane(step - 1)
        if 0 <= step - 2 < line:
            self.corner(step - 2)

    def finish(self):
        p = self.p
        for zz in range(p.line):
            for flip in range(4):
                self.arrived(CORE + flip, zz, flip, None, 1 - p.c)
        for zz in range(p.line):
            pl.when((zz <= p.z) & (p.z < p.line - 1))(lambda zz=zz: self.up(zz).wait_send())
            pl.when((zz >= p.z) & (p.z > 0))(lambda zz=zz: self.down(zz).wait_send())
            for one in (self.side(zz), self.face(zz), self.half0(zz), self.half1(zz)):
                one.wait_send()
            for flip in range(4):
                self.core(zz, flip).wait_send()
        pltpu.make_async_copy(self.own, self.held.at[p.index(p.z, 0, p.c)], self.keep).wait()


def gather_kernel(line, offsets, *refs):
    count = len(offsets)
    owns, helds = refs[:count], refs[count:2 * count]
    send, recv, keep = refs[2 * count:]
    place = Place(line)
    place.greet()
    arrays = [
        Gather(place, owns[i], helds[i], send.at[i], recv.at[i], keep.at[i]) for i in range(count)
    ]
    for step in range(max(offsets) + line + 2):
        for one, offset in zip(arrays, offsets):
            one.slot(step - offset)
    for one in arrays:
        one.finish()


def gather_all(arrays, offsets, number):
    line = lax.axis_size("dp") // 2
    devices = lax.axis_size(AXES)
    count = len(arrays)
    return pl.pallas_call(
        functools.partial(gather_kernel, line, offsets),
        out_shape=[jax.ShapeDtypeStruct((devices,) + a.shape, a.dtype) for a in arrays],
        in_specs=[pl.BlockSpec(memory_space=pltpu.VMEM)] * count,
        out_specs=[pl.BlockSpec(memory_space=pl.ANY)] * count,
        scratch_shapes=[
            pltpu.SemaphoreType.DMA((count, 10, line)),
            pltpu.SemaphoreType.DMA((count, 10, line)),
            pltpu.SemaphoreType.DMA((count,)),
        ],
        compiler_params=pltpu.CompilerParams(collective_id=number, has_side_effects=True),
        name=f"gather{number}",
    )(*arrays)


def add_rows(start, count, store, *loads):
    chunk = 16

    @pl.loop(0, count // chunk)
    def _(i):
        rows = pl.ds(pl.multiple_of(start + i * chunk, chunk), chunk)
        total = loads[0](rows).astype(f32)
        for load in loads[1:]:
            total = total + load(rows).astype(f32)
        store(rows, total)


def dot(a, b, ca, cb):
    return lax.dot_general(a, b, (((ca,), (cb,)), ((), ())), preferred_element_type=f32)


def row_grads(act_grad, gate_pre, up_pre):
    sigma = jax.nn.sigmoid(gate_pre)
    gate_pgrad = act_grad * up_pre * sigma * (1.0 + gate_pre * (1.0 - sigma))
    return gate_pgrad.astype(bf16), (act_grad * (gate_pre * sigma)).astype(bf16)


def backward_plain(cotan, gate_pre, up_pre, w_down, w_gate, w_up):
    gate_pgrad, up_pgrad = row_grads(dot(cotan, w_down, 1, 1), gate_pre, up_pre)
    back = dot(gate_pgrad, w_gate, 1, 1) + dot(up_pgrad, w_up, 1, 1)
    return gate_pgrad, up_pgrad, back.astype(bf16)


def backward_tile(step, ready, ins, outs):
    cotan, gate_pre, up_pre, w_down, w_gate, w_up = ins
    gate_pgrad, up_pgrad, back = outs
    if step == 0:
        ready(0, 1, 2, 3)
    count = cotan.shape[0] // 4
    rows = pl.ds(step * count, count)
    one, two = row_grads(dot(cotan[rows], w_down[...], 1, 1), gate_pre[rows], up_pre[rows])
    gate_pgrad[rows] = one
    up_pgrad[rows] = two
    if step == 0:
        ready(4, 5)
    wide = 512

    @pl.loop(0, back.shape[1] // wide)
    def _(i):
        cols = pl.ds(pl.multiple_of(i * wide, wide), wide)
        total = dot(gate_pgrad[rows], w_gate[cols], 1, 1) + dot(up_pgrad[rows], w_up[cols], 1, 1)
        back[rows, cols] = total.astype(bf16)


def weights_plain(inputs, gate_pgrad, up_pgrad, act, cotan):
    return tuple(
        dot(a, b, 0, 0).astype(bf16)
        for a, b in ((inputs, gate_pgrad), (inputs, up_pgrad), (act, cotan))
    )


def weights_tile(step, ready, ins, outs):
    inputs, gate_pgrad, up_pgrad, act, cotan = ins
    gate_wgrad, up_wgrad, down_grad = outs
    if step == 0:
        ready(0, 1, 2)
    deep, wide = 256, 512
    share = inputs.shape[1] // deep // 4

    @pl.loop(step * share, (step + 1) * share)
    def _(i):
        cols = pl.ds(pl.multiple_of(i * deep, deep), deep)
        block = inputs[:, cols]
        gate_wgrad[cols] = dot(block, gate_pgrad[...], 0, 0).astype(bf16)
        up_wgrad[cols] = dot(block, up_pgrad[...], 0, 0).astype(bf16)

    if step == 0:
        ready(3, 4)
    if step * deep < act.shape[1]:
        rows = pl.ds(step * deep, deep)

        @pl.loop(0, cotan.shape[1] // wide)
        def _(i):
            cols = pl.ds(pl.multiple_of(i * wide, wide), wide)
            down_grad[rows, cols] = dot(act[:, rows], cotan[:, cols], 0, 0).astype(bf16)


def scatter_kernel(line, job, n_in, n_out, *refs):
    part, refs = refs[0], refs[1:]
    job_in, refs = refs[:n_in], refs[n_in:]
    out, refs = refs[0], refs[1:]
    job_out, refs = refs[:n_out], refs[n_out:]
    mine, theirs, half_in, side_in, face_in, up_in, down_in, send, recv, keep = refs[:10]
    held_in, held_out = refs[10:10 + n_in], refs[10 + n_in:10 + n_in + n_out]
    if job is not None:
        in_sem, out_sem = refs[10 + n_in + n_out:]
        arriving = [
            pltpu.make_async_copy(job_in[i], held_in[i], in_sem.at[i]) for i in range(n_in)
        ]
        leaving = [
            pltpu.make_async_copy(held_out[i], job_out[i], out_sem.at[i]) for i in range(n_out)
        ]

    def ready(*which):
        for i in which:
            arriving[i].wait()

    p = Place(line)
    p.greet()
    count = out.shape[0]
    half = count // 2
    z = p.z

    def put(ref, index):
        def store(rows, value):
            ref[index + (rows,)] = value.astype(ref.dtype)
        return store

    def get(ref, index):
        return lambda rows: ref[index + (rows,)]

    def remote(src, dst, kind, zz, device):
        return pltpu.make_async_remote_copy(
            src_ref=src, dst_ref=dst, send_sem=send.at[kind, zz], recv_sem=recv.at[kind, zz],
            device_id=device, device_id_type=MESH,
        )

    def core(zz, flip):
        return remote(
            part.at[p.index(zz, flip, 1 - p.c)], theirs.at[zz, flip], CORE + flip, zz,
            p.device(z, 0, 1 - p.c),
        )

    def load(zz, flip):
        return pltpu.make_async_copy(
            part.at[p.index(zz, flip, p.c)], mine.at[zz, flip], keep.at[flip, zz]
        )

    def half0(zz):
        return remote(
            theirs.at[zz, 3, pl.ds(0, half)], half_in.at[zz, 0], HALF0, zz, p.device(z, 2, p.c)
        )

    def half1(zz):
        return remote(
            theirs.at[zz, 3, pl.ds(half, half)], half_in.at[zz, 1], HALF1, zz, p.device(z, 1, p.c)
        )

    def side(zz):
        return remote(theirs.at[zz, 1], side_in.at[zz], SIDE, zz, p.device(z, 1, p.c))

    def face(zz):
        return remote(theirs.at[zz, 2], face_in.at[zz], FACE, zz, p.device(z, 2, p.c))

    def up(zz):
        return remote(theirs.at[zz, 0], up_in.at[zz], UP, zz, p.device(z + 1, 0, p.c))

    def down(zz):
        return remote(theirs.at[zz, 0], down_in.at[zz], DOWN, zz, p.device(z - 1, 0, p.c))

    def joined(zz, flip):
        core(zz, flip).wait_recv()
        load(zz, flip).wait()
        add_rows(
            0, count, put(theirs, (zz, flip)), get(theirs, (zz, flip)), get(mine, (zz, flip))
        )

    for step in range(line):
        zz = p.order(step, True)
        for flip in (3, 1, 2, 0):
            core(zz, flip).start()
            load(zz, flip).start()

    if job is not None:
        for copy in arriving:
            copy.start()

    def corner(step):
        zz = p.order(step, True)
        joined(zz, 3)
        half0(zz).start()
        half1(zz).start()
        for flip in (1, 2, 0):
            joined(zz, flip)

    def plane(step):
        zz = p.order(step, True)
        half0(zz).wait_recv()
        here = (zz, 1)
        add_rows(
            0, half, put(theirs, here), get(theirs, here), get(half_in, (zz, 0))
        )
        side(zz).start()
        half1(zz).wait_recv()

        @pl.loop(0, half // 16)
        def _(i):
            low = pl.ds(pl.multiple_of(i * 16, 16), 16)
            high = pl.ds(pl.multiple_of(half + i * 16, 16), 16)
            total = theirs[zz, 2, high].astype(f32) + half_in[zz, 1, low].astype(f32)
            theirs[zz, 2, high] = total.astype(bf16)

        face(zz).start()

    def column(step):
        zz = p.order(step, True)
        side(zz).wait_recv()
        face(zz).wait_recv()
        base = (get(theirs, (zz, 0)), get(side_in, (zz,)), get(face_in, (zz,)))
        if step == line - 1:
            add_rows(0, count, put(out, ()), *base)

            @pl.when(z > 0)
            def _():
                up(zz).wait_recv()
                add_rows(0, count, put(out, ()), get(out, ()), get(up_in, (zz,)))

            @pl.when(z < line - 1)
            def _():
                down(zz).wait_recv()
                add_rows(0, count, put(out, ()), get(out, ()), get(down_in, (zz,)))

            return

        def onward(copy, source, more):
            @pl.when(more)
            def _():
                copy(zz).wait_recv()
                add_rows(0, count, put(theirs, (zz, 0)), *base, get(source, (zz,)))

            @pl.when(jnp.logical_not(more))
            def _():
                add_rows(0, count, put(theirs, (zz, 0)), *base)

            copy(zz).start()

        pl.when(zz > z)(lambda: onward(up, up_in, z > 0))
        pl.when(zz < z)(lambda: onward(down, down_in, z < line - 1))

    for step in range(line + 2):
        if step < line:
            corner(step)
        if 0 <= step - 1 < line:
            plane(step - 1)
        if 0 <= step - 2 < line:
            column(step - 2)
        if job is not None and step < 4:
            job(step, ready, held_in, held_out)
            if step == 3:
                for copy in leaving:
                    copy.start()

    for zz in range(line):
        for flip in range(4):
            core(zz, flip).wait_send()
        for one in (half0, half1, side, face):
            one(zz).wait_send()
        pl.when(zz > z)(lambda zz=zz: up(zz).wait_send())
        pl.when(zz < z)(lambda zz=zz: down(zz).wait_send())
    if job is not None:
        for copy in leaving:
            copy.wait()


def scatter_sum(part, number, job, plain, arrays):
    line = lax.axis_size("dp") // 2
    _, rows, width = part.shape
    results = jax.eval_shape(plain, *arrays)
    size = sum(a.size * a.dtype.itemsize for a in list(arrays) + list(results))
    extra = None
    if size + 13 * line * rows * width * 2 > 52 * 2**20:
        extra, job, arrays, results = plain(*arrays), None, (), ()
    anywhere = pl.BlockSpec(memory_space=pl.ANY)
    more = []
    if job is not None:
        more = [pltpu.VMEM(a.shape, a.dtype) for a in list(arrays) + list(results)] + [
            pltpu.SemaphoreType.DMA((len(arrays),)),
            pltpu.SemaphoreType.DMA((len(results),)),
        ]
    total, *done = pl.pallas_call(
        functools.partial(scatter_kernel, line, job, len(arrays), len(results)),
        out_shape=[jax.ShapeDtypeStruct((rows, width), f32)]
        + [jax.ShapeDtypeStruct(r.shape, r.dtype) for r in results],
        in_specs=[anywhere] * (1 + len(arrays)),
        out_specs=[pl.BlockSpec(memory_space=pltpu.VMEM)] + [anywhere] * len(results),
        scratch_shapes=[
            pltpu.VMEM((line, 4, rows, width), bf16),
            pltpu.VMEM((line, 4, rows, width), bf16),
            pltpu.VMEM((line, 2, rows // 2, width), bf16),
            pltpu.VMEM((line, rows, width), bf16),
            pltpu.VMEM((line, rows, width), bf16),
            pltpu.VMEM((line, rows, width), bf16),
            pltpu.VMEM((line, rows, width), bf16),
            pltpu.SemaphoreType.DMA((10, line)),
            pltpu.SemaphoreType.DMA((10, line)),
            pltpu.SemaphoreType.DMA((4, line)),
        ] + more,
        compiler_params=pltpu.CompilerParams(
            collective_id=number, has_side_effects=True, vmem_limit_bytes=62 * 2**20
        ),
        name=f"scatter{number}",
    )(part, *arrays)
    return total, tuple(done) if extra is None else extra


def last_kernel(line, small, grad, held, rows_out, send, recv, keep, tsend, trecv, tkeep):
    p = Place(line)
    p.greet()
    here = p.y * 2 + p.c
    other = (1 - p.y) * 2 + p.c

    def tremote(src, where, i, device):
        return pltpu.make_async_remote_copy(
            src_ref=src, dst_ref=rows_out.at[where], send_sem=tsend.at[i], recv_sem=trecv.at[i],
            device_id=device, device_id_type=MESH,
        )

    partner = p.device(p.z, 0, 1 - p.c)
    keeping = pltpu.make_async_copy(grad, rows_out.at[here], tkeep)
    keeping.start()
    across = tremote(grad, here, 0, p.device(p.z, 2, p.c))
    beside = tremote(grad, here, 1, partner)
    relay = tremote(rows_out.at[other], other, 2, partner)
    across.start()
    beside.start()
    one = Gather(p, small, held, send, recv, keep)
    for step in range(line + 2):
        one.slot(step)
        if step == 1:
            across.wait_recv()
            relay.start()
    one.finish()
    beside.wait_recv()
    relay.wait_recv()
    for copy in (across, beside, relay):
        copy.wait_send()
    keeping.wait()


def gather_last(small, grad, number):
    line = lax.axis_size("dp") // 2
    devices, quarters = lax.axis_size(AXES), lax.axis_size("tensor")
    anywhere = pl.BlockSpec(memory_space=pl.ANY)
    return pl.pallas_call(
        functools.partial(last_kernel, line),
        out_shape=[
            jax.ShapeDtypeStruct((devices,) + small.shape, small.dtype),
            jax.ShapeDtypeStruct((quarters,) + grad.shape, grad.dtype),
        ],
        in_specs=[pl.BlockSpec(memory_space=pltpu.VMEM)] * 2,
        out_specs=[anywhere, anywhere],
        scratch_shapes=[
            pltpu.SemaphoreType.DMA((10, line)),
            pltpu.SemaphoreType.DMA((10, line)),
            pltpu.SemaphoreType.DMA,
            pltpu.SemaphoreType.DMA((3,)),
            pltpu.SemaphoreType.DMA((3,)),
            pltpu.SemaphoreType.DMA,
        ],
        compiler_params=pltpu.CompilerParams(collective_id=number, has_side_effects=True),
        name=f"last{number}",
    )(small, grad)


def per_device(
    hidden, norm_gain, expert_ids, gate_probs, out_grad, gate_weight, up_weight, down_weight
):
    quarters = lax.axis_size("tensor")
    quarter = lax.axis_index("tensor")
    own_count = hidden.shape[0] // quarters
    width = hidden.shape[1]
    top_count = expert_ids.shape[1]
    devices = lax.axis_size(AXES)
    experts = gate_weight.shape[0] * devices
    capacity = 2 * own_count * top_count // experts
    tokens = own_count * devices
    blocks_in = min(4, devices)
    groups = devices // blocks_in
    gtok = own_count * blocks_in
    gslots = capacity * blocks_in
    slots = groups * gslots
    me = lax.axis_index(AXES)

    own_rows = lax.dynamic_slice_in_dim(hidden, quarter * own_count, own_count, 0)
    values = own_rows.astype(f32)
    inverse = lax.rsqrt(jnp.mean(values * values, axis=-1, keepdims=True) + epsilon)
    unit_rows = values * inverse
    normed = (unit_rows * norm_gain).astype(bf16)
    grad_rows = out_grad.astype(f32)

    meta = jnp.concatenate(
        [
            expert_ids.astype(f32),
            gate_probs,
            jnp.zeros((own_count, 128 - 2 * top_count), f32),
        ],
        axis=1,
    )
    meta_all, normed_all, grads_all = gather_all(
        [meta, normed, out_grad], (0, 0, lax.axis_size("dp") // 2 - 1), 0
    )
    meta_all = meta_all.reshape(tokens, 128)
    ids_all = meta_all[:, :top_count].astype(jnp.int32)
    probs_all = meta_all[:, top_count:2 * top_count]

    hits = ids_all == me
    member = jnp.any(hits, axis=1).reshape(devices, own_count)
    prob = jnp.sum(jnp.where(hits, probs_all, 0.0), axis=1)
    earlier = jnp.arange(own_count)[:, None] < jnp.arange(own_count)[None, :]
    place = jnp.dot(member.astype(bf16), earlier.astype(bf16), preferred_element_type=f32)
    place = place.astype(jnp.int32)
    block = jnp.arange(devices, dtype=jnp.int32)[:, None] % blocks_in
    slot = jnp.where(member, block * capacity + place, -1).reshape(groups, gtok)
    picks = slot[:, None, :] == jnp.arange(gslots, dtype=jnp.int32)[None, :, None]
    choose = picks.astype(bf16)
    slot_prob = jnp.sum(
        jnp.where(picks, prob.reshape(groups, 1, gtok), 0.0), axis=2
    ).reshape(slots, 1)

    def pack(rows):
        return jnp.einsum(
            "gst,gtd->gsd", choose, rows.reshape(groups, gtok, width), preferred_element_type=f32
        ).astype(bf16).reshape(slots, width)

    def spread(rows):
        return jnp.einsum(
            "gst,gsd->gtd", choose, rows.reshape(groups, gslots, width), preferred_element_type=f32
        ).astype(bf16).reshape(devices, own_count, width)

    w_gate, w_up, w_down = gate_weight[0], up_weight[0], down_weight[0]
    inputs = pack(normed_all)
    gate_pre = dot(inputs, w_gate, 1, 0)
    up_pre = dot(inputs, w_up, 1, 0)
    sigma = jax.nn.sigmoid(gate_pre)
    silu_vals = gate_pre * sigma
    act = (silu_vals * up_pre).astype(bf16)
    results = dot(act, w_down, 1, 0).astype(bf16)
    results_f = results.astype(f32)
    grads = pack(grads_all).astype(f32)
    cotan = (slot_prob * grads).astype(bf16)
    slot_gg = jnp.sum(grads * results_f, axis=1)
    layer_part, (gate_pgrad, up_pgrad, back) = scatter_sum(
        spread((slot_prob * results_f).astype(bf16)), 1, backward_tile, backward_plain,
        (cotan, gate_pre, up_pre, w_down, w_gate, w_up),
    )
    normed_total, (gate_wgrad, up_wgrad, down_grad) = scatter_sum(
        spread(back), 2, weights_tile, weights_plain,
        (inputs, gate_pgrad, up_pgrad, act, cotan),
    )
    gate_wgrad, up_wgrad, down_grad = gate_wgrad[None], up_wgrad[None], down_grad[None]
    token_gg = jnp.sum(jnp.where(picks, slot_gg.reshape(groups, gslots, 1), 0.0), axis=1)

    layer_out = (values + layer_part).astype(bf16)
    gain_part = jnp.sum(normed_total * unit_rows, axis=0)
    upstream = normed_total * norm_gain
    own_grad = grad_rows + inverse * (
        upstream - unit_rows * jnp.mean(upstream * unit_rows, axis=-1, keepdims=True)
    )
    small = jnp.concatenate([token_gg.reshape(-1, 128), gain_part.reshape(-1, 128)], axis=0)
    small_all, input_grad = gather_last(small, own_grad.astype(bf16), 3)
    input_grad = input_grad.reshape(hidden.shape)
    tiles = tokens // 128
    gain_grad = jnp.sum(small_all[:, tiles:, :], axis=0).reshape(width)
    mine = lax.dynamic_slice_in_dim(
        small_all[:, :tiles, :].reshape(devices, tokens), me * own_count, own_count, 1
    )
    named = expert_ids[:, :, None] == jnp.arange(devices, dtype=jnp.int32)[None, None, :]
    gate_grad = jnp.sum(jnp.where(named, mine.T[:, None, :], 0.0), axis=2)
    return (layer_out, input_grad, gate_grad, gain_grad, gate_wgrad, up_wgrad, down_grad)


class Stream(Gather):
    def order(self, step):
        return self.p.order(step, False)

    def done(self, step):
        p, zz = self.p, self.order(step)
        if step == 0:
            pltpu.make_async_copy(
                self.own, self.held.at[p.index(p.z, 0, p.c)], self.keep
            ).wait()
        for flip in range(4):
            self.arrived(CORE + flip, zz, flip, None, 1 - p.c)

    def sent(self):
        p = self.p
        for zz in range(p.line):
            pl.when((zz <= p.z) & (p.z < p.line - 1))(lambda zz=zz: self.up(zz).wait_send())
            pl.when((zz >= p.z) & (p.z > 0))(lambda zz=zz: self.down(zz).wait_send())
            for one in (self.side(zz), self.face(zz), self.half0(zz), self.half1(zz)):
                one.wait_send()
            for flip in range(4):
                self.core(zz, flip).wait_send()


def put(ref, index):
    def store(rows, value):
        ref[index + (rows,)] = value.astype(ref.dtype)
    return store


def get(ref, index):
    return lambda rows: ref[index + (rows,)]


class Scatter:
    def __init__(self, place, part, out, theirs, half_in, side_in, face_in, up_in, down_in, send, recv):
        self.p, self.part, self.out, self.theirs = place, part, out, theirs
        self.half_in, self.side_in, self.face_in = half_in, side_in, face_in
        self.up_in, self.down_in = up_in, down_in
        self.sends, self.recvs = send, recv
        self.count = out.shape[0]
        self.half = self.count // 2

    def order(self, step):
        return self.p.order(step, True)

    def remote(self, src, dst, kind, zz, device):
        return pltpu.make_async_remote_copy(
            src_ref=src, dst_ref=dst, send_sem=self.sends.at[kind, zz],
            recv_sem=self.recvs.at[kind, zz], device_id=device, device_id_type=MESH,
        )

    def core(self, zz, flip):
        p = self.p
        return self.remote(
            self.part.at[p.index(zz, flip, 1 - p.c)], self.theirs.at[zz, flip], CORE + flip, zz,
            p.device(p.z, 0, 1 - p.c),
        )

    def half0(self, zz):
        p = self.p
        return self.remote(
            self.theirs.at[zz, 3, pl.ds(0, self.half)], self.half_in.at[zz, 0], HALF0, zz,
            p.device(p.z, 2, p.c),
        )

    def half1(self, zz):
        p = self.p
        return self.remote(
            self.theirs.at[zz, 3, pl.ds(self.half, self.half)], self.half_in.at[zz, 1], HALF1, zz,
            p.device(p.z, 1, p.c),
        )

    def side(self, zz):
        p = self.p
        return self.remote(
            self.theirs.at[zz, 1], self.side_in.at[zz], SIDE, zz, p.device(p.z, 1, p.c)
        )

    def face(self, zz):
        p = self.p
        return self.remote(
            self.theirs.at[zz, 2], self.face_in.at[zz], FACE, zz, p.device(p.z, 2, p.c)
        )

    def up(self, zz):
        p = self.p
        return self.remote(
            self.theirs.at[zz, 0], self.up_in.at[zz], UP, zz, p.device(p.z + 1, 0, p.c)
        )

    def down(self, zz):
        p = self.p
        return self.remote(
            self.theirs.at[zz, 0], self.down_in.at[zz], DOWN, zz, p.device(p.z - 1, 0, p.c)
        )

    def give(self, step):
        zz = self.order(step)
        for flip in (3, 1, 2, 0):
            self.core(zz, flip).start()

    def joined(self, zz, flip):
        self.core(zz, flip).wait_recv()
        here = (zz, flip)
        add_rows(
            0, self.count, put(self.theirs, here), get(self.theirs, here),
            get(self.part, (self.p.index(zz, flip, self.p.c),)),
        )

    def corner(self, step):
        zz = self.order(step)
        self.joined(zz, 3)
        self.half0(zz).start()
        self.half1(zz).start()
        for flip in (1, 2, 0):
            self.joined(zz, flip)

    def plane(self, step):
        zz, half, theirs = self.order(step), self.half, self.theirs
        self.half0(zz).wait_recv()
        here = (zz, 1)
        add_rows(0, half, put(theirs, here), get(theirs, here), get(self.half_in, (zz, 0)))
        self.side(zz).start()
        self.half1(zz).wait_recv()

        @pl.loop(0, half // 16)
        def _(i):
            low = pl.ds(pl.multiple_of(i * 16, 16), 16)
            high = pl.ds(pl.multiple_of(half + i * 16, 16), 16)
            total = theirs[zz, 2, high].astype(f32) + self.half_in[zz, 1, low].astype(f32)
            theirs[zz, 2, high] = total.astype(bf16)

        self.face(zz).start()

    def column(self, step):
        p, zz, count, out = self.p, self.order(step), self.count, self.out
        z, line = p.z, p.line
        self.side(zz).wait_recv()
        self.face(zz).wait_recv()
        base = (
            get(self.theirs, (zz, 0)), get(self.side_in, (zz,)), get(self.face_in, (zz,))
        )
        if step == line - 1:
            add_rows(0, count, put(out, ()), *base)

            @pl.when(z > 0)
            def _():
                self.up(zz).wait_recv()
                add_rows(0, count, put(out, ()), get(out, ()), get(self.up_in, (zz,)))

            @pl.when(z < line - 1)
            def _():
                self.down(zz).wait_recv()
                add_rows(0, count, put(out, ()), get(out, ()), get(self.down_in, (zz,)))

            return

        def onward(copy, source, more):
            @pl.when(more)
            def _():
                copy(zz).wait_recv()
                add_rows(0, count, put(self.theirs, (zz, 0)), *base, get(source, (zz,)))

            @pl.when(jnp.logical_not(more))
            def _():
                add_rows(0, count, put(self.theirs, (zz, 0)), *base)

            copy(zz).start()

        pl.when(zz > z)(lambda: onward(self.up, self.up_in, z > 0))
        pl.when(zz < z)(lambda: onward(self.down, self.down_in, z < line - 1))

    def given(self):
        for zz in range(self.p.line):
            for flip in range(4):
                self.core(zz, flip).wait_send()

    def sent(self):
        z = self.p.z
        for zz in range(self.p.line):
            for one in (self.half0, self.half1, self.side, self.face):
                one(zz).wait_send()
            pl.when(zz > z)(lambda zz=zz: self.up(zz).wait_send())
            pl.when(zz < z)(lambda zz=zz: self.down(zz).wait_send())


def layer_kernel(
    line, tops, capacity,
    meta, hidden, gain, out_grad, w_gate_in, w_up_in, w_down_in,
    layer_out, rows_out, gg_out, gain_out, gate_wgrad, up_wgrad, down_wgrad, grads_all,
    meta_all, normed_all, hid, normed, inputs, cotan, stage, choose, w_gate, w_up, w_down,
    gate_pre, up_pre, act, gate_pgrad, up_pgrad, ggs, gacc, small, small_all, total, own_grad,
    theirs1, half1, side1, face1, up1, down1, theirs2, half2, side2, face2, up2, down2,
    gsend, grecv, gkeep, ssend, srecv, load, stage_sem, out_sem, tsend, trecv, tkeep,
):
    p = Place(line)
    own, width = hid.shape
    inner = act.shape[1]
    me = p.index(p.z, 0, p.c)
    gtok, gslots = choose.shape[1:]
    pslots = 2 * gslots
    barrier = pltpu.get_barrier_semaphore()

    def tell(device):
        pl.semaphore_signal(barrier, inc=1, device_id=device, device_id_type=MESH)

    for flip, c in ((1, p.c), (2, p.c), (0, 1 - p.c)):
        tell(p.device(p.z, flip, c))
    below, above = p.z > 0, p.z < line - 1
    pl.when(below)(lambda: tell(p.device(p.z - 1, 0, p.c)))
    pl.when(above)(lambda: tell(p.device(p.z + 1, 0, p.c)))

    quarter = p.y * 2 + p.c
    mine = pltpu.make_async_copy(
        hidden.at[pl.ds(pl.multiple_of(quarter * own, own), own)], hid, load.at[0]
    )
    mine.start()
    loads = [
        pltpu.make_async_copy(a, b, load.at[1 + i])
        for i, (a, b) in enumerate(((w_gate_in, w_gate), (w_up_in, w_up), (w_down_in, w_down)))
    ]
    mine.wait()

    def unit_of(rows):
        values = hid[rows].astype(f32)
        inverse = lax.rsqrt(jnp.mean(values * values, axis=-1, keepdims=True) + epsilon)
        return values, inverse

    @pl.loop(0, own // 16)
    def _(i):
        rows = pl.ds(pl.multiple_of(i * 16, 16), 16)
        values, inverse = unit_of(rows)
        normed[rows] = (values * inverse * gain[...]).astype(bf16)

    pl.semaphore_wait(barrier, 3 + below.astype(jnp.int32) + above.astype(jnp.int32))

    def stream(i, source, held):
        return Stream(p, source, held, gsend.at[i], grecv.at[i], gkeep.at[i])

    g_meta, g_norm = stream(0, meta, meta_all), stream(1, normed, normed_all)
    g_grad, g_small = stream(2, out_grad, grads_all), stream(3, small, small_all)
    s_out = Scatter(
        p, normed_all, total, theirs1, half1, side1, face1, up1, down1, ssend.at[0], srecv.at[0]
    )
    s_back = Scatter(
        p, normed_all, total, theirs2, half2, side2, face2, up2, down2, ssend.at[1], srecv.at[1]
    )
    me_f = me.astype(f32)
    wide = 512

    def columns(body, size=wide, full=width):
        @pl.loop(0, full // size)
        def _(i):
            body(pl.ds(pl.multiple_of(i * size, size), size))

    def hits_of(zz, h):
        got = meta_all[pl.ds(8 * zz + 4 * h, 4)].reshape(gtok, 128)
        lane = lax.broadcasted_iota(jnp.int32, (gtok, 128), 1)
        return got, lane, jnp.where((got == me_f) & (lane < tops), 1.0, 0.0)

    def prob_of(zz, h):
        got, _, hit = hits_of(zz, h)
        return jnp.sum(pltpu.roll(hit, tops, 1) * got, axis=1, keepdims=True)

    def route(zz):
        for h in range(2):
            _, lane, hit = hits_of(zz, h)
            member = jnp.sum(hit, axis=1, keepdims=True)
            a = lax.broadcasted_iota(jnp.int32, (gtok, gtok), 0)
            b = lax.broadcasted_iota(jnp.int32, (gtok, gtok), 1)
            earlier = jnp.where((a > b) & (a // own == b // own), 1.0, 0.0).astype(bf16)
            spot = dot(earlier, jnp.broadcast_to(member, (gtok, 128)).astype(bf16), 1, 0)
            block = lax.broadcasted_iota(jnp.int32, (gtok, 128), 0) // own
            spot = spot + (block * capacity).astype(f32)
            picked = (spot == lane.astype(f32)) & (member > 0.0)
            choose[2 * zz + h] = jnp.where(picked, 1.0, 0.0).astype(bf16)

    def slots(zz, h=None):
        if h is None:
            return pl.ds(pl.multiple_of(zz * pslots, pslots), pslots)
        return pl.ds(pl.multiple_of(zz * pslots + h * gslots, gslots), gslots)

    def forward(zz):
        route(zz)
        for h in range(2):
            pick = choose[2 * zz + h]

            def pack(cols, pick=pick, h=h):
                rows = normed_all[pl.ds(8 * zz + 4 * h, 4), :, cols].reshape(gtok, wide)
                inputs[slots(zz, h), cols] = dot(pick, rows, 0, 0).astype(bf16)

            columns(pack)
        rows = slots(zz)

        def products(cols):
            gate = dot(inputs[rows], w_gate[:, cols], 1, 0)
            up = dot(inputs[rows], w_up[:, cols], 1, 0)
            gate_pre[rows, cols] = gate
            up_pre[rows, cols] = up
            act[rows, cols] = (gate * jax.nn.sigmoid(gate) * up).astype(bf16)

        columns(products, 256, inner)

    def result(zz):
        rows = slots(zz)
        probs = [prob_of(zz, h) for h in range(2)]

        def expand(cols):
            done = dot(act[rows], w_down[:, cols], 1, 0).astype(bf16)
            for h in range(2):
                got = dot(choose[2 * zz + h], done[h * gslots:(h + 1) * gslots], 1, 0)
                normed_all[pl.ds(8 * zz + 4 * h, 4), :, cols] = (
                    (got * probs[h]).astype(bf16).reshape(4, own, wide)
                )

        columns(expand)

    def fetch(step):
        zz = s_back.order(step)
        return pltpu.make_async_copy(grads_all.at[pl.ds(8 * zz, 8)], stage, stage_sem)

    def cotangent(step):
        zz = s_back.order(step)
        fetch(step).wait()
        for h in range(2):
            pick, prob = choose[2 * zz + h], prob_of(zz, h)

            def pack(cols, pick=pick, prob=prob, h=h):
                rows = stage[4 * h:4 * h + 4, :, cols].reshape(gtok, wide).astype(f32)
                scaled = (rows * prob).astype(bf16)
                cotan[slots(zz, h), cols] = dot(pick, scaled, 0, 0).astype(bf16)

            columns(pack)
        if step < line - 1:
            fetch(step + 1).start()

    def hidden_grads(zz):
        rows = slots(zz)
        ggs[...] = jnp.zeros_like(ggs)

        def chunk(cols):
            act_grad = dot(cotan[rows], w_down[cols], 1, 1)
            one, two = row_grads(act_grad, gate_pre[rows, cols], up_pre[rows, cols])
            gate_pgrad[rows, cols] = one
            up_pgrad[rows, cols] = two
            both = act_grad * act[rows, cols].astype(f32)
            ggs[...] += both[:, :128] + both[:, 128:]

        columns(chunk, 256, inner)
        for h in range(2):
            line_sum = jnp.sum(ggs[h * gslots:(h + 1) * gslots].T, axis=0, keepdims=True)
            high = line_sum.astype(bf16).astype(f32)
            which = lax.broadcasted_iota(jnp.int32, (16, gslots), 0)
            parts = jnp.where(which == 0, high, jnp.where(which == 1, line_sum - high, 0.0))
            spread = dot(parts.astype(bf16), choose[2 * zz + h], 1, 1)
            row = jnp.sum(spread, axis=0, keepdims=True)
            for k in range(gtok // 128):
                small[pl.ds(4 * zz + 2 * h + k, 1)] = row[:, 128 * k:128 * k + 128]

    def backs(zz):
        rows = slots(zz)

        def chunk(cols):
            back = dot(gate_pgrad[rows], w_gate[cols], 1, 1)
            back = (back + dot(up_pgrad[rows], w_up[cols], 1, 1)).astype(bf16)
            terms = back.astype(f32) * inputs[rows, cols].astype(f32)
            gacc[:, cols] += jnp.sum(terms.reshape(pslots // 8, 8, wide), axis=0)
            for h in range(2):
                got = dot(choose[2 * zz + h], back[h * gslots:(h + 1) * gslots], 1, 0)
                normed_all[pl.ds(8 * zz + 4 * h, 4), :, cols] = (
                    got.astype(bf16).reshape(4, own, wide)
                )

        columns(chunk)

    def weight_grads(step):
        deep = 256
        share = width // deep // 4

        @pl.loop(step * share, (step + 1) * share)
        def _(i):
            cols = pl.ds(pl.multiple_of(i * deep, deep), deep)
            block = inputs[:, cols]
            w_gate[cols] = dot(block, gate_pgrad[...], 0, 0).astype(bf16)
            w_up[cols] = dot(block, up_pgrad[...], 0, 0).astype(bf16)

        if step * deep < inner:
            rows = pl.ds(step * deep, deep)

            def chunk(cols):
                w_down[rows, cols] = dot(act[:, rows], cotan[:, cols], 0, 0).astype(bf16)

            columns(chunk)

    g_meta.slot(0)
    g_norm.slot(0)
    for copy in loads:
        copy.start()
    gacc[...] = jnp.zeros_like(gacc)
    for step in range(1, line + 2):
        g_meta.slot(step)
        g_norm.slot(step)
        g_grad.slot(step - (line - 1))
        if step >= 3:
            g_meta.done(step - 3)
            g_norm.done(step - 3)
            if step == 3:
                for copy in loads:
                    copy.wait()
            forward(g_norm.order(step - 3))
    g_grad.slot(3)
    g_meta.done(line - 1)
    g_norm.done(line - 1)
    forward(g_norm.order(line - 1))
    g_norm.sent()
    result(s_out.order(0))
    s_out.give(0)
    g_grad.slot(4)
    result(s_out.order(1))
    s_out.give(1)
    s_out.corner(0)
    g_grad.slot(5)
    result(s_out.order(2))
    s_out.give(2)
    s_out.corner(1)
    s_out.plane(0)
    result(s_out.order(3))
    s_out.give(3)
    s_out.corner(2)
    s_out.plane(1)
    s_out.column(0)
    for step in range(line):
        g_grad.done(step)
    fetch(0).start()
    s_out.corner(3)
    s_out.plane(2)
    s_out.column(1)
    s_out.given()

    def backward(step):
        zz = s_back.order(step)
        cotangent(step)
        hidden_grads(zz)
        backs(zz)
        s_back.give(step)

    backward(0)
    s_out.plane(3)
    s_out.column(2)
    backward(1)
    s_back.corner(0)
    s_out.column(3)

    @pl.loop(0, own // 16)
    def _(i):
        rows = pl.ds(pl.multiple_of(i * 16, 16), 16)
        layer_out[rows] = (hid[rows].astype(f32) + total[rows]).astype(bf16)

    backward(2)
    s_back.corner(1)
    s_back.plane(0)
    backward(3)
    gsum = jnp.sum(gacc[...], axis=0, keepdims=True)
    first = small.shape[0] - width // 128
    for k in range(width // 128):
        small[first + k:first + k + 1] = gsum[:, 128 * k:128 * k + 128]
    g_small.slot(0)
    s_back.corner(2)
    s_back.plane(1)
    s_back.column(0)
    weight_grads(0)
    g_small.slot(1)
    s_back.corner(3)
    s_back.plane(2)
    s_back.column(1)
    weight_grads(1)
    g_small.slot(2)
    s_back.plane(3)
    s_back.column(2)
    weight_grads(2)
    g_small.slot(3)
    weight_grads(3)
    leaving = [
        pltpu.make_async_copy(a, b, out_sem.at[i])
        for i, (a, b) in enumerate(((w_gate, gate_wgrad), (w_up, up_wgrad), (w_down, down_wgrad)))
    ]
    for copy in leaving:
        copy.start()
    g_small.slot(4)
    s_back.column(3)

    @pl.loop(0, own // 16)
    def _(i):
        rows = pl.ds(pl.multiple_of(i * 16, 16), 16)
        values, inverse = unit_of(rows)
        unit = values * inverse
        upstream = total[rows] * gain[...]
        mean = jnp.mean(upstream * unit, axis=-1, keepdims=True)
        grad = out_grad[rows].astype(f32) + inverse * (upstream - unit * mean)
        own_grad[rows] = grad.astype(bf16)

    other = (1 - p.y) * 2 + p.c
    partner = p.device(p.z, 0, 1 - p.c)

    def tremote(src, where, i, device):
        return pltpu.make_async_remote_copy(
            src_ref=src, dst_ref=rows_out.at[where], send_sem=tsend.at[i], recv_sem=trecv.at[i],
            device_id=device, device_id_type=MESH,
        )

    across = tremote(own_grad, quarter, 0, p.device(p.z, 2, p.c))
    beside = tremote(own_grad, quarter, 1, partner)
    relay = tremote(rows_out.at[other], other, 2, partner)
    across.start()
    beside.start()
    keeping = pltpu.make_async_copy(own_grad, rows_out.at[quarter], tkeep)
    keeping.start()
    g_small.slot(5)
    for step in range(line):
        g_small.done(step)
    gain_out[...] = jnp.sum(small_all[:, first:], axis=0)
    gg_out[...] = small_all[:, pl.ds(me // 2, 1)].reshape(gg_out.shape)
    across.wait_recv()
    relay.start()
    g_meta.sent()
    g_grad.sent()
    g_small.sent()
    s_out.sent()
    s_back.given()
    s_back.sent()
    for copy in leaving:
        copy.wait()
    beside.wait_recv()
    relay.wait_recv()
    for copy in (across, beside, relay):
        copy.wait_send()
    keeping.wait()


def whole_layer(meta, hidden, gain, out_grad, w_gate, w_up, w_down, top_count, capacity):
    line = lax.axis_size("dp") // 2
    devices, quarters = lax.axis_size(AXES), lax.axis_size("tensor")
    own, width = out_grad.shape
    inner = w_gate.shape[1]
    groups, gtok, gslots = devices // 4, own * 4, capacity * 4
    slots = groups * gslots
    small_rows = devices * own // 128 + width // 128
    anywhere, vmem = pl.BlockSpec(memory_space=pl.ANY), pl.BlockSpec(memory_space=pltpu.VMEM)
    shape = jax.ShapeDtypeStruct
    dma = pltpu.SemaphoreType.DMA
    passing = [
        pltpu.VMEM((line, 4, own, width), bf16),
        pltpu.VMEM((line, 2, own // 2, width), bf16),
        pltpu.VMEM((line, own, width), bf16),
        pltpu.VMEM((line, own, width), bf16),
        pltpu.VMEM((line, own, width), bf16),
        pltpu.VMEM((line, own, width), bf16),
    ]
    return pl.pallas_call(
        functools.partial(layer_kernel, line, top_count, capacity),
        out_shape=[
            shape((own, width), bf16),
            shape((quarters, own, width), bf16),
            shape((devices, 128), f32),
            shape((width // 128, 128), f32),
            shape(w_gate.shape, bf16),
            shape(w_up.shape, bf16),
            shape(w_down.shape, bf16),
            shape((devices, own, width), bf16),
        ],
        in_specs=[vmem, anywhere, vmem, vmem, anywhere, anywhere, anywhere],
        out_specs=[vmem, anywhere, vmem, vmem, anywhere, anywhere, anywhere, anywhere],
        scratch_shapes=[
            pltpu.VMEM((devices, own, 128), f32),
            pltpu.VMEM((devices, own, width), bf16),
            pltpu.VMEM((own, width), bf16),
            pltpu.VMEM((own, width), bf16),
            pltpu.VMEM((slots, width), bf16),
            pltpu.VMEM((slots, width), bf16),
            pltpu.VMEM((8, own, width), bf16),
            pltpu.VMEM((groups, gtok, gslots), bf16),
            pltpu.VMEM(w_gate.shape, bf16),
            pltpu.VMEM(w_up.shape, bf16),
            pltpu.VMEM(w_down.shape, bf16),
            pltpu.VMEM((slots, inner), f32),
            pltpu.VMEM((slots, inner), f32),
            pltpu.VMEM((slots, inner), bf16),
            pltpu.VMEM((slots, inner), bf16),
            pltpu.VMEM((slots, inner), bf16),
            pltpu.VMEM((2 * gslots, 128), f32),
            pltpu.VMEM((8, width), f32),
            pltpu.VMEM((small_rows, 128), f32),
            pltpu.VMEM((devices, small_rows, 128), f32),
            pltpu.VMEM((own, width), f32),
            pltpu.VMEM((own, width), bf16),
        ] + passing + passing + [
            dma((4, 10, line)),
            dma((4, 10, line)),
            dma((4,)),
            dma((2, 10, line)),
            dma((2, 10, line)),
            dma((4,)),
            dma,
            dma((3,)),
            dma((3,)),
            dma((3,)),
            dma,
        ],
        compiler_params=pltpu.CompilerParams(
            collective_id=0, has_side_effects=True, vmem_limit_bytes=63 * 2**20
        ),
        name="layer",
    )(meta, hidden, gain, out_grad, w_gate, w_up, w_down)


def per_device_whole(
    hidden, norm_gain, expert_ids, gate_probs, out_grad, gate_weight, up_weight, down_weight
):
    own_count, width = out_grad.shape
    top_count = expert_ids.shape[1]
    devices = lax.axis_size(AXES)
    capacity = 2 * own_count * top_count // devices
    me = lax.axis_index(AXES)
    meta = jnp.concatenate(
        [
            expert_ids.astype(f32),
            gate_probs,
            jnp.zeros((own_count, 128 - 2 * top_count), f32),
        ],
        axis=1,
    )
    layer_out, input_grad, values, gain_sum, gate_wgrad, up_wgrad, down_grad, _ = whole_layer(
        meta, hidden, norm_gain[None], out_grad, gate_weight[0], up_weight[0], down_weight[0],
        top_count, capacity,
    )
    mine = lax.dynamic_slice_in_dim(values, me % 2 * own_count, own_count, 1)
    named = expert_ids[:, :, None] == jnp.arange(devices, dtype=jnp.int32)[None, None, :]
    gate_grad = jnp.sum(jnp.where(named, mine.T[:, None, :], 0.0), axis=2) / gate_probs
    gain_grad = gain_sum.reshape(width) / norm_gain
    return (
        layer_out, input_grad.reshape(hidden.shape), gate_grad, gain_grad,
        gate_wgrad[None], up_wgrad[None], down_grad[None],
    )


def choose_form(*arrays):
    hidden, _, expert_ids, _, out_grad = arrays[:5]
    devices = lax.axis_size(AXES)
    capacity = 2 * out_grad.shape[0] * expert_ids.shape[1] // devices
    fits = devices <= 32 and capacity * 4 == 128 and out_grad.shape[0] == 64
    return (per_device_whole if fits else per_device)(*arrays)


def solution(mesh):
    rows, wide = P(AXES, None), P(AXES, None, None)
    in_specs = (P("dp", None), P(), rows, rows, rows, wide, wide, wide)
    out_specs = (rows, P("dp", None), rows, P(), wide, wide, wide)
    return jax.shard_map(
        choose_form, mesh=mesh, in_specs=in_specs, out_specs=out_specs, check_vma=False
    )
```

```python
import functools

import jax
import jax.numpy as jnp
from jax import lax
from jax.experimental import pallas as pl
from jax.experimental.pallas import tpu as pltpu
from jax.sharding import PartitionSpec as P

epsilon = 1e-06
AXES = ("dp", "tensor")
MESH = pl.DeviceIdType.MESH
f32, bf16 = jnp.float32, jnp.bfloat16


class Place:
    def __init__(self, line):
        self.line = line
        dp, tensor = lax.axis_index("dp"), lax.axis_index("tensor")
        self.z, self.x = dp // 2, dp % 2
        self.y, self.c = tensor // 2, tensor % 2

    def block(self, z, flip):
        x = 1 - self.x if flip in (1, 3) else self.x
        y = 1 - self.y if flip in (2, 3) else self.y
        return x, y

    def index(self, z, flip, c):
        x, y = self.block(z, flip)
        return (z * 2 + x) * 4 + y * 2 + c

    def device(self, z, flip, c):
        x, y = self.block(z, flip)
        return (z * 2 + x, y * 2 + c)

    def order(self, step, farthest_first):
        result = jnp.int32(0)
        for own in range(self.line):
            listed = sorted(range(self.line), key=lambda p: (abs(p - own), p))
            if farthest_first:
                listed = listed[::-1]
            result = jnp.where(self.z == own, jnp.int32(listed[step]), result)
        return result

    def greet(self):
        barrier = pltpu.get_barrier_semaphore()

        def tell(device):
            pl.semaphore_signal(barrier, inc=1, device_id=device, device_id_type=MESH)

        for flip, c in ((1, self.c), (2, self.c), (0, 1 - self.c)):
            tell(self.device(self.z, flip, c))
        below, above = self.z > 0, self.z < self.line - 1
        pl.when(below)(lambda: tell(self.device(self.z - 1, 0, self.c)))
        pl.when(above)(lambda: tell(self.device(self.z + 1, 0, self.c)))
        pl.semaphore_wait(barrier, 3 + below.astype(jnp.int32) + above.astype(jnp.int32))


UP, DOWN, SIDE, FACE, HALF0, HALF1, CORE = 0, 1, 2, 3, 4, 5, 6


class Gather:
    def __init__(self, place, own, held, send, recv, keep):
        self.p, self.own, self.held = place, own, held
        self.send, self.recv, self.keep = send, recv, keep
        self.half = own.shape[0] // 2

    def copy(self, kind, zz, flip, part, device, own=False):
        where = self.p.index(zz, flip, self.p.c)
        dst = self.held.at[where]
        src = self.own if own else dst
        if part is not None:
            rows = pl.ds(part * self.half, self.half)
            src, dst = src.at[rows], dst.at[rows]
        return pltpu.make_async_remote_copy(
            src_ref=src, dst_ref=dst, send_sem=self.send.at[kind, zz],
            recv_sem=self.recv.at[kind, zz], device_id=device, device_id_type=MESH,
        )

    def up(self, zz, own=False):
        return self.copy(UP, zz, 0, None, self.p.device(self.p.z + 1, 0, self.p.c), own)

    def down(self, zz, own=False):
        return self.copy(DOWN, zz, 0, None, self.p.device(self.p.z - 1, 0, self.p.c), own)

    def side(self, zz, own=False):
        return self.copy(SIDE, zz, 0, None, self.p.device(self.p.z, 1, self.p.c), own)

    def face(self, zz, own=False):
        return self.copy(FACE, zz, 0, None, self.p.device(self.p.z, 2, self.p.c), own)

    def half0(self, zz):
        return self.copy(HALF0, zz, 1, 0, self.p.device(self.p.z, 2, self.p.c))

    def half1(self, zz):
        return self.copy(HALF1, zz, 2, 1, self.p.device(self.p.z, 1, self.p.c))

    def core(self, zz, flip, own=False):
        return self.copy(CORE + flip, zz, flip, None, self.p.device(self.p.z, 0, 1 - self.p.c), own)

    def arrived(self, kind, zz, flip, part, c=None):
        where = self.p.index(zz, flip, self.p.c if c is None else c)
        dst = self.held.at[where]
        if part is not None:
            dst = dst.at[pl.ds(part * self.half, self.half)]
        pltpu.make_async_remote_copy(
            src_ref=dst, dst_ref=dst, send_sem=self.send.at[kind, zz],
            recv_sem=self.recv.at[kind, zz],
            device_id=self.p.device(self.p.z, 0, 1 - self.p.c), device_id_type=MESH,
        ).wait_recv()

    def first(self):
        p = self.p
        pltpu.make_async_copy(self.own, self.held.at[p.index(p.z, 0, p.c)], self.keep).start()
        pl.when(p.z < p.line - 1)(lambda: self.up(p.z, True).start())
        pl.when(p.z > 0)(lambda: self.down(p.z, True).start())
        self.side(p.z, True).start()
        self.face(p.z, True).start()
        self.core(p.z, 0, True).start()

    def column(self, step):
        p, zz = self.p, self.p.order(step, False)

        @pl.when(zz < p.z)
        def _():
            self.arrived(UP, zz, 0, None)
            pl.when(p.z < p.line - 1)(lambda: self.up(zz).start())

        @pl.when(zz > p.z)
        def _():
            self.arrived(DOWN, zz, 0, None)
            pl.when(p.z > 0)(lambda: self.down(zz).start())

        self.side(zz).start()
        self.face(zz).start()
        self.core(zz, 0).start()

    def plane(self, step):
        zz = self.p.order(step, False)
        self.arrived(SIDE, zz, 1, None)
        self.half0(zz).start()
        self.core(zz, 1).start()
        self.arrived(FACE, zz, 2, None)
        self.half1(zz).start()
        self.core(zz, 2).start()

    def corner(self, step):
        zz = self.p.order(step, False)
        self.arrived(HALF0, zz, 3, 0)
        self.arrived(HALF1, zz, 3, 1)
        self.core(zz, 3).start()

    def slot(self, step):
        line = self.p.line
        if step == 0:
            self.first()
        elif 0 < step < line:
            self.column(step)
        if 0 <= step - 1 < line:
            self.plane(step - 1)
        if 0 <= step - 2 < line:
            self.corner(step - 2)

    def finish(self):
        p = self.p
        for zz in range(p.line):
            for flip in range(4):
                self.arrived(CORE + flip, zz, flip, None, 1 - p.c)
        for zz in range(p.line):
            pl.when((zz <= p.z) & (p.z < p.line - 1))(lambda zz=zz: self.up(zz).wait_send())
            pl.when((zz >= p.z) & (p.z > 0))(lambda zz=zz: self.down(zz).wait_send())
            for one in (self.side(zz), self.face(zz), self.half0(zz), self.half1(zz)):
                one.wait_send()
            for flip in range(4):
                self.core(zz, flip).wait_send()
        pltpu.make_async_copy(self.own, self.held.at[p.index(p.z, 0, p.c)], self.keep).wait()


def gather_kernel(line, offsets, *refs):
    count = len(offsets)
    owns, helds = refs[:count], refs[count:2 * count]
    send, recv, keep = refs[2 * count:]
    place = Place(line)
    place.greet()
    arrays = [
        Gather(place, owns[i], helds[i], send.at[i], recv.at[i], keep.at[i]) for i in range(count)
    ]
    for step in range(max(offsets) + line + 2):
        for one, offset in zip(arrays, offsets):
            one.slot(step - offset)
    for one in arrays:
        one.finish()


def gather_all(arrays, offsets, number):
    line = lax.axis_size("dp") // 2
    devices = lax.axis_size(AXES)
    count = len(arrays)
    return pl.pallas_call(
        functools.partial(gather_kernel, line, offsets),
        out_shape=[jax.ShapeDtypeStruct((devices,) + a.shape, a.dtype) for a in arrays],
        in_specs=[pl.BlockSpec(memory_space=pltpu.VMEM)] * count,
        out_specs=[pl.BlockSpec(memory_space=pl.ANY)] * count,
        scratch_shapes=[
            pltpu.SemaphoreType.DMA((count, 10, line)),
            pltpu.SemaphoreType.DMA((count, 10, line)),
            pltpu.SemaphoreType.DMA((count,)),
        ],
        compiler_params=pltpu.CompilerParams(collective_id=number, has_side_effects=True),
        name=f"gather{number}",
    )(*arrays)


def add_rows(start, count, store, *loads):
    chunk = 16

    @pl.loop(0, count // chunk)
    def _(i):
        rows = pl.ds(pl.multiple_of(start + i * chunk, chunk), chunk)
        total = loads[0](rows).astype(f32)
        for load in loads[1:]:
            total = total + load(rows).astype(f32)
        store(rows, total)


def dot(a, b, ca, cb):
    return lax.dot_general(a, b, (((ca,), (cb,)), ((), ())), preferred_element_type=f32)


def row_grads(act_grad, gate_pre, up_pre):
    sigma = jax.nn.sigmoid(gate_pre)
    gate_pgrad = act_grad * up_pre * sigma * (1.0 + gate_pre * (1.0 - sigma))
    return gate_pgrad.astype(bf16), (act_grad * (gate_pre * sigma)).astype(bf16)


def backward_plain(cotan, gate_pre, up_pre, w_down, w_gate, w_up):
    gate_pgrad, up_pgrad = row_grads(dot(cotan, w_down, 1, 1), gate_pre, up_pre)
    back = dot(gate_pgrad, w_gate, 1, 1) + dot(up_pgrad, w_up, 1, 1)
    return gate_pgrad, up_pgrad, back.astype(bf16)


def backward_tile(step, ready, ins, outs):
    cotan, gate_pre, up_pre, w_down, w_gate, w_up = ins
    gate_pgrad, up_pgrad, back = outs
    if step == 0:
        ready(0, 1, 2, 3)
    count = cotan.shape[0] // 4
    rows = pl.ds(step * count, count)
    one, two = row_grads(dot(cotan[rows], w_down[...], 1, 1), gate_pre[rows], up_pre[rows])
    gate_pgrad[rows] = one
    up_pgrad[rows] = two
    if step == 0:
        ready(4, 5)
    wide = 512

    @pl.loop(0, back.shape[1] // wide)
    def _(i):
        cols = pl.ds(pl.multiple_of(i * wide, wide), wide)
        total = dot(gate_pgrad[rows], w_gate[cols], 1, 1) + dot(up_pgrad[rows], w_up[cols], 1, 1)
        back[rows, cols] = total.astype(bf16)


def weights_plain(inputs, gate_pgrad, up_pgrad, act, cotan):
    return tuple(
        dot(a, b, 0, 0).astype(bf16)
        for a, b in ((inputs, gate_pgrad), (inputs, up_pgrad), (act, cotan))
    )


def weights_tile(step, ready, ins, outs):
    inputs, gate_pgrad, up_pgrad, act, cotan = ins
    gate_wgrad, up_wgrad, down_grad = outs
    if step == 0:
        ready(0, 1, 2)
    deep, wide = 256, 512
    share = inputs.shape[1] // deep // 4

    @pl.loop(step * share, (step + 1) * share)
    def _(i):
        cols = pl.ds(pl.multiple_of(i * deep, deep), deep)
        block = inputs[:, cols]
        gate_wgrad[cols] = dot(block, gate_pgrad[...], 0, 0).astype(bf16)
        up_wgrad[cols] = dot(block, up_pgrad[...], 0, 0).astype(bf16)

    if step == 0:
        ready(3, 4)
    if step * deep < act.shape[1]:
        rows = pl.ds(step * deep, deep)

        @pl.loop(0, cotan.shape[1] // wide)
        def _(i):
            cols = pl.ds(pl.multiple_of(i * wide, wide), wide)
            down_grad[rows, cols] = dot(act[:, rows], cotan[:, cols], 0, 0).astype(bf16)


def scatter_kernel(line, job, n_in, n_out, *refs):
    part, refs = refs[0], refs[1:]
    job_in, refs = refs[:n_in], refs[n_in:]
    out, refs = refs[0], refs[1:]
    job_out, refs = refs[:n_out], refs[n_out:]
    mine, theirs, half_in, side_in, face_in, up_in, down_in, send, recv, keep = refs[:10]
    held_in, held_out = refs[10:10 + n_in], refs[10 + n_in:10 + n_in + n_out]
    if job is not None:
        in_sem, out_sem = refs[10 + n_in + n_out:]
        arriving = [
            pltpu.make_async_copy(job_in[i], held_in[i], in_sem.at[i]) for i in range(n_in)
        ]
        leaving = [
            pltpu.make_async_copy(held_out[i], job_out[i], out_sem.at[i]) for i in range(n_out)
        ]

    def ready(*which):
        for i in which:
            arriving[i].wait()

    p = Place(line)
    p.greet()
    count = out.shape[0]
    half = count // 2
    z = p.z

    def put(ref, index):
        def store(rows, value):
            ref[index + (rows,)] = value.astype(ref.dtype)
        return store

    def get(ref, index):
        return lambda rows: ref[index + (rows,)]

    def remote(src, dst, kind, zz, device):
        return pltpu.make_async_remote_copy(
            src_ref=src, dst_ref=dst, send_sem=send.at[kind, zz], recv_sem=recv.at[kind, zz],
            device_id=device, device_id_type=MESH,
        )

    def core(zz, flip):
        return remote(
            part.at[p.index(zz, flip, 1 - p.c)], theirs.at[zz, flip], CORE + flip, zz,
            p.device(z, 0, 1 - p.c),
        )

    def load(zz, flip):
        return pltpu.make_async_copy(
            part.at[p.index(zz, flip, p.c)], mine.at[zz, flip], keep.at[flip, zz]
        )

    def half0(zz):
        return remote(
            theirs.at[zz, 3, pl.ds(0, half)], half_in.at[zz, 0], HALF0, zz, p.device(z, 2, p.c)
        )

    def half1(zz):
        return remote(
            theirs.at[zz, 3, pl.ds(half, half)], half_in.at[zz, 1], HALF1, zz, p.device(z, 1, p.c)
        )

    def side(zz):
        return remote(theirs.at[zz, 1], side_in.at[zz], SIDE, zz, p.device(z, 1, p.c))

    def face(zz):
        return remote(theirs.at[zz, 2], face_in.at[zz], FACE, zz, p.device(z, 2, p.c))

    def up(zz):
        return remote(theirs.at[zz, 0], up_in.at[zz], UP, zz, p.device(z + 1, 0, p.c))

    def down(zz):
        return remote(theirs.at[zz, 0], down_in.at[zz], DOWN, zz, p.device(z - 1, 0, p.c))

    def joined(zz, flip):
        core(zz, flip).wait_recv()
        load(zz, flip).wait()
        add_rows(
            0, count, put(theirs, (zz, flip)), get(theirs, (zz, flip)), get(mine, (zz, flip))
        )

    for step in range(line):
        zz = p.order(step, True)
        for flip in (3, 1, 2, 0):
            core(zz, flip).start()
            load(zz, flip).start()

    if job is not None:
        for copy in arriving:
            copy.start()

    def corner(step):
        zz = p.order(step, True)
        joined(zz, 3)
        half0(zz).start()
        half1(zz).start()
        for flip in (1, 2, 0):
            joined(zz, flip)

    def plane(step):
        zz = p.order(step, True)
        half0(zz).wait_recv()
        here = (zz, 1)
        add_rows(
            0, half, put(theirs, here), get(theirs, here), get(half_in, (zz, 0))
        )
        side(zz).start()
        half1(zz).wait_recv()

        @pl.loop(0, half // 16)
        def _(i):
            low = pl.ds(pl.multiple_of(i * 16, 16), 16)
            high = pl.ds(pl.multiple_of(half + i * 16, 16), 16)
            total = theirs[zz, 2, high].astype(f32) + half_in[zz, 1, low].astype(f32)
            theirs[zz, 2, high] = total.astype(bf16)

        face(zz).start()

    def column(step):
        zz = p.order(step, True)
        side(zz).wait_recv()
        face(zz).wait_recv()
        base = (get(theirs, (zz, 0)), get(side_in, (zz,)), get(face_in, (zz,)))
        if step == line - 1:
            add_rows(0, count, put(out, ()), *base)

            @pl.when(z > 0)
            def _():
                up(zz).wait_recv()
                add_rows(0, count, put(out, ()), get(out, ()), get(up_in, (zz,)))

            @pl.when(z < line - 1)
            def _():
                down(zz).wait_recv()
                add_rows(0, count, put(out, ()), get(out, ()), get(down_in, (zz,)))

            return

        def onward(copy, source, more):
            @pl.when(more)
            def _():
                copy(zz).wait_recv()
                add_rows(0, count, put(theirs, (zz, 0)), *base, get(source, (zz,)))

            @pl.when(jnp.logical_not(more))
            def _():
                add_rows(0, count, put(theirs, (zz, 0)), *base)

            copy(zz).start()

        pl.when(zz > z)(lambda: onward(up, up_in, z > 0))
        pl.when(zz < z)(lambda: onward(down, down_in, z < line - 1))

    for step in range(line + 2):
        if step < line:
            corner(step)
        if 0 <= step - 1 < line:
            plane(step - 1)
        if 0 <= step - 2 < line:
            column(step - 2)
        if job is not None and step < 4:
            job(step, ready, held_in, held_out)
            if step == 3:
                for copy in leaving:
                    copy.start()

    for zz in range(line):
        for flip in range(4):
            core(zz, flip).wait_send()
        for one in (half0, half1, side, face):
            one(zz).wait_send()
        pl.when(zz > z)(lambda zz=zz: up(zz).wait_send())
        pl.when(zz < z)(lambda zz=zz: down(zz).wait_send())
    if job is not None:
        for copy in leaving:
            copy.wait()


def scatter_sum(part, number, job, plain, arrays):
    line = lax.axis_size("dp") // 2
    _, rows, width = part.shape
    results = jax.eval_shape(plain, *arrays)
    size = sum(a.size * a.dtype.itemsize for a in list(arrays) + list(results))
    extra = None
    if size + 13 * line * rows * width * 2 > 52 * 2**20:
        extra, job, arrays, results = plain(*arrays), None, (), ()
    anywhere = pl.BlockSpec(memory_space=pl.ANY)
    more = []
    if job is not None:
        more = [pltpu.VMEM(a.shape, a.dtype) for a in list(arrays) + list(results)] + [
            pltpu.SemaphoreType.DMA((len(arrays),)),
            pltpu.SemaphoreType.DMA((len(results),)),
        ]
    total, *done = pl.pallas_call(
        functools.partial(scatter_kernel, line, job, len(arrays), len(results)),
        out_shape=[jax.ShapeDtypeStruct((rows, width), f32)]
        + [jax.ShapeDtypeStruct(r.shape, r.dtype) for r in results],
        in_specs=[anywhere] * (1 + len(arrays)),
        out_specs=[pl.BlockSpec(memory_space=pltpu.VMEM)] + [anywhere] * len(results),
        scratch_shapes=[
            pltpu.VMEM((line, 4, rows, width), bf16),
            pltpu.VMEM((line, 4, rows, width), bf16),
            pltpu.VMEM((line, 2, rows // 2, width), bf16),
            pltpu.VMEM((line, rows, width), bf16),
            pltpu.VMEM((line, rows, width), bf16),
            pltpu.VMEM((line, rows, width), bf16),
            pltpu.VMEM((line, rows, width), bf16),
            pltpu.SemaphoreType.DMA((10, line)),
            pltpu.SemaphoreType.DMA((10, line)),
            pltpu.SemaphoreType.DMA((4, line)),
        ] + more,
        compiler_params=pltpu.CompilerParams(
            collective_id=number, has_side_effects=True, vmem_limit_bytes=62 * 2**20
        ),
        name=f"scatter{number}",
    )(part, *arrays)
    return total, tuple(done) if extra is None else extra


def last_kernel(line, small, grad, held, rows_out, send, recv, keep, tsend, trecv, tkeep):
    p = Place(line)
    p.greet()
    here = p.y * 2 + p.c
    other = (1 - p.y) * 2 + p.c

    def tremote(src, where, i, device):
        return pltpu.make_async_remote_copy(
            src_ref=src, dst_ref=rows_out.at[where], send_sem=tsend.at[i], recv_sem=trecv.at[i],
            device_id=device, device_id_type=MESH,
        )

    partner = p.device(p.z, 0, 1 - p.c)
    keeping = pltpu.make_async_copy(grad, rows_out.at[here], tkeep)
    keeping.start()
    across = tremote(grad, here, 0, p.device(p.z, 2, p.c))
    beside = tremote(grad, here, 1, partner)
    relay = tremote(rows_out.at[other], other, 2, partner)
    across.start()
    beside.start()
    one = Gather(p, small, held, send, recv, keep)
    for step in range(line + 2):
        one.slot(step)
        if step == 1:
            across.wait_recv()
            relay.start()
    one.finish()
    beside.wait_recv()
    relay.wait_recv()
    for copy in (across, beside, relay):
        copy.wait_send()
    keeping.wait()


def gather_last(small, grad, number):
    line = lax.axis_size("dp") // 2
    devices, quarters = lax.axis_size(AXES), lax.axis_size("tensor")
    anywhere = pl.BlockSpec(memory_space=pl.ANY)
    return pl.pallas_call(
        functools.partial(last_kernel, line),
        out_shape=[
            jax.ShapeDtypeStruct((devices,) + small.shape, small.dtype),
            jax.ShapeDtypeStruct((quarters,) + grad.shape, grad.dtype),
        ],
        in_specs=[pl.BlockSpec(memory_space=pltpu.VMEM)] * 2,
        out_specs=[anywhere, anywhere],
        scratch_shapes=[
            pltpu.SemaphoreType.DMA((10, line)),
            pltpu.SemaphoreType.DMA((10, line)),
            pltpu.SemaphoreType.DMA,
            pltpu.SemaphoreType.DMA((3,)),
            pltpu.SemaphoreType.DMA((3,)),
            pltpu.SemaphoreType.DMA,
        ],
        compiler_params=pltpu.CompilerParams(collective_id=number, has_side_effects=True),
        name=f"last{number}",
    )(small, grad)


def per_device(
    hidden, norm_gain, expert_ids, gate_probs, out_grad, gate_weight, up_weight, down_weight
):
    quarters = lax.axis_size("tensor")
    quarter = lax.axis_index("tensor")
    own_count = hidden.shape[0] // quarters
    width = hidden.shape[1]
    top_count = expert_ids.shape[1]
    devices = lax.axis_size(AXES)
    experts = gate_weight.shape[0] * devices
    capacity = 2 * own_count * top_count // experts
    tokens = own_count * devices
    blocks_in = min(4, devices)
    groups = devices // blocks_in
    gtok = own_count * blocks_in
    gslots = capacity * blocks_in
    slots = groups * gslots
    me = lax.axis_index(AXES)

    own_rows = lax.dynamic_slice_in_dim(hidden, quarter * own_count, own_count, 0)
    values = own_rows.astype(f32)
    inverse = lax.rsqrt(jnp.mean(values * values, axis=-1, keepdims=True) + epsilon)
    unit_rows = values * inverse
    normed = (unit_rows * norm_gain).astype(bf16)
    grad_rows = out_grad.astype(f32)

    meta = jnp.concatenate(
        [
            expert_ids.astype(f32),
            gate_probs,
            jnp.zeros((own_count, 128 - 2 * top_count), f32),
        ],
        axis=1,
    )
    meta_all, normed_all, grads_all = gather_all(
        [meta, normed, out_grad], (0, 0, lax.axis_size("dp") // 2 - 1), 0
    )
    meta_all = meta_all.reshape(tokens, 128)
    ids_all = meta_all[:, :top_count].astype(jnp.int32)
    probs_all = meta_all[:, top_count:2 * top_count]

    hits = ids_all == me
    member = jnp.any(hits, axis=1).reshape(devices, own_count)
    prob = jnp.sum(jnp.where(hits, probs_all, 0.0), axis=1)
    earlier = jnp.arange(own_count)[:, None] < jnp.arange(own_count)[None, :]
    place = jnp.dot(member.astype(bf16), earlier.astype(bf16), preferred_element_type=f32)
    place = place.astype(jnp.int32)
    block = jnp.arange(devices, dtype=jnp.int32)[:, None] % blocks_in
    slot = jnp.where(member, block * capacity + place, -1).reshape(groups, gtok)
    picks = slot[:, None, :] == jnp.arange(gslots, dtype=jnp.int32)[None, :, None]
    choose = picks.astype(bf16)
    slot_prob = jnp.sum(
        jnp.where(picks, prob.reshape(groups, 1, gtok), 0.0), axis=2
    ).reshape(slots, 1)

    def pack(rows):
        return jnp.einsum(
            "gst,gtd->gsd", choose, rows.reshape(groups, gtok, width), preferred_element_type=f32
        ).astype(bf16).reshape(slots, width)

    def spread(rows):
        return jnp.einsum(
            "gst,gsd->gtd", choose, rows.reshape(groups, gslots, width), preferred_element_type=f32
        ).astype(bf16).reshape(devices, own_count, width)

    w_gate, w_up, w_down = gate_weight[0], up_weight[0], down_weight[0]
    inputs = pack(normed_all)
    gate_pre = dot(inputs, w_gate, 1, 0)
    up_pre = dot(inputs, w_up, 1, 0)
    sigma = jax.nn.sigmoid(gate_pre)
    silu_vals = gate_pre * sigma
    act = (silu_vals * up_pre).astype(bf16)
    results = dot(act, w_down, 1, 0).astype(bf16)
    results_f = results.astype(f32)
    grads = pack(grads_all).astype(f32)
    cotan = (slot_prob * grads).astype(bf16)
    slot_gg = jnp.sum(grads * results_f, axis=1)
    layer_part, (gate_pgrad, up_pgrad, back) = scatter_sum(
        spread((slot_prob * results_f).astype(bf16)), 1, backward_tile, backward_plain,
        (cotan, gate_pre, up_pre, w_down, w_gate, w_up),
    )
    normed_total, (gate_wgrad, up_wgrad, down_grad) = scatter_sum(
        spread(back), 2, weights_tile, weights_plain,
        (inputs, gate_pgrad, up_pgrad, act, cotan),
    )
    gate_wgrad, up_wgrad, down_grad = gate_wgrad[None], up_wgrad[None], down_grad[None]
    token_gg = jnp.sum(jnp.where(picks, slot_gg.reshape(groups, gslots, 1), 0.0), axis=1)

    layer_out = (values + layer_part).astype(bf16)
    gain_part = jnp.sum(normed_total * unit_rows, axis=0)
    upstream = normed_total * norm_gain
    own_grad = grad_rows + inverse * (
        upstream - unit_rows * jnp.mean(upstream * unit_rows, axis=-1, keepdims=True)
    )
    small = jnp.concatenate([token_gg.reshape(-1, 128), gain_part.reshape(-1, 128)], axis=0)
    small_all, input_grad = gather_last(small, own_grad.astype(bf16), 3)
    input_grad = input_grad.reshape(hidden.shape)
    tiles = tokens // 128
    gain_grad = jnp.sum(small_all[:, tiles:, :], axis=0).reshape(width)
    mine = lax.dynamic_slice_in_dim(
        small_all[:, :tiles, :].reshape(devices, tokens), me * own_count, own_count, 1
    )
    named = expert_ids[:, :, None] == jnp.arange(devices, dtype=jnp.int32)[None, None, :]
    gate_grad = jnp.sum(jnp.where(named, mine.T[:, None, :], 0.0), axis=2)
    return (layer_out, input_grad, gate_grad, gain_grad, gate_wgrad, up_wgrad, down_grad)


CORNER_UP, CORNER_DOWN = 10, 11


def along_z(line, z, zz):
    apart = jnp.abs(jnp.int32(z) - zz)
    return (apart == 1) | ((apart == 2) & ((z == 0) | (z == line - 1)))


class Stream(Gather):
    def order(self, step):
        return self.p.order(step, False)

    def corner_up(self, zz):
        p = self.p
        return self.copy(CORNER_UP, zz, 3, None, p.device(p.z + 1, 0, p.c))

    def corner_down(self, zz):
        p = self.p
        return self.copy(CORNER_DOWN, zz, 3, None, p.device(p.z - 1, 0, p.c))

    def routes(self, zz):
        z, line = self.p.z, self.p.line
        up = (z < line - 1) & (zz <= z) & along_z(line, z + 1, zz)
        down = (z > 0) & (zz >= z) & along_z(line, z - 1, zz)
        return along_z(line, z, zz), up, down

    def plane(self, step):
        zz = self.order(step)
        flat = jnp.logical_not(self.routes(zz)[0])
        self.arrived(SIDE, zz, 1, None)
        pl.when(flat)(lambda: self.half0(zz).start())
        self.core(zz, 1).start()
        self.arrived(FACE, zz, 2, None)
        pl.when(flat)(lambda: self.half1(zz).start())
        self.core(zz, 2).start()

    def corner(self, step):
        zz, z = self.order(step), self.p.z
        via, up, down = self.routes(zz)

        @pl.when(jnp.logical_not(via))
        def _():
            self.arrived(HALF0, zz, 3, 0)
            self.arrived(HALF1, zz, 3, 1)

        pl.when(via & (zz < z))(lambda: self.arrived(CORNER_UP, zz, 3, None))
        pl.when(via & (zz > z))(lambda: self.arrived(CORNER_DOWN, zz, 3, None))
        pl.when(up)(lambda: self.corner_up(zz).start())
        pl.when(down)(lambda: self.corner_down(zz).start())
        self.core(zz, 3).start()

    def done(self, step):
        p, zz = self.p, self.order(step)
        if step == 0:
            pltpu.make_async_copy(
                self.own, self.held.at[p.index(p.z, 0, p.c)], self.keep
            ).wait()
        for flip in range(4):
            self.arrived(CORE + flip, zz, flip, None, 1 - p.c)

    def sent(self):
        p = self.p
        for zz in range(p.line):
            pl.when((zz <= p.z) & (p.z < p.line - 1))(lambda zz=zz: self.up(zz).wait_send())
            pl.when((zz >= p.z) & (p.z > 0))(lambda zz=zz: self.down(zz).wait_send())
            self.side(zz).wait_send()
            self.face(zz).wait_send()
            via, up, down = self.routes(jnp.int32(zz))

            @pl.when(jnp.logical_not(via))
            def _(zz=zz):
                self.half0(zz).wait_send()
                self.half1(zz).wait_send()

            pl.when(up)(lambda zz=zz: self.corner_up(zz).wait_send())
            pl.when(down)(lambda zz=zz: self.corner_down(zz).wait_send())
            for flip in range(4):
                self.core(zz, flip).wait_send()


def put(ref, index):
    def store(rows, value):
        ref[index + (rows,)] = value.astype(ref.dtype)
    return store


def get(ref, index):
    return lambda rows: ref[index + (rows,)]


class Scatter:
    def __init__(
        self, place, part, out, theirs, half_in, side_in, face_in, up_in, down_in, corner_up_in,
        corner_down_in, send, recv,
    ):
        self.p, self.part, self.out, self.theirs = place, part, out, theirs
        self.half_in, self.side_in, self.face_in = half_in, side_in, face_in
        self.up_in, self.down_in = up_in, down_in
        self.corner_up_in, self.corner_down_in = corner_up_in, corner_down_in
        self.sends, self.recvs = send, recv
        self.count = out.shape[0]
        self.half = self.count // 2

    def order(self, step):
        return self.p.order(step, True)

    def remote(self, src, dst, kind, zz, device):
        return pltpu.make_async_remote_copy(
            src_ref=src, dst_ref=dst, send_sem=self.sends.at[kind, zz],
            recv_sem=self.recvs.at[kind, zz], device_id=device, device_id_type=MESH,
        )

    def core(self, zz, flip):
        p = self.p
        return self.remote(
            self.part.at[p.index(zz, flip, 1 - p.c)], self.theirs.at[zz, flip], CORE + flip, zz,
            p.device(p.z, 0, 1 - p.c),
        )

    def half0(self, zz):
        p = self.p
        return self.remote(
            self.theirs.at[zz, 3, pl.ds(0, self.half)], self.half_in.at[self.flat(zz), 0], HALF0, zz,
            p.device(p.z, 2, p.c),
        )

    def half1(self, zz):
        p = self.p
        return self.remote(
            self.theirs.at[zz, 3, pl.ds(self.half, self.half)], self.half_in.at[self.flat(zz), 1], HALF1, zz,
            p.device(p.z, 1, p.c),
        )

    def side(self, zz):
        p = self.p
        return self.remote(
            self.theirs.at[zz, 1], self.side_in.at[zz], SIDE, zz, p.device(p.z, 1, p.c)
        )

    def face(self, zz):
        p = self.p
        return self.remote(
            self.theirs.at[zz, 2], self.face_in.at[zz], FACE, zz, p.device(p.z, 2, p.c)
        )

    def up(self, zz):
        p = self.p
        return self.remote(
            self.theirs.at[zz, 0], self.up_in.at[zz], UP, zz, p.device(p.z + 1, 0, p.c)
        )

    def down(self, zz):
        p = self.p
        return self.remote(
            self.theirs.at[zz, 0], self.down_in.at[zz], DOWN, zz, p.device(p.z - 1, 0, p.c)
        )

    def flat(self, zz):
        return jnp.where(zz == self.p.z, 0, 1)

    def corner_up(self, zz, slot):
        p = self.p
        return self.remote(
            self.theirs.at[zz, 3], self.corner_up_in.at[slot], CORNER_UP, zz,
            p.device(p.z + 1, 0, p.c),
        )

    def corner_down(self, zz, slot):
        p = self.p
        return self.remote(
            self.theirs.at[zz, 3], self.corner_down_in.at[slot], CORNER_DOWN, zz,
            p.device(p.z - 1, 0, p.c),
        )

    def give(self, step):
        zz = self.order(step)
        for flip in (3, 1, 2, 0):
            self.core(zz, flip).start()

    def joined(self, zz, flip):
        self.core(zz, flip).wait_recv()
        here = (zz, flip)
        add_rows(
            0, self.count, put(self.theirs, here), get(self.theirs, here),
            get(self.part, (self.p.index(zz, flip, self.p.c),)),
        )

    def corner(self, step):
        p, zz, here = self.p, self.order(step), (self.order(step), 3)
        z, line = p.z, p.line
        via = along_z(line, z, zz)
        below = (z > 0) & (zz >= z) & along_z(line, z - 1, zz)
        above = (z < line - 1) & (zz <= z) & along_z(line, z + 1, zz)

        def onward():
            pl.when(via & (zz > z))(lambda: self.corner_up(zz, zz - z - 1).start())
            pl.when(via & (zz < z))(lambda: self.corner_down(zz, z - 1 - zz).start())

            @pl.when(jnp.logical_not(via))
            def _():
                self.half0(zz).start()
                self.half1(zz).start()

        self.joined(zz, 3)
        pl.when(jnp.logical_not(below | above))(onward)
        for flip in (1, 2, 0):
            self.joined(zz, flip)

        @pl.when(below)
        def _():
            slot = zz - z
            self.corner_up(zz, slot).wait_recv()
            add_rows(
                0, self.count, put(self.theirs, here), get(self.theirs, here),
                get(self.corner_up_in, (slot,)),
            )

        @pl.when(above)
        def _():
            slot = z - zz
            self.corner_down(zz, slot).wait_recv()
            add_rows(
                0, self.count, put(self.theirs, here), get(self.theirs, here),
                get(self.corner_down_in, (slot,)),
            )

        pl.when(below | above)(onward)

    def plane(self, step):
        zz, half, theirs = self.order(step), self.half, self.theirs
        flat, slot = jnp.logical_not(along_z(self.p.line, self.p.z, zz)), self.flat(zz)
        here = (zz, 1)

        @pl.when(flat)
        def _():
            self.half0(zz).wait_recv()
            add_rows(0, half, put(theirs, here), get(theirs, here), get(self.half_in, (slot, 0)))

        self.side(zz).start()

        @pl.when(flat)
        def _():
            self.half1(zz).wait_recv()

            @pl.loop(0, half // 16)
            def _(i):
                low = pl.ds(pl.multiple_of(i * 16, 16), 16)
                high = pl.ds(pl.multiple_of(half + i * 16, 16), 16)
                total = theirs[zz, 2, high].astype(f32) + self.half_in[slot, 1, low].astype(f32)
                theirs[zz, 2, high] = total.astype(bf16)

        self.face(zz).start()

    def column(self, step):
        p, zz, count, out = self.p, self.order(step), self.count, self.out
        z, line = p.z, p.line
        self.side(zz).wait_recv()
        self.face(zz).wait_recv()
        base = (
            get(self.theirs, (zz, 0)), get(self.side_in, (zz,)), get(self.face_in, (zz,))
        )
        if step == line - 1:
            add_rows(0, count, put(out, ()), *base)

            @pl.when(z > 0)
            def _():
                self.up(zz).wait_recv()
                add_rows(0, count, put(out, ()), get(out, ()), get(self.up_in, (zz,)))

            @pl.when(z < line - 1)
            def _():
                self.down(zz).wait_recv()
                add_rows(0, count, put(out, ()), get(out, ()), get(self.down_in, (zz,)))

            return

        def onward(copy, source, more):
            @pl.when(more)
            def _():
                copy(zz).wait_recv()
                add_rows(0, count, put(self.theirs, (zz, 0)), *base, get(source, (zz,)))

            @pl.when(jnp.logical_not(more))
            def _():
                add_rows(0, count, put(self.theirs, (zz, 0)), *base)

            copy(zz).start()

        pl.when(zz > z)(lambda: onward(self.up, self.up_in, z > 0))
        pl.when(zz < z)(lambda: onward(self.down, self.down_in, z < line - 1))

    def given(self):
        for zz in range(self.p.line):
            for flip in range(4):
                self.core(zz, flip).wait_send()

    def sent(self):
        z = self.p.z
        for zz in range(self.p.line):
            self.side(zz).wait_send()
            self.face(zz).wait_send()
            via = along_z(self.p.line, z, jnp.int32(zz))

            @pl.when(jnp.logical_not(via))
            def _(zz=zz):
                self.half0(zz).wait_send()
                self.half1(zz).wait_send()

            pl.when(via & (zz > z))(lambda zz=zz: self.corner_up(zz, 0).wait_send())
            pl.when(via & (zz < z))(lambda zz=zz: self.corner_down(zz, 0).wait_send())
            pl.when(zz > z)(lambda zz=zz: self.up(zz).wait_send())
            pl.when(zz < z)(lambda zz=zz: self.down(zz).wait_send())


def layer_kernel(
    line, tops, capacity,
    ids, probs, hidden, gain, out_grad, w_gate_in, w_up_in, w_down_in,
    layer_out, rows_out, gg_out, gain_out, w_gate, w_up, w_down, grads_all,
    turn, meta, meta_all, normed_all, hid, normed, inputs, cotan, stage, choose,
    gate_pre, up_pre, act, gate_pgrad, up_pgrad, ggs, gacc, small, small_all, total, own_grad,
    theirs1, half1, side1, face1, up1, down1, cup1, cdown1,
    theirs2, half2, side2, face2, up2, down2, cup2, cdown2,
    gsend, grecv, gkeep, ssend, srecv, load, stage_sem, tsend, trecv, tkeep,
):
    p = Place(line)
    own, width = hid.shape
    inner = act.shape[1]
    me = p.index(p.z, 0, p.c)
    gtok, gslots = choose.shape[1:]
    pslots = 2 * gslots
    barrier = pltpu.get_barrier_semaphore()

    def tell(device):
        pl.semaphore_signal(barrier, inc=1, device_id=device, device_id_type=MESH)

    for flip, c in ((1, p.c), (2, p.c), (0, 1 - p.c)):
        tell(p.device(p.z, flip, c))
    below, above = p.z > 0, p.z < line - 1
    pl.when(below)(lambda: tell(p.device(p.z - 1, 0, p.c)))
    pl.when(above)(lambda: tell(p.device(p.z + 1, 0, p.c)))

    quarter = p.y * 2 + p.c
    mine = pltpu.make_async_copy(
        hidden.at[pl.ds(pl.multiple_of(quarter * own, own), own)], hid, load.at[0]
    )
    mine.start()
    loads = [
        pltpu.make_async_copy(a, b, load.at[1 + i])
        for i, (a, b) in enumerate(((w_gate_in, w_gate), (w_up_in, w_up), (w_down_in, w_down)))
    ]
    turn[...] = jnp.zeros_like(turn)
    turn[0:tops, 0:own] = ids[...].astype(f32)
    turn[tops:2 * tops, 0:own] = probs[...]
    meta[...] = turn[...].T[0:own]
    mine.wait()

    def unit_of(rows):
        values = hid[rows].astype(f32)
        inverse = lax.rsqrt(jnp.mean(values * values, axis=-1, keepdims=True) + epsilon)
        return values, inverse

    @pl.loop(0, own // 16)
    def _(i):
        rows = pl.ds(pl.multiple_of(i * 16, 16), 16)
        values, inverse = unit_of(rows)
        normed[rows] = (values * inverse * gain[...]).astype(bf16)

    pl.semaphore_wait(barrier, 3 + below.astype(jnp.int32) + above.astype(jnp.int32))

    def stream(i, source, held):
        return Stream(p, source, held, gsend.at[i], grecv.at[i], gkeep.at[i])

    g_meta, g_norm = stream(0, meta, meta_all), stream(1, normed, normed_all)
    g_grad, g_small = stream(2, out_grad, grads_all), stream(3, small, small_all)
    s_out = Scatter(
        p, normed_all, total, theirs1, half1, side1, face1, up1, down1, cup1, cdown1, ssend.at[0],
        srecv.at[0],
    )
    s_back = Scatter(
        p, normed_all, total, theirs2, half2, side2, face2, up2, down2, cup2, cdown2, ssend.at[1],
        srecv.at[1],
    )
    me_f = me.astype(f32)
    wide = 512

    def columns(body, size=wide, full=width):
        @pl.loop(0, full // size)
        def _(i):
            body(pl.ds(pl.multiple_of(i * size, size), size))

    def hits_of(zz, h):
        got = meta_all[pl.ds(8 * zz + 4 * h, 4)].reshape(gtok, 128)
        lane = lax.broadcasted_iota(jnp.int32, (gtok, 128), 1)
        return got, lane, jnp.where((got == me_f) & (lane < tops), 1.0, 0.0)

    def prob_of(zz, h):
        got, _, hit = hits_of(zz, h)
        return jnp.sum(pltpu.roll(hit, tops, 1) * got, axis=1, keepdims=True)

    def route(zz):
        for h in range(2):
            _, lane, hit = hits_of(zz, h)
            member = jnp.sum(hit, axis=1, keepdims=True)
            a = lax.broadcasted_iota(jnp.int32, (gtok, gtok), 0)
            b = lax.broadcasted_iota(jnp.int32, (gtok, gtok), 1)
            earlier = jnp.where((a > b) & (a // own == b // own), 1.0, 0.0).astype(bf16)
            spot = dot(earlier, jnp.broadcast_to(member, (gtok, 128)).astype(bf16), 1, 0)
            block = lax.broadcasted_iota(jnp.int32, (gtok, 128), 0) // own
            spot = spot + (block * capacity).astype(f32)
            picked = (spot == lane.astype(f32)) & (member > 0.0)
            choose[2 * zz + h] = jnp.where(picked, 1.0, 0.0).astype(bf16)

    def slots(zz, h=None):
        if h is None:
            return pl.ds(pl.multiple_of(zz * pslots, pslots), pslots)
        return pl.ds(pl.multiple_of(zz * pslots + h * gslots, gslots), gslots)

    def forward(zz):
        route(zz)
        for h in range(2):
            pick = choose[2 * zz + h]

            def pack(cols, pick=pick, h=h):
                rows = normed_all[pl.ds(8 * zz + 4 * h, 4), :, cols].reshape(gtok, wide)
                inputs[slots(zz, h), cols] = dot(pick, rows, 0, 0).astype(bf16)

            columns(pack)
        rows = slots(zz)

        def products(cols):
            gate = dot(inputs[rows], w_gate[:, cols], 1, 0)
            up = dot(inputs[rows], w_up[:, cols], 1, 0)
            gate_pre[rows, cols] = gate
            up_pre[rows, cols] = up
            act[rows, cols] = (gate * jax.nn.sigmoid(gate) * up).astype(bf16)

        columns(products, 256, inner)

    def result(zz):
        rows = slots(zz)
        probs = [prob_of(zz, h) for h in range(2)]

        def expand(cols):
            done = dot(act[rows], w_down[:, cols], 1, 0).astype(bf16)
            for h in range(2):
                got = dot(choose[2 * zz + h], done[h * gslots:(h + 1) * gslots], 1, 0)
                normed_all[pl.ds(8 * zz + 4 * h, 4), :, cols] = (
                    (got * probs[h]).astype(bf16).reshape(4, own, wide)
                )

        columns(expand)

    def fetch(step):
        zz = s_back.order(step)
        return pltpu.make_async_copy(grads_all.at[pl.ds(8 * zz, 8)], stage, stage_sem)

    def cotangent(step):
        zz = s_back.order(step)
        fetch(step).wait()
        for h in range(2):
            pick, prob = choose[2 * zz + h], prob_of(zz, h)

            def pack(cols, pick=pick, prob=prob, h=h):
                rows = stage[4 * h:4 * h + 4, :, cols].reshape(gtok, wide).astype(f32)
                scaled = (rows * prob).astype(bf16)
                cotan[slots(zz, h), cols] = dot(pick, scaled, 0, 0).astype(bf16)

            columns(pack)
        if step < line - 1:
            fetch(step + 1).start()

    def hidden_grads(zz):
        rows = slots(zz)
        ggs[...] = jnp.zeros_like(ggs)

        def chunk(cols):
            act_grad = dot(cotan[rows], w_down[cols], 1, 1)
            one, two = row_grads(act_grad, gate_pre[rows, cols], up_pre[rows, cols])
            gate_pgrad[rows, cols] = one
            up_pgrad[rows, cols] = two
            both = act_grad * act[rows, cols].astype(f32)
            ggs[...] += both[:, :128] + both[:, 128:]

        columns(chunk, 256, inner)
        for h in range(2):
            line_sum = jnp.sum(ggs[h * gslots:(h + 1) * gslots].T, axis=0, keepdims=True)
            high = line_sum.astype(bf16).astype(f32)
            which = lax.broadcasted_iota(jnp.int32, (16, gslots), 0)
            parts = jnp.where(which == 0, high, jnp.where(which == 1, line_sum - high, 0.0))
            spread = dot(parts.astype(bf16), choose[2 * zz + h], 1, 1)
            row = jnp.sum(spread, axis=0, keepdims=True)
            for k in range(gtok // 128):
                small[pl.ds(4 * zz + 2 * h + k, 1)] = row[:, 128 * k:128 * k + 128]

    def backs(zz):
        rows = slots(zz)

        def chunk(cols):
            back = dot(gate_pgrad[rows], w_gate[cols], 1, 1)
            back = (back + dot(up_pgrad[rows], w_up[cols], 1, 1)).astype(bf16)
            terms = back.astype(f32) * inputs[rows, cols].astype(f32)
            gacc[:, cols] += jnp.sum(terms.reshape(pslots // 8, 8, wide), axis=0)
            for h in range(2):
                got = dot(choose[2 * zz + h], back[h * gslots:(h + 1) * gslots], 1, 0)
                normed_all[pl.ds(8 * zz + 4 * h, 4), :, cols] = (
                    got.astype(bf16).reshape(4, own, wide)
                )

        columns(chunk)

    def weight_grads(step):
        deep = 256
        share = width // deep // 4

        @pl.loop(step * share, (step + 1) * share)
        def _(i):
            cols = pl.ds(pl.multiple_of(i * deep, deep), deep)
            block = inputs[:, cols]
            w_gate[cols] = dot(block, gate_pgrad[...], 0, 0).astype(bf16)
            w_up[cols] = dot(block, up_pgrad[...], 0, 0).astype(bf16)

        if step * deep < inner:
            rows = pl.ds(step * deep, deep)

            def chunk(cols):
                w_down[rows, cols] = dot(act[:, rows], cotan[:, cols], 0, 0).astype(bf16)

            columns(chunk)

    g_meta.slot(0)
    g_norm.slot(0)
    for copy in loads:
        copy.start()
    gacc[...] = jnp.zeros_like(gacc)
    for step in range(1, line + 2):
        g_meta.slot(step)
        g_norm.slot(step)
        g_grad.slot(step - (line - 1))
        if step >= 3:
            g_meta.done(step - 3)
            g_norm.done(step - 3)
            if step == 3:
                for copy in loads:
                    copy.wait()
            forward(g_norm.order(step - 3))
    g_grad.slot(3)
    g_meta.done(line - 1)
    g_norm.done(line - 1)
    forward(g_norm.order(line - 1))
    g_norm.sent()
    result(s_out.order(0))
    s_out.give(0)
    g_grad.slot(4)
    result(s_out.order(1))
    s_out.give(1)
    s_out.corner(0)
    g_grad.slot(5)
    result(s_out.order(2))
    s_out.give(2)
    s_out.corner(1)
    s_out.plane(0)
    result(s_out.order(3))
    s_out.give(3)
    s_out.corner(2)
    s_out.plane(1)
    s_out.column(0)
    for step in range(line):
        g_grad.done(step)
    fetch(0).start()
    s_out.corner(3)
    s_out.plane(2)
    s_out.column(1)
    s_out.given()

    def backward(step):
        zz = s_back.order(step)
        cotangent(step)
        hidden_grads(zz)
        backs(zz)
        s_back.give(step)

    backward(0)
    s_out.plane(3)
    s_out.column(2)
    backward(1)
    s_back.corner(0)
    s_out.column(3)

    @pl.loop(0, own // 16)
    def _(i):
        rows = pl.ds(pl.multiple_of(i * 16, 16), 16)
        layer_out[rows] = (hid[rows].astype(f32) + total[rows]).astype(bf16)

    backward(2)
    s_back.corner(1)
    s_back.plane(0)
    backward(3)
    gsum = jnp.sum(gacc[...], axis=0, keepdims=True)
    first = small.shape[0] - width // 128
    for k in range(width // 128):
        small[first + k:first + k + 1] = gsum[:, 128 * k:128 * k + 128]
    g_small.slot(0)
    s_back.corner(2)
    s_back.plane(1)
    s_back.column(0)
    weight_grads(0)
    g_small.slot(1)
    s_back.corner(3)
    s_back.plane(2)
    s_back.column(1)
    weight_grads(1)
    g_small.slot(2)
    s_back.plane(3)
    s_back.column(2)
    weight_grads(2)
    g_small.slot(3)
    weight_grads(3)
    g_small.slot(4)
    s_back.column(3)

    @pl.loop(0, own // 16)
    def _(i):
        rows = pl.ds(pl.multiple_of(i * 16, 16), 16)
        values, inverse = unit_of(rows)
        unit = values * inverse
        upstream = total[rows] * gain[...]
        mean = jnp.mean(upstream * unit, axis=-1, keepdims=True)
        grad = out_grad[rows].astype(f32) + inverse * (upstream - unit * mean)
        own_grad[rows] = grad.astype(bf16)

    other = (1 - p.y) * 2 + p.c
    partner = p.device(p.z, 0, 1 - p.c)

    def tremote(src, where, i, device):
        return pltpu.make_async_remote_copy(
            src_ref=src, dst_ref=rows_out.at[where], send_sem=tsend.at[i], recv_sem=trecv.at[i],
            device_id=device, device_id_type=MESH,
        )

    across = tremote(own_grad, quarter, 0, p.device(p.z, 2, p.c))
    beside = tremote(own_grad, quarter, 1, partner)
    relay = tremote(rows_out.at[other], other, 2, partner)
    across.start()
    beside.start()
    keeping = pltpu.make_async_copy(own_grad, rows_out.at[quarter], tkeep)
    keeping.start()
    g_small.slot(5)
    for step in range(line):
        g_small.done(step)
    gain_out[...] = jnp.sum(small_all[:, first:], axis=0)
    gg_out[...] = small_all[:, pl.ds(me // 2, 1)].reshape(gg_out.shape)
    across.wait_recv()
    relay.start()
    g_meta.sent()
    g_grad.sent()
    g_small.sent()
    s_out.sent()
    s_back.given()
    s_back.sent()
    beside.wait_recv()
    relay.wait_recv()
    for copy in (across, beside, relay):
        copy.wait_send()
    keeping.wait()


def whole_layer(ids, probs, hidden, gain, out_grad, w_gate, w_up, w_down, capacity):
    line = lax.axis_size("dp") // 2
    devices, quarters = lax.axis_size(AXES), lax.axis_size("tensor")
    own, width = out_grad.shape
    inner = w_gate.shape[1]
    groups, gtok, gslots = devices // 4, own * 4, capacity * 4
    slots = groups * gslots
    small_rows = devices * own // 128 + width // 128
    anywhere, vmem = pl.BlockSpec(memory_space=pl.ANY), pl.BlockSpec(memory_space=pltpu.VMEM)
    shape = jax.ShapeDtypeStruct
    dma = pltpu.SemaphoreType.DMA
    passing = [
        pltpu.VMEM((line, 4, own, width), bf16),
        pltpu.VMEM((2, 2, own // 2, width), bf16),
        pltpu.VMEM((line, own, width), bf16),
        pltpu.VMEM((line, own, width), bf16),
        pltpu.VMEM((line, own, width), bf16),
        pltpu.VMEM((line, own, width), bf16),
        pltpu.VMEM((2, own, width), bf16),
        pltpu.VMEM((2, own, width), bf16),
    ]
    return pl.pallas_call(
        functools.partial(layer_kernel, line, ids.shape[0], capacity),
        out_shape=[
            pltpu.VMEM((own, width), bf16),
            pltpu.VMEM((quarters, own, width), bf16),
            pltpu.VMEM((devices, 128), f32),
            pltpu.VMEM((width // 128, 128), f32),
            pltpu.VMEM(w_gate.shape, bf16),
            pltpu.VMEM(w_up.shape, bf16),
            pltpu.VMEM(w_down.shape, bf16),
            shape((devices, own, width), bf16),
        ],
        in_specs=[vmem, vmem, anywhere, vmem, vmem, anywhere, anywhere, anywhere],
        out_specs=[vmem] * 7 + [anywhere],
        scratch_shapes=[
            pltpu.VMEM((128, 128), f32),
            pltpu.VMEM((own, 128), f32),
            pltpu.VMEM((devices, own, 128), f32),
            pltpu.VMEM((devices, own, width), bf16),
            pltpu.VMEM((own, width), bf16),
            pltpu.VMEM((own, width), bf16),
            pltpu.VMEM((slots, width), bf16),
            pltpu.VMEM((slots, width), bf16),
            pltpu.VMEM((8, own, width), bf16),
            pltpu.VMEM((groups, gtok, gslots), bf16),
            pltpu.VMEM((slots, inner), f32),
            pltpu.VMEM((slots, inner), f32),
            pltpu.VMEM((slots, inner), bf16),
            pltpu.VMEM((slots, inner), bf16),
            pltpu.VMEM((slots, inner), bf16),
            pltpu.VMEM((2 * gslots, 128), f32),
            pltpu.VMEM((8, width), f32),
            pltpu.VMEM((small_rows, 128), f32),
            pltpu.VMEM((devices, small_rows, 128), f32),
            pltpu.VMEM((own, width), f32),
            pltpu.VMEM((own, width), bf16),
        ] + passing + passing + [
            dma((4, 12, line)),
            dma((4, 12, line)),
            dma((4,)),
            dma((2, 12, line)),
            dma((2, 12, line)),
            dma((4,)),
            dma,
            dma((3,)),
            dma((3,)),
            dma,
        ],
        compiler_params=pltpu.CompilerParams(
            collective_id=0, has_side_effects=True, vmem_limit_bytes=53 * 2**20
        ),
        name="layer",
    )(ids, probs, hidden, gain, out_grad, w_gate, w_up, w_down)


def finish_kernel(
    layer, rows, gg, gain_sum, gate_wgrad, up_wgrad, down_wgrad, ids, probs, gain,
    layer_out, rows_out, gate_grad, gain_grad, gate_out, up_out, down_out, sems,
):
    pairs = [
        (layer, layer_out), (rows, rows_out), (gate_wgrad, gate_out), (up_wgrad, up_out),
        (down_wgrad, down_out),
    ]
    copies = []
    for a, b in pairs:
        count = a.shape[0] // 4
        for i in range(4):
            part = pl.ds(i * count, count)
            copies.append(pltpu.make_async_copy(a.at[part], b.at[part], sems.at[len(copies)]))
    for copy in copies:
        copy.start()
    own = ids.shape[1]
    tensor, dp = lax.axis_index("tensor"), lax.axis_index("dp")
    odd = (dp * 4 + tensor) % 2 == 1
    found = jnp.where(odd, gg[:, own:2 * own], gg[:, 0:own])
    device = lax.broadcasted_iota(jnp.int32, found.shape, 0)
    for k in range(ids.shape[0]):
        hit = device == ids[k:k + 1]
        value = jnp.sum(jnp.where(hit, found, 0.0), axis=0, keepdims=True)
        gate_grad[k:k + 1] = value / probs[k:k + 1]
    gain_grad[...] = gain_sum[...] / gain[...]
    for copy in copies:
        copy.wait()


def finish(*arrays):
    layer, rows, gg, gain_sum, gate_wgrad, up_wgrad, down_wgrad, ids, probs, gain = arrays
    anywhere, vmem = pl.BlockSpec(memory_space=pl.ANY), pl.BlockSpec(memory_space=pltpu.VMEM)
    return pl.pallas_call(
        finish_kernel,
        out_shape=[
            jax.ShapeDtypeStruct(a.shape, a.dtype)
            for a in (layer, rows, probs, gain, gate_wgrad, up_wgrad, down_wgrad)
        ],
        in_specs=[anywhere, anywhere, vmem, vmem, anywhere, anywhere, anywhere, vmem, vmem, vmem],
        out_specs=[anywhere, anywhere, vmem, vmem, anywhere, anywhere, anywhere],
        scratch_shapes=[pltpu.SemaphoreType.DMA((20,))],
        compiler_params=pltpu.CompilerParams(vmem_limit_bytes=4 * 2**20),
        name="finish",
    )(*arrays)


def per_device_whole(
    hidden, norm_gain, expert_ids, gate_probs, out_grad, gate_weight, up_weight, down_weight
):
    own_count, width = out_grad.shape
    top_count = expert_ids.shape[1]
    capacity = 2 * own_count * top_count // lax.axis_size(AXES)
    ids, probs = expert_ids.T, gate_probs.T
    *results, _ = whole_layer(
        ids, probs, hidden, norm_gain[None], out_grad, gate_weight[0], up_weight[0],
        down_weight[0], capacity,
    )
    layer_out, input_grad, gate_grad, gain_grad, gate_wgrad, up_wgrad, down_grad = finish(
        *results, ids, probs, norm_gain.reshape(-1, 128)
    )
    return (
        layer_out, input_grad.reshape(hidden.shape), gate_grad.T, gain_grad.reshape(width),
        gate_wgrad[None], up_wgrad[None], down_grad[None],
    )


def choose_form(*arrays):
    hidden, _, expert_ids, _, out_grad = arrays[:5]
    devices = lax.axis_size(AXES)
    capacity = 2 * out_grad.shape[0] * expert_ids.shape[1] // devices
    fits = devices <= 32 and capacity * 4 == 128 and out_grad.shape[0] == 64
    return (per_device_whole if fits else per_device)(*arrays)


def solution(mesh):
    rows, wide = P(AXES, None), P(AXES, None, None)
    in_specs = (P("dp", None), P(), rows, rows, rows, wide, wide, wide)
    out_specs = (rows, P("dp", None), rows, P(), wide, wide, wide)
    return jax.shard_map(
        choose_form, mesh=mesh, in_specs=in_specs, out_specs=out_specs, check_vma=False
    )
```

```python
import functools

import jax
import jax.numpy as jnp
from jax import lax
from jax.experimental import pallas as pl
from jax.experimental.pallas import tpu as pltpu
from jax.sharding import PartitionSpec as P

epsilon = 1e-06
AXES = ("dp", "tensor")
MESH = pl.DeviceIdType.MESH
f32, bf16 = jnp.float32, jnp.bfloat16


class Place:
    def __init__(self, line):
        self.line = line
        dp, tensor = lax.axis_index("dp"), lax.axis_index("tensor")
        self.z, self.x = dp // 2, dp % 2
        self.y, self.c = tensor // 2, tensor % 2

    def block(self, z, flip):
        x = 1 - self.x if flip in (1, 3) else self.x
        y = 1 - self.y if flip in (2, 3) else self.y
        return x, y

    def index(self, z, flip, c):
        x, y = self.block(z, flip)
        return (z * 2 + x) * 4 + y * 2 + c

    def device(self, z, flip, c):
        x, y = self.block(z, flip)
        return (z * 2 + x, y * 2 + c)

    def order(self, step, farthest_first):
        result = jnp.int32(0)
        for own in range(self.line):
            listed = sorted(range(self.line), key=lambda p: (abs(p - own), p))
            if farthest_first:
                listed = listed[::-1]
            result = jnp.where(self.z == own, jnp.int32(listed[step]), result)
        return result

    def greet(self):
        barrier = pltpu.get_barrier_semaphore()

        def tell(device):
            pl.semaphore_signal(barrier, inc=1, device_id=device, device_id_type=MESH)

        for flip, c in ((1, self.c), (2, self.c), (0, 1 - self.c)):
            tell(self.device(self.z, flip, c))
        below, above = self.z > 0, self.z < self.line - 1
        pl.when(below)(lambda: tell(self.device(self.z - 1, 0, self.c)))
        pl.when(above)(lambda: tell(self.device(self.z + 1, 0, self.c)))
        pl.semaphore_wait(barrier, 3 + below.astype(jnp.int32) + above.astype(jnp.int32))


UP, DOWN, SIDE, FACE, HALF0, HALF1, CORE = 0, 1, 2, 3, 4, 5, 6


class Gather:
    def __init__(self, place, own, held, send, recv, keep):
        self.p, self.own, self.held = place, own, held
        self.send, self.recv, self.keep = send, recv, keep
        self.half = own.shape[0] // 2

    def landing(self, kind):
        return kind

    def copy(self, kind, zz, flip, part, device, own=False):
        where = self.p.index(zz, flip, self.p.c)
        dst = self.held.at[where]
        src = self.own if own else dst
        if part is not None:
            rows = pl.ds(part * self.half, self.half)
            src, dst = src.at[rows], dst.at[rows]
        return pltpu.make_async_remote_copy(
            src_ref=src, dst_ref=dst, send_sem=self.send.at[kind, zz],
            recv_sem=self.recv.at[self.landing(kind), zz], device_id=device,
            device_id_type=MESH,
        )

    def up(self, zz, own=False):
        return self.copy(UP, zz, 0, None, self.p.device(self.p.z + 1, 0, self.p.c), own)

    def down(self, zz, own=False):
        return self.copy(DOWN, zz, 0, None, self.p.device(self.p.z - 1, 0, self.p.c), own)

    def side(self, zz, own=False):
        return self.copy(SIDE, zz, 0, None, self.p.device(self.p.z, 1, self.p.c), own)

    def face(self, zz, own=False):
        return self.copy(FACE, zz, 0, None, self.p.device(self.p.z, 2, self.p.c), own)

    def half0(self, zz):
        return self.copy(HALF0, zz, 1, 0, self.p.device(self.p.z, 2, self.p.c))

    def half1(self, zz):
        return self.copy(HALF1, zz, 2, 1, self.p.device(self.p.z, 1, self.p.c))

    def core(self, zz, flip, own=False):
        return self.copy(CORE + flip, zz, flip, None, self.p.device(self.p.z, 0, 1 - self.p.c), own)

    def arrived(self, kind, zz, flip, part, c=None):
        where = self.p.index(zz, flip, self.p.c if c is None else c)
        dst = self.held.at[where]
        if part is not None:
            dst = dst.at[pl.ds(part * self.half, self.half)]
        pltpu.make_async_remote_copy(
            src_ref=dst, dst_ref=dst, send_sem=self.send.at[kind, zz],
            recv_sem=self.recv.at[self.landing(kind), zz],
            device_id=self.p.device(self.p.z, 0, 1 - self.p.c), device_id_type=MESH,
        ).wait_recv()

    def first(self):
        p = self.p
        pltpu.make_async_copy(self.own, self.held.at[p.index(p.z, 0, p.c)], self.keep).start()
        pl.when(p.z < p.line - 1)(lambda: self.up(p.z, True).start())
        pl.when(p.z > 0)(lambda: self.down(p.z, True).start())
        self.side(p.z, True).start()
        self.face(p.z, True).start()
        self.core(p.z, 0, True).start()

    def column(self, step):
        p, zz = self.p, self.p.order(step, False)

        @pl.when(zz < p.z)
        def _():
            self.arrived(UP, zz, 0, None)
            pl.when(p.z < p.line - 1)(lambda: self.up(zz).start())

        @pl.when(zz > p.z)
        def _():
            self.arrived(DOWN, zz, 0, None)
            pl.when(p.z > 0)(lambda: self.down(zz).start())

        self.side(zz).start()
        self.face(zz).start()
        self.core(zz, 0).start()

    def plane(self, step):
        zz = self.p.order(step, False)
        self.arrived(SIDE, zz, 1, None)
        self.half0(zz).start()
        self.core(zz, 1).start()
        self.arrived(FACE, zz, 2, None)
        self.half1(zz).start()
        self.core(zz, 2).start()

    def corner(self, step):
        zz = self.p.order(step, False)
        self.arrived(HALF0, zz, 3, 0)
        self.arrived(HALF1, zz, 3, 1)
        self.core(zz, 3).start()

    def slot(self, step):
        line = self.p.line
        if step == 0:
            self.first()
        elif 0 < step < line:
            self.column(step)
        if 0 <= step - 1 < line:
            self.plane(step - 1)
        if 0 <= step - 2 < line:
            self.corner(step - 2)

    def finish(self):
        p = self.p
        for zz in range(p.line):
            for flip in range(4):
                self.arrived(CORE + flip, zz, flip, None, 1 - p.c)
        for zz in range(p.line):
            pl.when((zz <= p.z) & (p.z < p.line - 1))(lambda zz=zz: self.up(zz).wait_send())
            pl.when((zz >= p.z) & (p.z > 0))(lambda zz=zz: self.down(zz).wait_send())
            for one in (self.side(zz), self.face(zz), self.half0(zz), self.half1(zz)):
                one.wait_send()
            for flip in range(4):
                self.core(zz, flip).wait_send()
        pltpu.make_async_copy(self.own, self.held.at[p.index(p.z, 0, p.c)], self.keep).wait()


def gather_kernel(line, offsets, *refs):
    count = len(offsets)
    owns, helds = refs[:count], refs[count:2 * count]
    send, recv, keep = refs[2 * count:]
    place = Place(line)
    place.greet()
    arrays = [
        Gather(place, owns[i], helds[i], send.at[i], recv.at[i], keep.at[i]) for i in range(count)
    ]
    for step in range(max(offsets) + line + 2):
        for one, offset in zip(arrays, offsets):
            one.slot(step - offset)
    for one in arrays:
        one.finish()


def gather_all(arrays, offsets, number):
    line = lax.axis_size("dp") // 2
    devices = lax.axis_size(AXES)
    count = len(arrays)
    return pl.pallas_call(
        functools.partial(gather_kernel, line, offsets),
        out_shape=[jax.ShapeDtypeStruct((devices,) + a.shape, a.dtype) for a in arrays],
        in_specs=[pl.BlockSpec(memory_space=pltpu.VMEM)] * count,
        out_specs=[pl.BlockSpec(memory_space=pl.ANY)] * count,
        scratch_shapes=[
            pltpu.SemaphoreType.DMA((count, 10, line)),
            pltpu.SemaphoreType.DMA((count, 10, line)),
            pltpu.SemaphoreType.DMA((count,)),
        ],
        compiler_params=pltpu.CompilerParams(collective_id=number, has_side_effects=True),
        name=f"gather{number}",
    )(*arrays)


def add_rows(start, count, store, *loads):
    chunk = 16

    @pl.loop(0, count // chunk)
    def _(i):
        rows = pl.ds(pl.multiple_of(start + i * chunk, chunk), chunk)
        total = loads[0](rows).astype(f32)
        for load in loads[1:]:
            total = total + load(rows).astype(f32)
        store(rows, total)


def dot(a, b, ca, cb):
    return lax.dot_general(a, b, (((ca,), (cb,)), ((), ())), preferred_element_type=f32)


def row_grads(act_grad, gate_pre, up_pre):
    sigma = jax.nn.sigmoid(gate_pre)
    gate_pgrad = act_grad * up_pre * sigma * (1.0 + gate_pre * (1.0 - sigma))
    return gate_pgrad.astype(bf16), (act_grad * (gate_pre * sigma)).astype(bf16)


def backward_plain(cotan, gate_pre, up_pre, w_down, w_gate, w_up):
    gate_pgrad, up_pgrad = row_grads(dot(cotan, w_down, 1, 1), gate_pre, up_pre)
    back = dot(gate_pgrad, w_gate, 1, 1) + dot(up_pgrad, w_up, 1, 1)
    return gate_pgrad, up_pgrad, back.astype(bf16)


def backward_tile(step, ready, ins, outs):
    cotan, gate_pre, up_pre, w_down, w_gate, w_up = ins
    gate_pgrad, up_pgrad, back = outs
    if step == 0:
        ready(0, 1, 2, 3)
    count = cotan.shape[0] // 4
    rows = pl.ds(step * count, count)
    one, two = row_grads(dot(cotan[rows], w_down[...], 1, 1), gate_pre[rows], up_pre[rows])
    gate_pgrad[rows] = one
    up_pgrad[rows] = two
    if step == 0:
        ready(4, 5)
    wide = 512

    @pl.loop(0, back.shape[1] // wide)
    def _(i):
        cols = pl.ds(pl.multiple_of(i * wide, wide), wide)
        total = dot(gate_pgrad[rows], w_gate[cols], 1, 1) + dot(up_pgrad[rows], w_up[cols], 1, 1)
        back[rows, cols] = total.astype(bf16)


def weights_plain(inputs, gate_pgrad, up_pgrad, act, cotan):
    return tuple(
        dot(a, b, 0, 0).astype(bf16)
        for a, b in ((inputs, gate_pgrad), (inputs, up_pgrad), (act, cotan))
    )


def weights_tile(step, ready, ins, outs):
    inputs, gate_pgrad, up_pgrad, act, cotan = ins
    gate_wgrad, up_wgrad, down_grad = outs
    if step == 0:
        ready(0, 1, 2)
    deep, wide = 256, 512
    share = inputs.shape[1] // deep // 4

    @pl.loop(step * share, (step + 1) * share)
    def _(i):
        cols = pl.ds(pl.multiple_of(i * deep, deep), deep)
        block = inputs[:, cols]
        gate_wgrad[cols] = dot(block, gate_pgrad[...], 0, 0).astype(bf16)
        up_wgrad[cols] = dot(block, up_pgrad[...], 0, 0).astype(bf16)

    if step == 0:
        ready(3, 4)
    if step * deep < act.shape[1]:
        rows = pl.ds(step * deep, deep)

        @pl.loop(0, cotan.shape[1] // wide)
        def _(i):
            cols = pl.ds(pl.multiple_of(i * wide, wide), wide)
            down_grad[rows, cols] = dot(act[:, rows], cotan[:, cols], 0, 0).astype(bf16)


def scatter_kernel(line, job, n_in, n_out, *refs):
    part, refs = refs[0], refs[1:]
    job_in, refs = refs[:n_in], refs[n_in:]
    out, refs = refs[0], refs[1:]
    job_out, refs = refs[:n_out], refs[n_out:]
    mine, theirs, half_in, side_in, face_in, up_in, down_in, send, recv, keep = refs[:10]
    held_in, held_out = refs[10:10 + n_in], refs[10 + n_in:10 + n_in + n_out]
    if job is not None:
        in_sem, out_sem = refs[10 + n_in + n_out:]
        arriving = [
            pltpu.make_async_copy(job_in[i], held_in[i], in_sem.at[i]) for i in range(n_in)
        ]
        leaving = [
            pltpu.make_async_copy(held_out[i], job_out[i], out_sem.at[i]) for i in range(n_out)
        ]

    def ready(*which):
        for i in which:
            arriving[i].wait()

    p = Place(line)
    p.greet()
    count = out.shape[0]
    half = count // 2
    z = p.z

    def put(ref, index):
        def store(rows, value):
            ref[index + (rows,)] = value.astype(ref.dtype)
        return store

    def get(ref, index):
        return lambda rows: ref[index + (rows,)]

    def remote(src, dst, kind, zz, device):
        return pltpu.make_async_remote_copy(
            src_ref=src, dst_ref=dst, send_sem=send.at[kind, zz], recv_sem=recv.at[kind, zz],
            device_id=device, device_id_type=MESH,
        )

    def core(zz, flip):
        return remote(
            part.at[p.index(zz, flip, 1 - p.c)], theirs.at[zz, flip], CORE + flip, zz,
            p.device(z, 0, 1 - p.c),
        )

    def load(zz, flip):
        return pltpu.make_async_copy(
            part.at[p.index(zz, flip, p.c)], mine.at[zz, flip], keep.at[flip, zz]
        )

    def half0(zz):
        return remote(
            theirs.at[zz, 3, pl.ds(0, half)], half_in.at[zz, 0], HALF0, zz, p.device(z, 2, p.c)
        )

    def half1(zz):
        return remote(
            theirs.at[zz, 3, pl.ds(half, half)], half_in.at[zz, 1], HALF1, zz, p.device(z, 1, p.c)
        )

    def side(zz):
        return remote(theirs.at[zz, 1], side_in.at[zz], SIDE, zz, p.device(z, 1, p.c))

    def face(zz):
        return remote(theirs.at[zz, 2], face_in.at[zz], FACE, zz, p.device(z, 2, p.c))

    def up(zz):
        return remote(theirs.at[zz, 0], up_in.at[zz], UP, zz, p.device(z + 1, 0, p.c))

    def down(zz):
        return remote(theirs.at[zz, 0], down_in.at[zz], DOWN, zz, p.device(z - 1, 0, p.c))

    def joined(zz, flip):
        core(zz, flip).wait_recv()
        load(zz, flip).wait()
        add_rows(
            0, count, put(theirs, (zz, flip)), get(theirs, (zz, flip)), get(mine, (zz, flip))
        )

    for step in range(line):
        zz = p.order(step, True)
        for flip in (3, 1, 2, 0):
            core(zz, flip).start()
            load(zz, flip).start()

    if job is not None:
        for copy in arriving:
            copy.start()

    def corner(step):
        zz = p.order(step, True)
        joined(zz, 3)
        half0(zz).start()
        half1(zz).start()
        for flip in (1, 2, 0):
            joined(zz, flip)

    def plane(step):
        zz = p.order(step, True)
        half0(zz).wait_recv()
        here = (zz, 1)
        add_rows(
            0, half, put(theirs, here), get(theirs, here), get(half_in, (zz, 0))
        )
        side(zz).start()
        half1(zz).wait_recv()

        @pl.loop(0, half // 16)
        def _(i):
            low = pl.ds(pl.multiple_of(i * 16, 16), 16)
            high = pl.ds(pl.multiple_of(half + i * 16, 16), 16)
            total = theirs[zz, 2, high].astype(f32) + half_in[zz, 1, low].astype(f32)
            theirs[zz, 2, high] = total.astype(bf16)

        face(zz).start()

    def column(step):
        zz = p.order(step, True)
        side(zz).wait_recv()
        face(zz).wait_recv()
        base = (get(theirs, (zz, 0)), get(side_in, (zz,)), get(face_in, (zz,)))
        if step == line - 1:
            add_rows(0, count, put(out, ()), *base)

            @pl.when(z > 0)
            def _():
                up(zz).wait_recv()
                add_rows(0, count, put(out, ()), get(out, ()), get(up_in, (zz,)))

            @pl.when(z < line - 1)
            def _():
                down(zz).wait_recv()
                add_rows(0, count, put(out, ()), get(out, ()), get(down_in, (zz,)))

            return

        def onward(copy, source, more):
            @pl.when(more)
            def _():
                copy(zz).wait_recv()
                add_rows(0, count, put(theirs, (zz, 0)), *base, get(source, (zz,)))

            @pl.when(jnp.logical_not(more))
            def _():
                add_rows(0, count, put(theirs, (zz, 0)), *base)

            copy(zz).start()

        pl.when(zz > z)(lambda: onward(up, up_in, z > 0))
        pl.when(zz < z)(lambda: onward(down, down_in, z < line - 1))

    for step in range(line + 2):
        if step < line:
            corner(step)
        if 0 <= step - 1 < line:
            plane(step - 1)
        if 0 <= step - 2 < line:
            column(step - 2)
        if job is not None and step < 4:
            job(step, ready, held_in, held_out)
            if step == 3:
                for copy in leaving:
                    copy.start()

    for zz in range(line):
        for flip in range(4):
            core(zz, flip).wait_send()
        for one in (half0, half1, side, face):
            one(zz).wait_send()
        pl.when(zz > z)(lambda zz=zz: up(zz).wait_send())
        pl.when(zz < z)(lambda zz=zz: down(zz).wait_send())
    if job is not None:
        for copy in leaving:
            copy.wait()


def scatter_sum(part, number, job, plain, arrays):
    line = lax.axis_size("dp") // 2
    _, rows, width = part.shape
    results = jax.eval_shape(plain, *arrays)
    size = sum(a.size * a.dtype.itemsize for a in list(arrays) + list(results))
    extra = None
    if size + 13 * line * rows * width * 2 > 52 * 2**20:
        extra, job, arrays, results = plain(*arrays), None, (), ()
    anywhere = pl.BlockSpec(memory_space=pl.ANY)
    more = []
    if job is not None:
        more = [pltpu.VMEM(a.shape, a.dtype) for a in list(arrays) + list(results)] + [
            pltpu.SemaphoreType.DMA((len(arrays),)),
            pltpu.SemaphoreType.DMA((len(results),)),
        ]
    total, *done = pl.pallas_call(
        functools.partial(scatter_kernel, line, job, len(arrays), len(results)),
        out_shape=[jax.ShapeDtypeStruct((rows, width), f32)]
        + [jax.ShapeDtypeStruct(r.shape, r.dtype) for r in results],
        in_specs=[anywhere] * (1 + len(arrays)),
        out_specs=[pl.BlockSpec(memory_space=pltpu.VMEM)] + [anywhere] * len(results),
        scratch_shapes=[
            pltpu.VMEM((line, 4, rows, width), bf16),
            pltpu.VMEM((line, 4, rows, width), bf16),
            pltpu.VMEM((line, 2, rows // 2, width), bf16),
            pltpu.VMEM((line, rows, width), bf16),
            pltpu.VMEM((line, rows, width), bf16),
            pltpu.VMEM((line, rows, width), bf16),
            pltpu.VMEM((line, rows, width), bf16),
            pltpu.SemaphoreType.DMA((10, line)),
            pltpu.SemaphoreType.DMA((10, line)),
            pltpu.SemaphoreType.DMA((4, line)),
        ] + more,
        compiler_params=pltpu.CompilerParams(
            collective_id=number, has_side_effects=True, vmem_limit_bytes=62 * 2**20
        ),
        name=f"scatter{number}",
    )(part, *arrays)
    return total, tuple(done) if extra is None else extra


def last_kernel(line, small, grad, held, rows_out, send, recv, keep, tsend, trecv, tkeep):
    p = Place(line)
    p.greet()
    here = p.y * 2 + p.c
    other = (1 - p.y) * 2 + p.c

    def tremote(src, where, i, device):
        return pltpu.make_async_remote_copy(
            src_ref=src, dst_ref=rows_out.at[where], send_sem=tsend.at[i], recv_sem=trecv.at[i],
            device_id=device, device_id_type=MESH,
        )

    partner = p.device(p.z, 0, 1 - p.c)
    keeping = pltpu.make_async_copy(grad, rows_out.at[here], tkeep)
    keeping.start()
    across = tremote(grad, here, 0, p.device(p.z, 2, p.c))
    beside = tremote(grad, here, 1, partner)
    relay = tremote(rows_out.at[other], other, 2, partner)
    across.start()
    beside.start()
    one = Gather(p, small, held, send, recv, keep)
    for step in range(line + 2):
        one.slot(step)
        if step == 1:
            across.wait_recv()
            relay.start()
    one.finish()
    beside.wait_recv()
    relay.wait_recv()
    for copy in (across, beside, relay):
        copy.wait_send()
    keeping.wait()


def gather_last(small, grad, number):
    line = lax.axis_size("dp") // 2
    devices, quarters = lax.axis_size(AXES), lax.axis_size("tensor")
    anywhere = pl.BlockSpec(memory_space=pl.ANY)
    return pl.pallas_call(
        functools.partial(last_kernel, line),
        out_shape=[
            jax.ShapeDtypeStruct((devices,) + small.shape, small.dtype),
            jax.ShapeDtypeStruct((quarters,) + grad.shape, grad.dtype),
        ],
        in_specs=[pl.BlockSpec(memory_space=pltpu.VMEM)] * 2,
        out_specs=[anywhere, anywhere],
        scratch_shapes=[
            pltpu.SemaphoreType.DMA((10, line)),
            pltpu.SemaphoreType.DMA((10, line)),
            pltpu.SemaphoreType.DMA,
            pltpu.SemaphoreType.DMA((3,)),
            pltpu.SemaphoreType.DMA((3,)),
            pltpu.SemaphoreType.DMA,
        ],
        compiler_params=pltpu.CompilerParams(collective_id=number, has_side_effects=True),
        name=f"last{number}",
    )(small, grad)


def per_device(
    hidden, norm_gain, expert_ids, gate_probs, out_grad, gate_weight, up_weight, down_weight
):
    quarters = lax.axis_size("tensor")
    quarter = lax.axis_index("tensor")
    own_count = hidden.shape[0] // quarters
    width = hidden.shape[1]
    top_count = expert_ids.shape[1]
    devices = lax.axis_size(AXES)
    experts = gate_weight.shape[0] * devices
    capacity = 2 * own_count * top_count // experts
    tokens = own_count * devices
    blocks_in = min(4, devices)
    groups = devices // blocks_in
    gtok = own_count * blocks_in
    gslots = capacity * blocks_in
    slots = groups * gslots
    me = lax.axis_index(AXES)

    own_rows = lax.dynamic_slice_in_dim(hidden, quarter * own_count, own_count, 0)
    values = own_rows.astype(f32)
    inverse = lax.rsqrt(jnp.mean(values * values, axis=-1, keepdims=True) + epsilon)
    unit_rows = values * inverse
    normed = (unit_rows * norm_gain).astype(bf16)
    grad_rows = out_grad.astype(f32)

    meta = jnp.concatenate(
        [
            expert_ids.astype(f32),
            gate_probs,
            jnp.zeros((own_count, 128 - 2 * top_count), f32),
        ],
        axis=1,
    )
    meta_all, normed_all, grads_all = gather_all(
        [meta, normed, out_grad], (0, 0, lax.axis_size("dp") // 2 - 1), 0
    )
    meta_all = meta_all.reshape(tokens, 128)
    ids_all = meta_all[:, :top_count].astype(jnp.int32)
    probs_all = meta_all[:, top_count:2 * top_count]

    hits = ids_all == me
    member = jnp.any(hits, axis=1).reshape(devices, own_count)
    prob = jnp.sum(jnp.where(hits, probs_all, 0.0), axis=1)
    earlier = jnp.arange(own_count)[:, None] < jnp.arange(own_count)[None, :]
    place = jnp.dot(member.astype(bf16), earlier.astype(bf16), preferred_element_type=f32)
    place = place.astype(jnp.int32)
    block = jnp.arange(devices, dtype=jnp.int32)[:, None] % blocks_in
    slot = jnp.where(member, block * capacity + place, -1).reshape(groups, gtok)
    picks = slot[:, None, :] == jnp.arange(gslots, dtype=jnp.int32)[None, :, None]
    choose = picks.astype(bf16)
    slot_prob = jnp.sum(
        jnp.where(picks, prob.reshape(groups, 1, gtok), 0.0), axis=2
    ).reshape(slots, 1)

    def pack(rows):
        return jnp.einsum(
            "gst,gtd->gsd", choose, rows.reshape(groups, gtok, width), preferred_element_type=f32
        ).astype(bf16).reshape(slots, width)

    def spread(rows):
        return jnp.einsum(
            "gst,gsd->gtd", choose, rows.reshape(groups, gslots, width), preferred_element_type=f32
        ).astype(bf16).reshape(devices, own_count, width)

    w_gate, w_up, w_down = gate_weight[0], up_weight[0], down_weight[0]
    inputs = pack(normed_all)
    gate_pre = dot(inputs, w_gate, 1, 0)
    up_pre = dot(inputs, w_up, 1, 0)
    sigma = jax.nn.sigmoid(gate_pre)
    silu_vals = gate_pre * sigma
    act = (silu_vals * up_pre).astype(bf16)
    results = dot(act, w_down, 1, 0).astype(bf16)
    results_f = results.astype(f32)
    grads = pack(grads_all).astype(f32)
    cotan = (slot_prob * grads).astype(bf16)
    slot_gg = jnp.sum(grads * results_f, axis=1)
    layer_part, (gate_pgrad, up_pgrad, back) = scatter_sum(
        spread((slot_prob * results_f).astype(bf16)), 1, backward_tile, backward_plain,
        (cotan, gate_pre, up_pre, w_down, w_gate, w_up),
    )
    normed_total, (gate_wgrad, up_wgrad, down_grad) = scatter_sum(
        spread(back), 2, weights_tile, weights_plain,
        (inputs, gate_pgrad, up_pgrad, act, cotan),
    )
    gate_wgrad, up_wgrad, down_grad = gate_wgrad[None], up_wgrad[None], down_grad[None]
    token_gg = jnp.sum(jnp.where(picks, slot_gg.reshape(groups, gslots, 1), 0.0), axis=1)

    layer_out = (values + layer_part).astype(bf16)
    gain_part = jnp.sum(normed_total * unit_rows, axis=0)
    upstream = normed_total * norm_gain
    own_grad = grad_rows + inverse * (
        upstream - unit_rows * jnp.mean(upstream * unit_rows, axis=-1, keepdims=True)
    )
    small = jnp.concatenate([token_gg.reshape(-1, 128), gain_part.reshape(-1, 128)], axis=0)
    small_all, input_grad = gather_last(small, own_grad.astype(bf16), 3)
    input_grad = input_grad.reshape(hidden.shape)
    tiles = tokens // 128
    gain_grad = jnp.sum(small_all[:, tiles:, :], axis=0).reshape(width)
    mine = lax.dynamic_slice_in_dim(
        small_all[:, :tiles, :].reshape(devices, tokens), me * own_count, own_count, 1
    )
    named = expert_ids[:, :, None] == jnp.arange(devices, dtype=jnp.int32)[None, None, :]
    gate_grad = jnp.sum(jnp.where(named, mine.T[:, None, :], 0.0), axis=2)
    return (layer_out, input_grad, gate_grad, gain_grad, gate_wgrad, up_wgrad, down_grad)


CORNER_UP, CORNER_DOWN = 10, 11


def along_z(line, z, zz):
    apart = jnp.abs(jnp.int32(z) - zz)
    return (apart == 1) | ((apart == 2) & ((z == 0) | (z == line - 1)))


class Stream(Gather):
    def landing(self, kind):
        return (0, 0, 1, 2, 3, 4, 5, 6, 7, 8, 3, 3)[kind]

    def order(self, step):
        return self.p.order(step, False)

    def corner_up(self, zz):
        p = self.p
        return self.copy(CORNER_UP, zz, 3, None, p.device(p.z + 1, 0, p.c))

    def corner_down(self, zz):
        p = self.p
        return self.copy(CORNER_DOWN, zz, 3, None, p.device(p.z - 1, 0, p.c))

    def routes(self, zz):
        z, line = self.p.z, self.p.line
        up = (z < line - 1) & (zz <= z) & along_z(line, z + 1, zz)
        down = (z > 0) & (zz >= z) & along_z(line, z - 1, zz)
        return along_z(line, z, zz), up, down

    def plane(self, step):
        zz = self.order(step)
        flat = jnp.logical_not(self.routes(zz)[0])
        self.arrived(SIDE, zz, 1, None)
        pl.when(flat)(lambda: self.half0(zz).start())
        self.core(zz, 1).start()
        self.arrived(FACE, zz, 2, None)
        pl.when(flat)(lambda: self.half1(zz).start())
        self.core(zz, 2).start()

    def corner(self, step):
        zz, z = self.order(step), self.p.z
        via, up, down = self.routes(zz)

        @pl.when(jnp.logical_not(via))
        def _():
            self.arrived(HALF0, zz, 3, 0)
            self.arrived(HALF1, zz, 3, 1)

        pl.when(via & (zz < z))(lambda: self.arrived(CORNER_UP, zz, 3, None))
        pl.when(via & (zz > z))(lambda: self.arrived(CORNER_DOWN, zz, 3, None))
        pl.when(up)(lambda: self.corner_up(zz).start())
        pl.when(down)(lambda: self.corner_down(zz).start())
        self.core(zz, 3).start()

    def done(self, step):
        p, zz = self.p, self.order(step)
        if step == 0:
            pltpu.make_async_copy(
                self.own, self.held.at[p.index(p.z, 0, p.c)], self.keep
            ).wait()
        for flip in range(4):
            self.arrived(CORE + flip, zz, flip, None, 1 - p.c)

    def sent(self):
        p = self.p
        for zz in range(p.line):
            pl.when((zz <= p.z) & (p.z < p.line - 1))(lambda zz=zz: self.up(zz).wait_send())
            pl.when((zz >= p.z) & (p.z > 0))(lambda zz=zz: self.down(zz).wait_send())
            self.side(zz).wait_send()
            self.face(zz).wait_send()
            via, up, down = self.routes(jnp.int32(zz))

            @pl.when(jnp.logical_not(via))
            def _(zz=zz):
                self.half0(zz).wait_send()
                self.half1(zz).wait_send()

            pl.when(up)(lambda zz=zz: self.corner_up(zz).wait_send())
            pl.when(down)(lambda zz=zz: self.corner_down(zz).wait_send())
            for flip in range(4):
                self.core(zz, flip).wait_send()


def put(ref, index):
    def store(rows, value):
        ref[index + (rows,)] = value.astype(ref.dtype)
    return store


def get(ref, index):
    return lambda rows: ref[index + (rows,)]


class Scatter:
    def __init__(
        self, place, part, out, theirs, half_in, side_in, face_in, up_in, down_in, corner_up_in,
        corner_down_in, send, recv,
    ):
        self.p, self.part, self.out, self.theirs = place, part, out, theirs
        self.half_in, self.side_in, self.face_in = half_in, side_in, face_in
        self.up_in, self.down_in = up_in, down_in
        self.corner_up_in, self.corner_down_in = corner_up_in, corner_down_in
        self.sends, self.recvs = send, recv
        self.count = out.shape[0]
        self.half = self.count // 2

    def order(self, step):
        return self.p.order(step, True)

    def remote(self, src, dst, kind, zz, device):
        return pltpu.make_async_remote_copy(
            src_ref=src, dst_ref=dst, send_sem=self.sends.at[kind, zz],
            recv_sem=self.recvs.at[kind, zz], device_id=device, device_id_type=MESH,
        )

    def core(self, zz, flip):
        p = self.p
        return self.remote(
            self.part.at[p.index(zz, flip, 1 - p.c)], self.theirs.at[zz, flip], CORE + flip, zz,
            p.device(p.z, 0, 1 - p.c),
        )

    def half0(self, zz):
        p = self.p
        return self.remote(
            self.theirs.at[zz, 3, pl.ds(0, self.half)], self.half_in.at[self.flat(zz), 0], HALF0, zz,
            p.device(p.z, 2, p.c),
        )

    def half1(self, zz):
        p = self.p
        return self.remote(
            self.theirs.at[zz, 3, pl.ds(self.half, self.half)], self.half_in.at[self.flat(zz), 1], HALF1, zz,
            p.device(p.z, 1, p.c),
        )

    def side(self, zz):
        p = self.p
        return self.remote(
            self.theirs.at[zz, 1], self.side_in.at[zz], SIDE, zz, p.device(p.z, 1, p.c)
        )

    def face(self, zz):
        p = self.p
        return self.remote(
            self.theirs.at[zz, 2], self.face_in.at[zz], FACE, zz, p.device(p.z, 2, p.c)
        )

    def up(self, zz):
        p = self.p
        return self.remote(
            self.theirs.at[zz, 0], self.up_in.at[zz], UP, zz, p.device(p.z + 1, 0, p.c)
        )

    def down(self, zz):
        p = self.p
        return self.remote(
            self.theirs.at[zz, 0], self.down_in.at[zz], DOWN, zz, p.device(p.z - 1, 0, p.c)
        )

    def flat(self, zz):
        return jnp.where(zz == self.p.z, 0, 1)

    def corner_up(self, zz, slot):
        p = self.p
        return self.remote(
            self.theirs.at[zz, 3], self.corner_up_in.at[slot], CORNER_UP, zz,
            p.device(p.z + 1, 0, p.c),
        )

    def corner_down(self, zz, slot):
        p = self.p
        return self.remote(
            self.theirs.at[zz, 3], self.corner_down_in.at[slot], CORNER_DOWN, zz,
            p.device(p.z - 1, 0, p.c),
        )

    def give(self, step):
        zz = self.order(step)
        for flip in (3, 1, 2, 0):
            self.core(zz, flip).start()

    def joined(self, zz, flip):
        self.core(zz, flip).wait_recv()
        here = (zz, flip)
        add_rows(
            0, self.count, put(self.theirs, here), get(self.theirs, here),
            get(self.part, (self.p.index(zz, flip, self.p.c),)),
        )

    def corner(self, step):
        p, zz, here = self.p, self.order(step), (self.order(step), 3)
        z, line = p.z, p.line
        via = along_z(line, z, zz)
        below = (z > 0) & (zz >= z) & along_z(line, z - 1, zz)
        above = (z < line - 1) & (zz <= z) & along_z(line, z + 1, zz)

        def onward():
            pl.when(via & (zz > z))(lambda: self.corner_up(zz, zz - z - 1).start())
            pl.when(via & (zz < z))(lambda: self.corner_down(zz, z - 1 - zz).start())

            @pl.when(jnp.logical_not(via))
            def _():
                self.half0(zz).start()
                self.half1(zz).start()

        self.joined(zz, 3)
        pl.when(jnp.logical_not(below | above))(onward)
        for flip in (1, 2, 0):
            self.joined(zz, flip)

        @pl.when(below)
        def _():
            slot = zz - z
            self.corner_up(zz, slot).wait_recv()
            add_rows(
                0, self.count, put(self.theirs, here), get(self.theirs, here),
                get(self.corner_up_in, (slot,)),
            )

        @pl.when(above)
        def _():
            slot = z - zz
            self.corner_down(zz, slot).wait_recv()
            add_rows(
                0, self.count, put(self.theirs, here), get(self.theirs, here),
                get(self.corner_down_in, (slot,)),
            )

        pl.when(below | above)(onward)

    def plane(self, step):
        zz, half, theirs = self.order(step), self.half, self.theirs
        flat, slot = jnp.logical_not(along_z(self.p.line, self.p.z, zz)), self.flat(zz)
        here = (zz, 1)

        @pl.when(flat)
        def _():
            self.half0(zz).wait_recv()
            add_rows(0, half, put(theirs, here), get(theirs, here), get(self.half_in, (slot, 0)))

        self.side(zz).start()

        @pl.when(flat)
        def _():
            self.half1(zz).wait_recv()

            @pl.loop(0, half // 16)
            def _(i):
                low = pl.ds(pl.multiple_of(i * 16, 16), 16)
                high = pl.ds(pl.multiple_of(half + i * 16, 16), 16)
                total = theirs[zz, 2, high].astype(f32) + self.half_in[slot, 1, low].astype(f32)
                theirs[zz, 2, high] = total.astype(bf16)

        self.face(zz).start()

    def column(self, step):
        p, zz, count, out = self.p, self.order(step), self.count, self.out
        z, line = p.z, p.line
        self.side(zz).wait_recv()
        self.face(zz).wait_recv()
        base = (
            get(self.theirs, (zz, 0)), get(self.side_in, (zz,)), get(self.face_in, (zz,))
        )
        if step == line - 1:
            add_rows(0, count, put(out, ()), *base)

            @pl.when(z > 0)
            def _():
                self.up(zz).wait_recv()
                add_rows(0, count, put(out, ()), get(out, ()), get(self.up_in, (zz,)))

            @pl.when(z < line - 1)
            def _():
                self.down(zz).wait_recv()
                add_rows(0, count, put(out, ()), get(out, ()), get(self.down_in, (zz,)))

            return

        def onward(copy, source, more):
            @pl.when(more)
            def _():
                copy(zz).wait_recv()
                add_rows(0, count, put(self.theirs, (zz, 0)), *base, get(source, (zz,)))

            @pl.when(jnp.logical_not(more))
            def _():
                add_rows(0, count, put(self.theirs, (zz, 0)), *base)

            copy(zz).start()

        pl.when(zz > z)(lambda: onward(self.up, self.up_in, z > 0))
        pl.when(zz < z)(lambda: onward(self.down, self.down_in, z < line - 1))

    def given(self, step):
        zz = self.order(step)
        for flip in range(4):
            self.core(zz, flip).wait_send()

    def sent(self):
        z = self.p.z
        for zz in range(self.p.line):
            self.side(zz).wait_send()
            self.face(zz).wait_send()
            via = along_z(self.p.line, z, jnp.int32(zz))

            @pl.when(jnp.logical_not(via))
            def _(zz=zz):
                self.half0(zz).wait_send()
                self.half1(zz).wait_send()

            pl.when(via & (zz > z))(lambda zz=zz: self.corner_up(zz, 0).wait_send())
            pl.when(via & (zz < z))(lambda zz=zz: self.corner_down(zz, 0).wait_send())
            pl.when(zz > z)(lambda zz=zz: self.up(zz).wait_send())
            pl.when(zz < z)(lambda zz=zz: self.down(zz).wait_send())


class Both:
    def __init__(self, first, second, whole):
        self.parts, self.whole = (first, second), whole
        self.order = first.order

    def each(self, name, *args):
        for part in self.parts:
            getattr(part, name)(*args)

    def slot(self, step):
        line = self.parts[0].p.line
        if step == 0:
            self.each("first")
        elif 0 < step < line:
            self.each("column", step)
        if 0 <= step - 1 < line:
            self.each("plane", step - 1)
        if 0 <= step - 2 < line:
            self.each("corner", step - 2)

    def done(self, step):
        self.each("done", step)

    def sent(self):
        self.whole.sent()

    def give(self, step):
        self.each("give", step)

    def given(self, step):
        self.whole.given(step)

    def corner(self, step):
        self.each("corner", step)

    def plane(self, step):
        self.each("plane", step)

    def column(self, step):
        self.each("column", step)


def layer_kernel(
    line, tops, capacity,
    ids, probs, hidden, gain, out_grad, w_gate_in, w_up_in, w_down_in,
    layer_out, rows_out, gg_out, gain_out, w_gate, w_up, w_down, grads_all,
    turn, meta, meta_all, normed_all, hid, normed, inputs, cotan, stage, choose,
    gate_pre, up_pre, act, gate_pgrad, up_pgrad, ggs, gacc, small, small_all, total, own_grad,
    theirs1, half1, side1, face1, up1, down1, cup1, cdown1,
    theirs2, half2, side2, face2, up2, down2, cup2, cdown2,
    gsend, grecv, gkeep, ssend, srecv, load, stage_sem, tsend, trecv, tkeep,
):
    p = Place(line)
    own, width = hid.shape
    inner = act.shape[1]
    me = p.index(p.z, 0, p.c)
    gtok, gslots = choose.shape[1:]
    pslots = 2 * gslots
    barrier = pltpu.get_barrier_semaphore()

    def tell(device):
        pl.semaphore_signal(barrier, inc=1, device_id=device, device_id_type=MESH)

    for flip, c in ((1, p.c), (2, p.c), (0, 1 - p.c)):
        tell(p.device(p.z, flip, c))
    below, above = p.z > 0, p.z < line - 1
    pl.when(below)(lambda: tell(p.device(p.z - 1, 0, p.c)))
    pl.when(above)(lambda: tell(p.device(p.z + 1, 0, p.c)))

    quarter = p.y * 2 + p.c
    mine = pltpu.make_async_copy(
        hidden.at[pl.ds(pl.multiple_of(quarter * own, own), own)], hid, load.at[0]
    )
    mine.start()
    loads = [
        pltpu.make_async_copy(a, b, load.at[1 + i])
        for i, (a, b) in enumerate(((w_gate_in, w_gate), (w_up_in, w_up), (w_down_in, w_down)))
    ]
    turn[...] = jnp.zeros_like(turn)
    turn[0:tops, 0:own] = ids[...].astype(f32)
    turn[tops:2 * tops, 0:own] = probs[...]
    meta[...] = turn[...].T[0:own]
    mine.wait()

    def unit_of(rows):
        values = hid[rows].astype(f32)
        inverse = lax.rsqrt(jnp.mean(values * values, axis=-1, keepdims=True) + epsilon)
        return values, inverse

    @pl.loop(0, own // 16)
    def _(i):
        rows = pl.ds(pl.multiple_of(i * 16, 16), 16)
        values, inverse = unit_of(rows)
        normed[rows] = (values * inverse * gain[...]).astype(bf16)

    pl.semaphore_wait(barrier, 3 + below.astype(jnp.int32) + above.astype(jnp.int32))

    def stream(i, j, source, held):
        return Stream(p, source, held, gsend.at[i], grecv.at[j], gkeep.at[j])

    upper = own // 2

    def streams(i, j, source, held):
        halves = [
            stream(i, j + k, source.at[pl.ds(k * upper, upper)], held.at[:, pl.ds(k * upper, upper)])
            for k in range(2)
        ]
        return Both(*halves, stream(i, j, source, held))

    g_meta, g_small = stream(0, 0, meta, meta_all), stream(1, 1, small, small_all)
    g_norm, g_grad = streams(2, 2, normed, normed_all), streams(3, 4, out_grad, grads_all)
    def scatter(i, theirs, half_in, side_in, face_in, up_in, down_in, cup_in, cdown_in):
        def one(k):
            rows, quarter_rows = pl.ds(k * upper, upper), pl.ds(k * upper // 2, upper // 2)
            return Scatter(
                p, normed_all.at[:, rows], total.at[rows], theirs.at[:, :, rows],
                half_in.at[:, :, quarter_rows], side_in.at[:, rows], face_in.at[:, rows],
                up_in.at[:, rows], down_in.at[:, rows], cup_in.at[:, rows], cdown_in.at[:, rows],
                ssend.at[i], srecv.at[2 * i + k],
            )
        whole = Scatter(
            p, normed_all, total, theirs, half_in, side_in, face_in, up_in, down_in, cup_in,
            cdown_in, ssend.at[i], srecv.at[2 * i],
        )
        return Both(one(0), one(1), whole)

    s_out = scatter(0, theirs1, half1, side1, face1, up1, down1, cup1, cdown1)
    s_back = scatter(1, theirs2, half2, side2, face2, up2, down2, cup2, cdown2)
    me_f = me.astype(f32)
    wide = 512

    def columns(body, size=wide, full=width):
        @pl.loop(0, full // size)
        def _(i):
            body(pl.ds(pl.multiple_of(i * size, size), size))

    def hits_of(zz, h):
        got = meta_all[pl.ds(8 * zz + 4 * h, 4)].reshape(gtok, 128)
        lane = lax.broadcasted_iota(jnp.int32, (gtok, 128), 1)
        return got, lane, jnp.where((got == me_f) & (lane < tops), 1.0, 0.0)

    def prob_of(zz, h):
        got, _, hit = hits_of(zz, h)
        return jnp.sum(pltpu.roll(hit, tops, 1) * got, axis=1, keepdims=True)

    def route(zz):
        for h in range(2):
            _, lane, hit = hits_of(zz, h)
            member = jnp.sum(hit, axis=1, keepdims=True)
            a = lax.broadcasted_iota(jnp.int32, (gtok, gtok), 0)
            b = lax.broadcasted_iota(jnp.int32, (gtok, gtok), 1)
            earlier = jnp.where((a > b) & (a // own == b // own), 1.0, 0.0).astype(bf16)
            spot = dot(earlier, jnp.broadcast_to(member, (gtok, 128)).astype(bf16), 1, 0)
            block = lax.broadcasted_iota(jnp.int32, (gtok, 128), 0) // own
            spot = spot + (block * capacity).astype(f32)
            picked = (spot == lane.astype(f32)) & (member > 0.0)
            choose[2 * zz + h] = jnp.where(picked, 1.0, 0.0).astype(bf16)

    def slots(zz, h=None):
        if h is None:
            return pl.ds(pl.multiple_of(zz * pslots, pslots), pslots)
        return pl.ds(pl.multiple_of(zz * pslots + h * gslots, gslots), gslots)

    def forward(zz):
        route(zz)
        for h in range(2):
            pick = choose[2 * zz + h]

            def pack(cols, pick=pick, h=h):
                rows = normed_all[pl.ds(8 * zz + 4 * h, 4), :, cols].reshape(gtok, wide)
                inputs[slots(zz, h), cols] = dot(pick, rows, 0, 0).astype(bf16)

            columns(pack)
        rows = slots(zz)

        def products(cols):
            gate = dot(inputs[rows], w_gate[:, cols], 1, 0)
            up = dot(inputs[rows], w_up[:, cols], 1, 0)
            gate_pre[rows, cols] = gate
            up_pre[rows, cols] = up
            act[rows, cols] = (gate * jax.nn.sigmoid(gate) * up).astype(bf16)

        columns(products, 256, inner)

    def result(zz):
        rows = slots(zz)
        probs = [prob_of(zz, h) for h in range(2)]

        def expand(cols):
            done = dot(act[rows], w_down[:, cols], 1, 0).astype(bf16)
            for h in range(2):
                got = dot(choose[2 * zz + h], done[h * gslots:(h + 1) * gslots], 1, 0)
                normed_all[pl.ds(8 * zz + 4 * h, 4), :, cols] = (
                    (got * probs[h]).astype(bf16).reshape(4, own, wide)
                )

        columns(expand)

    def fetch(step):
        zz = s_back.order(step)
        return pltpu.make_async_copy(grads_all.at[pl.ds(8 * zz, 8)], stage, stage_sem)

    def cotangent(step):
        zz = s_back.order(step)
        fetch(step).wait()
        for h in range(2):
            pick, prob = choose[2 * zz + h], prob_of(zz, h)
            which = lax.broadcasted_iota(jnp.int32, (gtok, 128), 1)
            high = prob.astype(bf16).astype(f32)
            middle = (prob - high).astype(bf16).astype(f32)
            low = prob - high - middle
            parts = jnp.where(
                which == 0, high, jnp.where(which == 1, middle, jnp.where(which == 2, low, 0.0))
            )
            factor = jnp.sum(dot(pick, parts.astype(bf16), 0, 0), axis=1, keepdims=True)

            def pack(cols, pick=pick, factor=factor, h=h):
                rows = stage[4 * h:4 * h + 4, :, cols].reshape(gtok, wide)
                cotan[slots(zz, h), cols] = (dot(pick, rows, 0, 0) * factor).astype(bf16)

            columns(pack)
        if step < line - 1:
            fetch(step + 1).start()

    def hidden_grads(zz):
        rows = slots(zz)
        ggs[...] = jnp.zeros_like(ggs)

        def chunk(cols):
            act_grad = dot(cotan[rows], w_down[cols], 1, 1)
            one, two = row_grads(act_grad, gate_pre[rows, cols], up_pre[rows, cols])
            gate_pgrad[rows, cols] = one
            up_pgrad[rows, cols] = two
            both = act_grad * act[rows, cols].astype(f32)
            ggs[...] += both[:, :128] + both[:, 128:]

        columns(chunk, 256, inner)
        for h in range(2):
            line_sum = jnp.sum(ggs[h * gslots:(h + 1) * gslots].T, axis=0, keepdims=True)
            high = line_sum.astype(bf16).astype(f32)
            which = lax.broadcasted_iota(jnp.int32, (16, gslots), 0)
            parts = jnp.where(which == 0, high, jnp.where(which == 1, line_sum - high, 0.0))
            spread = dot(parts.astype(bf16), choose[2 * zz + h], 1, 1)
            row = jnp.sum(spread, axis=0, keepdims=True)
            for k in range(gtok // 128):
                small[pl.ds(4 * zz + 2 * h + k, 1)] = row[:, 128 * k:128 * k + 128]

    def backs(zz):
        rows = slots(zz)

        def chunk(cols):
            back = dot(gate_pgrad[rows], w_gate[cols], 1, 1)
            back = (back + dot(up_pgrad[rows], w_up[cols], 1, 1)).astype(bf16)
            terms = back.astype(f32) * inputs[rows, cols].astype(f32)
            gacc[:, cols] += jnp.sum(terms.reshape(pslots // 8, 8, wide), axis=0)
            for h in range(2):
                got = dot(choose[2 * zz + h], back[h * gslots:(h + 1) * gslots], 1, 0)
                normed_all[pl.ds(8 * zz + 4 * h, 4), :, cols] = (
                    got.astype(bf16).reshape(4, own, wide)
                )

        columns(chunk)

    def weight_grads(step):
        deep = 256
        share = width // deep // 4

        @pl.loop(step * share, (step + 1) * share)
        def _(i):
            cols = pl.ds(pl.multiple_of(i * deep, deep), deep)
            block = inputs[:, cols]
            w_gate[cols] = dot(block, gate_pgrad[...], 0, 0).astype(bf16)
            w_up[cols] = dot(block, up_pgrad[...], 0, 0).astype(bf16)

        if step * deep < inner:
            rows = pl.ds(step * deep, deep)

            def chunk(cols):
                w_down[rows, cols] = dot(act[:, rows], cotan[:, cols], 0, 0).astype(bf16)

            columns(chunk)

    g_meta.slot(0)
    g_norm.slot(0)
    for copy in loads:
        copy.start()
    gacc[...] = jnp.zeros_like(gacc)

    def arrived(step):
        g_meta.done(step)
        g_norm.done(step)

    def relay_norm(step):
        g_meta.slot(step)
        g_norm.slot(step)

    def loaded():
        for copy in loads:
            copy.wait()

    def expand_results(step):
        result(s_out.order(step))
        s_out.give(step)

    def grads_here():
        for step in range(line):
            g_grad.done(step)
        fetch(0).start()

    def input_grads(step):
        s_out.given(step)
        backs(s_back.order(step))
        s_back.give(step)

    def add_hidden():
        @pl.loop(0, own // 16)
        def _(i):
            rows = pl.ds(pl.multiple_of(i * 16, 16), 16)
            layer_out[rows] = (hid[rows].astype(f32) + total[rows]).astype(bf16)

    first = small.shape[0] - width // 128

    def small_start():
        gsum = jnp.sum(gacc[...], axis=0, keepdims=True)
        for k in range(width // 128):
            small[first + k:first + k + 1] = gsum[:, 128 * k:128 * k + 128]
        g_small.slot(0)

    relay_norm(1)
    relay_norm(2)
    relay_norm(3)
    g_grad.slot(0)
    arrived(0)
    loaded()
    forward(g_norm.order(0))
    relay_norm(4)
    g_grad.slot(1)
    arrived(1)
    forward(g_norm.order(1))
    relay_norm(5)
    g_grad.slot(2)
    arrived(2)
    forward(g_norm.order(2))
    g_grad.slot(3)
    arrived(3)
    forward(g_norm.order(3))
    g_norm.sent()
    expand_results(0)
    g_grad.slot(4)
    expand_results(1)
    s_out.corner(0)
    g_grad.slot(5)
    expand_results(2)
    s_out.corner(1)
    s_out.plane(0)
    expand_results(3)
    s_out.corner(2)
    s_out.plane(1)
    s_out.column(0)
    grads_here()
    s_out.corner(3)
    s_out.plane(2)
    s_out.column(1)
    cotangent(0)
    hidden_grads(s_back.order(0))
    input_grads(0)
    s_out.plane(3)
    s_out.column(2)
    cotangent(1)
    hidden_grads(s_back.order(1))
    input_grads(1)
    s_back.corner(0)
    cotangent(2)
    hidden_grads(s_back.order(2))
    input_grads(2)
    s_out.column(3)
    add_hidden()
    s_back.corner(1)
    s_back.plane(0)
    cotangent(3)
    hidden_grads(s_back.order(3))
    input_grads(3)
    small_start()
    s_back.corner(2)
    s_back.plane(1)
    s_back.column(0)
    weight_grads(0)
    g_small.slot(1)
    s_back.corner(3)
    s_back.plane(2)
    s_back.column(1)
    weight_grads(1)
    g_small.slot(2)
    s_back.plane(3)
    s_back.column(2)
    weight_grads(2)
    g_small.slot(3)
    weight_grads(3)

    g_small.slot(4)
    other = (1 - p.y) * 2 + p.c
    partner = p.device(p.z, 0, 1 - p.c)
    keeping = pltpu.make_async_copy(own_grad, rows_out.at[quarter], tkeep)

    def tremote(k, i, src, where, device):
        rows = pl.ds(k * upper, upper)
        return pltpu.make_async_remote_copy(
            src_ref=src.at[rows], dst_ref=rows_out.at[where, rows], send_sem=tsend.at[k, i],
            recv_sem=trecv.at[k, i], device_id=device, device_id_type=MESH,
        )

    across = [tremote(k, 0, own_grad, quarter, p.device(p.z, 2, p.c)) for k in range(2)]
    beside = [tremote(k, 1, own_grad, quarter, partner) for k in range(2)]
    relay = [tremote(k, 2, rows_out.at[other], other, partner) for k in range(2)]
    for k in range(2):
        s_back.parts[k].column(line - 1)

        @pl.loop(k * upper // 16, (k + 1) * upper // 16)
        def _(i):
            rows = pl.ds(pl.multiple_of(i * 16, 16), 16)
            values, inverse = unit_of(rows)
            unit = values * inverse
            upstream = total[rows] * gain[...]
            mean = jnp.mean(upstream * unit, axis=-1, keepdims=True)
            grad = out_grad[rows].astype(f32) + inverse * (upstream - unit * mean)
            own_grad[rows] = grad.astype(bf16)

        across[k].start()
        beside[k].start()
    keeping.start()
    g_small.slot(5)
    for step in range(line):
        g_small.done(step)
    gain_out[...] = jnp.sum(small_all[:, first:], axis=0)
    gg_out[...] = small_all[:, pl.ds(me // 2, 1)].reshape(gg_out.shape)
    for k in range(2):
        across[k].wait_recv()
        relay[k].start()
    g_meta.sent()
    g_grad.sent()
    g_small.sent()
    s_out.sent()
    for step in range(line):
        s_back.given(step)
    s_back.sent()
    for k in range(2):
        beside[k].wait_recv()
        relay[k].wait_recv()
        for copy in (across[k], beside[k], relay[k]):
            copy.wait_send()
    keeping.wait()


def whole_layer(ids, probs, hidden, gain, out_grad, w_gate, w_up, w_down, capacity):
    line = lax.axis_size("dp") // 2
    devices, quarters = lax.axis_size(AXES), lax.axis_size("tensor")
    own, width = out_grad.shape
    inner = w_gate.shape[1]
    groups, gtok, gslots = devices // 4, own * 4, capacity * 4
    slots = groups * gslots
    small_rows = devices * own // 128 + width // 128
    anywhere, vmem = pl.BlockSpec(memory_space=pl.ANY), pl.BlockSpec(memory_space=pltpu.VMEM)
    shape = jax.ShapeDtypeStruct
    dma = pltpu.SemaphoreType.DMA
    passing = [
        pltpu.VMEM((line, 4, own, width), bf16),
        pltpu.VMEM((2, 2, own // 2, width), bf16),
        pltpu.VMEM((line, own, width), bf16),
        pltpu.VMEM((line, own, width), bf16),
        pltpu.VMEM((line, own, width), bf16),
        pltpu.VMEM((line, own, width), bf16),
        pltpu.VMEM((2, own, width), bf16),
        pltpu.VMEM((2, own, width), bf16),
    ]
    return pl.pallas_call(
        functools.partial(layer_kernel, line, ids.shape[0], capacity),
        out_shape=[
            pltpu.VMEM((own, width), bf16),
            pltpu.VMEM((quarters, own, width), bf16),
            pltpu.VMEM((devices, 128), f32),
            pltpu.VMEM((width // 128, 128), f32),
            pltpu.VMEM(w_gate.shape, bf16),
            pltpu.VMEM(w_up.shape, bf16),
            pltpu.VMEM(w_down.shape, bf16),
            shape((devices, own, width), bf16),
        ],
        in_specs=[vmem, vmem, anywhere, vmem, vmem, anywhere, anywhere, anywhere],
        out_specs=[vmem] * 7 + [anywhere],
        scratch_shapes=[
            pltpu.VMEM((128, 128), f32),
            pltpu.VMEM((own, 128), f32),
            pltpu.VMEM((devices, own, 128), f32),
            pltpu.VMEM((devices, own, width), bf16),
            pltpu.VMEM((own, width), bf16),
            pltpu.VMEM((own, width), bf16),
            pltpu.VMEM((slots, width), bf16),
            pltpu.VMEM((slots, width), bf16),
            pltpu.VMEM((8, own, width), bf16),
            pltpu.VMEM((groups, gtok, gslots), bf16),
            pltpu.VMEM((slots, inner), f32),
            pltpu.VMEM((slots, inner), f32),
            pltpu.VMEM((slots, inner), bf16),
            pltpu.VMEM((slots, inner), bf16),
            pltpu.VMEM((slots, inner), bf16),
            pltpu.VMEM((2 * gslots, 128), f32),
            pltpu.VMEM((8, width), f32),
            pltpu.VMEM((small_rows, 128), f32),
            pltpu.VMEM((devices, small_rows, 128), f32),
            pltpu.VMEM((own, width), f32),
            pltpu.VMEM((own, width), bf16),
        ] + passing + passing + [
            dma((4, 12, line)),
            dma((6, 9, line)),
            dma((6,)),
            dma((2, 12, line)),
            dma((4, 12, line)),
            dma((4,)),
            dma,
            dma((2, 3)),
            dma((2, 3)),
            dma,
        ],
        compiler_params=pltpu.CompilerParams(
            collective_id=0, has_side_effects=True, vmem_limit_bytes=53 * 2**20
        ),
        name="layer",
    )(ids, probs, hidden, gain, out_grad, w_gate, w_up, w_down)


def finish_kernel(
    layer, rows, gg, gain_sum, gate_wgrad, up_wgrad, down_wgrad, ids, probs, gain,
    layer_out, rows_out, gate_grad, gain_grad, gate_out, up_out, down_out, sems,
):
    pairs = [
        (layer, layer_out), (rows, rows_out), (gate_wgrad, gate_out), (up_wgrad, up_out),
        (down_wgrad, down_out),
    ]
    copies = []
    for a, b in pairs:
        count = a.shape[0] // 4
        for i in range(4):
            part = pl.ds(i * count, count)
            copies.append(pltpu.make_async_copy(a.at[part], b.at[part], sems.at[len(copies)]))
    for copy in copies:
        copy.start()
    own = ids.shape[1]
    tensor, dp = lax.axis_index("tensor"), lax.axis_index("dp")
    odd = (dp * 4 + tensor) % 2 == 1
    found = jnp.where(odd, gg[:, own:2 * own], gg[:, 0:own])
    device = lax.broadcasted_iota(jnp.int32, found.shape, 0)
    for k in range(ids.shape[0]):
        hit = device == ids[k:k + 1]
        value = jnp.sum(jnp.where(hit, found, 0.0), axis=0, keepdims=True)
        gate_grad[k:k + 1] = value / probs[k:k + 1]
    gain_grad[...] = gain_sum[...] / gain[...]
    for copy in copies:
        copy.wait()


def finish(*arrays):
    layer, rows, gg, gain_sum, gate_wgrad, up_wgrad, down_wgrad, ids, probs, gain = arrays
    anywhere, vmem = pl.BlockSpec(memory_space=pl.ANY), pl.BlockSpec(memory_space=pltpu.VMEM)
    return pl.pallas_call(
        finish_kernel,
        out_shape=[
            jax.ShapeDtypeStruct(a.shape, a.dtype)
            for a in (layer, rows, probs, gain, gate_wgrad, up_wgrad, down_wgrad)
        ],
        in_specs=[anywhere, anywhere, vmem, vmem, anywhere, anywhere, anywhere, vmem, vmem, vmem],
        out_specs=[anywhere, anywhere, vmem, vmem, anywhere, anywhere, anywhere],
        scratch_shapes=[pltpu.SemaphoreType.DMA((20,))],
        compiler_params=pltpu.CompilerParams(vmem_limit_bytes=4 * 2**20),
        name="finish",
    )(*arrays)


def per_device_whole(
    hidden, norm_gain, expert_ids, gate_probs, out_grad, gate_weight, up_weight, down_weight
):
    own_count, width = out_grad.shape
    top_count = expert_ids.shape[1]
    capacity = 2 * own_count * top_count // lax.axis_size(AXES)
    ids, probs = expert_ids.T, gate_probs.T
    *results, _ = whole_layer(
        ids, probs, hidden, norm_gain[None], out_grad, gate_weight[0], up_weight[0],
        down_weight[0], capacity,
    )
    layer_out, input_grad, gate_grad, gain_grad, gate_wgrad, up_wgrad, down_grad = finish(
        *results, ids, probs, norm_gain.reshape(-1, 128)
    )
    return (
        layer_out, input_grad.reshape(hidden.shape), gate_grad.T, gain_grad.reshape(width),
        gate_wgrad[None], up_wgrad[None], down_grad[None],
    )


def choose_form(*arrays):
    hidden, _, expert_ids, _, out_grad = arrays[:5]
    devices = lax.axis_size(AXES)
    capacity = 2 * out_grad.shape[0] * expert_ids.shape[1] // devices
    fits = devices <= 32 and capacity * 4 == 128 and out_grad.shape[0] == 64
    return (per_device_whole if fits else per_device)(*arrays)


def solution(mesh):
    rows, wide = P(AXES, None), P(AXES, None, None)
    in_specs = (P("dp", None), P(), rows, rows, rows, wide, wide, wide)
    out_specs = (rows, P("dp", None), rows, P(), wide, wide, wide)
    return jax.shard_map(
        choose_form, mesh=mesh, in_specs=in_specs, out_specs=out_specs, check_vma=False
    )
```

```python
import functools

import jax
import jax.numpy as jnp
from jax import lax
from jax.experimental import pallas as pl
from jax.experimental.pallas import tpu as pltpu
from jax.sharding import PartitionSpec as P

epsilon = 1e-06
AXES = ("dp", "tensor")
MESH = pl.DeviceIdType.MESH
f32, bf16 = jnp.float32, jnp.bfloat16


class Place:
    def __init__(self, line):
        self.line = line
        dp, tensor = lax.axis_index("dp"), lax.axis_index("tensor")
        self.z, self.x = dp // 2, dp % 2
        self.y, self.c = tensor // 2, tensor % 2

    def block(self, z, flip):
        x = 1 - self.x if flip in (1, 3) else self.x
        y = 1 - self.y if flip in (2, 3) else self.y
        return x, y

    def index(self, z, flip, c):
        x, y = self.block(z, flip)
        return (z * 2 + x) * 4 + y * 2 + c

    def device(self, z, flip, c):
        x, y = self.block(z, flip)
        return (z * 2 + x, y * 2 + c)

    def order(self, step, farthest_first):
        result = jnp.int32(0)
        for own in range(self.line):
            listed = sorted(range(self.line), key=lambda p: (abs(p - own), p))
            if farthest_first:
                listed = listed[::-1]
            result = jnp.where(self.z == own, jnp.int32(listed[step]), result)
        return result

    def greet(self):
        barrier = pltpu.get_barrier_semaphore()

        def tell(device):
            pl.semaphore_signal(barrier, inc=1, device_id=device, device_id_type=MESH)

        for flip, c in ((1, self.c), (2, self.c), (0, 1 - self.c)):
            tell(self.device(self.z, flip, c))
        below, above = self.z > 0, self.z < self.line - 1
        pl.when(below)(lambda: tell(self.device(self.z - 1, 0, self.c)))
        pl.when(above)(lambda: tell(self.device(self.z + 1, 0, self.c)))
        pl.semaphore_wait(barrier, 3 + below.astype(jnp.int32) + above.astype(jnp.int32))


UP, DOWN, SIDE, FACE, HALF0, HALF1, CORE = 0, 1, 2, 3, 4, 5, 6


class Gather:
    def __init__(self, place, own, held, send, recv, keep):
        self.p, self.own, self.held = place, own, held
        self.send, self.recv, self.keep = send, recv, keep
        self.half = own.shape[0] // 2

    def landing(self, kind):
        return kind

    def copy(self, kind, zz, flip, part, device, own=False):
        where = self.p.index(zz, flip, self.p.c)
        dst = self.held.at[where]
        src = self.own if own else dst
        if part is not None:
            rows = pl.ds(part * self.half, self.half)
            src, dst = src.at[rows], dst.at[rows]
        return pltpu.make_async_remote_copy(
            src_ref=src, dst_ref=dst, send_sem=self.send.at[kind, zz],
            recv_sem=self.recv.at[self.landing(kind), zz], device_id=device,
            device_id_type=MESH,
        )

    def up(self, zz, own=False):
        return self.copy(UP, zz, 0, None, self.p.device(self.p.z + 1, 0, self.p.c), own)

    def down(self, zz, own=False):
        return self.copy(DOWN, zz, 0, None, self.p.device(self.p.z - 1, 0, self.p.c), own)

    def side(self, zz, own=False):
        return self.copy(SIDE, zz, 0, None, self.p.device(self.p.z, 1, self.p.c), own)

    def face(self, zz, own=False):
        return self.copy(FACE, zz, 0, None, self.p.device(self.p.z, 2, self.p.c), own)

    def half0(self, zz):
        return self.copy(HALF0, zz, 1, 0, self.p.device(self.p.z, 2, self.p.c))

    def half1(self, zz):
        return self.copy(HALF1, zz, 2, 1, self.p.device(self.p.z, 1, self.p.c))

    def core(self, zz, flip, own=False):
        return self.copy(CORE + flip, zz, flip, None, self.p.device(self.p.z, 0, 1 - self.p.c), own)

    def arrived(self, kind, zz, flip, part, c=None):
        where = self.p.index(zz, flip, self.p.c if c is None else c)
        dst = self.held.at[where]
        if part is not None:
            dst = dst.at[pl.ds(part * self.half, self.half)]
        pltpu.make_async_remote_copy(
            src_ref=dst, dst_ref=dst, send_sem=self.send.at[kind, zz],
            recv_sem=self.recv.at[self.landing(kind), zz],
            device_id=self.p.device(self.p.z, 0, 1 - self.p.c), device_id_type=MESH,
        ).wait_recv()

    def first(self):
        p = self.p
        pltpu.make_async_copy(self.own, self.held.at[p.index(p.z, 0, p.c)], self.keep).start()
        pl.when(p.z < p.line - 1)(lambda: self.up(p.z, True).start())
        pl.when(p.z > 0)(lambda: self.down(p.z, True).start())
        self.side(p.z, True).start()
        self.face(p.z, True).start()
        self.core(p.z, 0, True).start()

    def column(self, step):
        p, zz = self.p, self.p.order(step, False)

        @pl.when(zz < p.z)
        def _():
            self.arrived(UP, zz, 0, None)
            pl.when(p.z < p.line - 1)(lambda: self.up(zz).start())

        @pl.when(zz > p.z)
        def _():
            self.arrived(DOWN, zz, 0, None)
            pl.when(p.z > 0)(lambda: self.down(zz).start())

        self.side(zz).start()
        self.face(zz).start()
        self.core(zz, 0).start()

    def plane(self, step):
        zz = self.p.order(step, False)
        self.arrived(SIDE, zz, 1, None)
        self.half0(zz).start()
        self.core(zz, 1).start()
        self.arrived(FACE, zz, 2, None)
        self.half1(zz).start()
        self.core(zz, 2).start()

    def corner(self, step):
        zz = self.p.order(step, False)
        self.arrived(HALF0, zz, 3, 0)
        self.arrived(HALF1, zz, 3, 1)
        self.core(zz, 3).start()

    def slot(self, step):
        line = self.p.line
        if step == 0:
            self.first()
        elif 0 < step < line:
            self.column(step)
        if 0 <= step - 1 < line:
            self.plane(step - 1)
        if 0 <= step - 2 < line:
            self.corner(step - 2)

    def finish(self):
        p = self.p
        for zz in range(p.line):
            for flip in range(4):
                self.arrived(CORE + flip, zz, flip, None, 1 - p.c)
        for zz in range(p.line):
            pl.when((zz <= p.z) & (p.z < p.line - 1))(lambda zz=zz: self.up(zz).wait_send())
            pl.when((zz >= p.z) & (p.z > 0))(lambda zz=zz: self.down(zz).wait_send())
            for one in (self.side(zz), self.face(zz), self.half0(zz), self.half1(zz)):
                one.wait_send()
            for flip in range(4):
                self.core(zz, flip).wait_send()
        pltpu.make_async_copy(self.own, self.held.at[p.index(p.z, 0, p.c)], self.keep).wait()


def gather_kernel(line, offsets, *refs):
    count = len(offsets)
    owns, helds = refs[:count], refs[count:2 * count]
    send, recv, keep = refs[2 * count:]
    place = Place(line)
    place.greet()
    arrays = [
        Gather(place, owns[i], helds[i], send.at[i], recv.at[i], keep.at[i]) for i in range(count)
    ]
    for step in range(max(offsets) + line + 2):
        for one, offset in zip(arrays, offsets):
            one.slot(step - offset)
    for one in arrays:
        one.finish()


def gather_all(arrays, offsets, number):
    line = lax.axis_size("dp") // 2
    devices = lax.axis_size(AXES)
    count = len(arrays)
    return pl.pallas_call(
        functools.partial(gather_kernel, line, offsets),
        out_shape=[jax.ShapeDtypeStruct((devices,) + a.shape, a.dtype) for a in arrays],
        in_specs=[pl.BlockSpec(memory_space=pltpu.VMEM)] * count,
        out_specs=[pl.BlockSpec(memory_space=pl.ANY)] * count,
        scratch_shapes=[
            pltpu.SemaphoreType.DMA((count, 10, line)),
            pltpu.SemaphoreType.DMA((count, 10, line)),
            pltpu.SemaphoreType.DMA((count,)),
        ],
        compiler_params=pltpu.CompilerParams(collective_id=number, has_side_effects=True),
        name=f"gather{number}",
    )(*arrays)


def add_rows(start, count, store, *loads):
    chunk = 16

    @pl.loop(0, count // chunk)
    def _(i):
        rows = pl.ds(pl.multiple_of(start + i * chunk, chunk), chunk)
        total = loads[0](rows).astype(f32)
        for load in loads[1:]:
            total = total + load(rows).astype(f32)
        store(rows, total)


def dot(a, b, ca, cb):
    return lax.dot_general(a, b, (((ca,), (cb,)), ((), ())), preferred_element_type=f32)


def row_grads(act_grad, gate_pre, up_pre):
    sigma = jax.nn.sigmoid(gate_pre)
    gate_pgrad = act_grad * up_pre * sigma * (1.0 + gate_pre * (1.0 - sigma))
    return gate_pgrad.astype(bf16), (act_grad * (gate_pre * sigma)).astype(bf16)


def backward_plain(cotan, gate_pre, up_pre, w_down, w_gate, w_up):
    gate_pgrad, up_pgrad = row_grads(dot(cotan, w_down, 1, 1), gate_pre, up_pre)
    back = dot(gate_pgrad, w_gate, 1, 1) + dot(up_pgrad, w_up, 1, 1)
    return gate_pgrad, up_pgrad, back.astype(bf16)


def backward_tile(step, ready, ins, outs):
    cotan, gate_pre, up_pre, w_down, w_gate, w_up = ins
    gate_pgrad, up_pgrad, back = outs
    if step == 0:
        ready(0, 1, 2, 3)
    count = cotan.shape[0] // 4
    rows = pl.ds(step * count, count)
    one, two = row_grads(dot(cotan[rows], w_down[...], 1, 1), gate_pre[rows], up_pre[rows])
    gate_pgrad[rows] = one
    up_pgrad[rows] = two
    if step == 0:
        ready(4, 5)
    wide = 512

    @pl.loop(0, back.shape[1] // wide)
    def _(i):
        cols = pl.ds(pl.multiple_of(i * wide, wide), wide)
        total = dot(gate_pgrad[rows], w_gate[cols], 1, 1) + dot(up_pgrad[rows], w_up[cols], 1, 1)
        back[rows, cols] = total.astype(bf16)


def weights_plain(inputs, gate_pgrad, up_pgrad, act, cotan):
    return tuple(
        dot(a, b, 0, 0).astype(bf16)
        for a, b in ((inputs, gate_pgrad), (inputs, up_pgrad), (act, cotan))
    )


def weights_tile(step, ready, ins, outs):
    inputs, gate_pgrad, up_pgrad, act, cotan = ins
    gate_wgrad, up_wgrad, down_grad = outs
    if step == 0:
        ready(0, 1, 2)
    deep, wide = 256, 512
    share = inputs.shape[1] // deep // 4

    @pl.loop(step * share, (step + 1) * share)
    def _(i):
        cols = pl.ds(pl.multiple_of(i * deep, deep), deep)
        block = inputs[:, cols]
        gate_wgrad[cols] = dot(block, gate_pgrad[...], 0, 0).astype(bf16)
        up_wgrad[cols] = dot(block, up_pgrad[...], 0, 0).astype(bf16)

    if step == 0:
        ready(3, 4)
    if step * deep < act.shape[1]:
        rows = pl.ds(step * deep, deep)

        @pl.loop(0, cotan.shape[1] // wide)
        def _(i):
            cols = pl.ds(pl.multiple_of(i * wide, wide), wide)
            down_grad[rows, cols] = dot(act[:, rows], cotan[:, cols], 0, 0).astype(bf16)


def scatter_kernel(line, job, n_in, n_out, *refs):
    part, refs = refs[0], refs[1:]
    job_in, refs = refs[:n_in], refs[n_in:]
    out, refs = refs[0], refs[1:]
    job_out, refs = refs[:n_out], refs[n_out:]
    mine, theirs, half_in, side_in, face_in, up_in, down_in, send, recv, keep = refs[:10]
    held_in, held_out = refs[10:10 + n_in], refs[10 + n_in:10 + n_in + n_out]
    if job is not None:
        in_sem, out_sem = refs[10 + n_in + n_out:]
        arriving = [
            pltpu.make_async_copy(job_in[i], held_in[i], in_sem.at[i]) for i in range(n_in)
        ]
        leaving = [
            pltpu.make_async_copy(held_out[i], job_out[i], out_sem.at[i]) for i in range(n_out)
        ]

    def ready(*which):
        for i in which:
            arriving[i].wait()

    p = Place(line)
    p.greet()
    count = out.shape[0]
    half = count // 2
    z = p.z

    def put(ref, index):
        def store(rows, value):
            ref[index + (rows,)] = value.astype(ref.dtype)
        return store

    def get(ref, index):
        return lambda rows: ref[index + (rows,)]

    def remote(src, dst, kind, zz, device):
        return pltpu.make_async_remote_copy(
            src_ref=src, dst_ref=dst, send_sem=send.at[kind, zz], recv_sem=recv.at[kind, zz],
            device_id=device, device_id_type=MESH,
        )

    def core(zz, flip):
        return remote(
            part.at[p.index(zz, flip, 1 - p.c)], theirs.at[zz, flip], CORE + flip, zz,
            p.device(z, 0, 1 - p.c),
        )

    def load(zz, flip):
        return pltpu.make_async_copy(
            part.at[p.index(zz, flip, p.c)], mine.at[zz, flip], keep.at[flip, zz]
        )

    def half0(zz):
        return remote(
            theirs.at[zz, 3, pl.ds(0, half)], half_in.at[zz, 0], HALF0, zz, p.device(z, 2, p.c)
        )

    def half1(zz):
        return remote(
            theirs.at[zz, 3, pl.ds(half, half)], half_in.at[zz, 1], HALF1, zz, p.device(z, 1, p.c)
        )

    def side(zz):
        return remote(theirs.at[zz, 1], side_in.at[zz], SIDE, zz, p.device(z, 1, p.c))

    def face(zz):
        return remote(theirs.at[zz, 2], face_in.at[zz], FACE, zz, p.device(z, 2, p.c))

    def up(zz):
        return remote(theirs.at[zz, 0], up_in.at[zz], UP, zz, p.device(z + 1, 0, p.c))

    def down(zz):
        return remote(theirs.at[zz, 0], down_in.at[zz], DOWN, zz, p.device(z - 1, 0, p.c))

    def joined(zz, flip):
        core(zz, flip).wait_recv()
        load(zz, flip).wait()
        add_rows(
            0, count, put(theirs, (zz, flip)), get(theirs, (zz, flip)), get(mine, (zz, flip))
        )

    for step in range(line):
        zz = p.order(step, True)
        for flip in (3, 1, 2, 0):
            core(zz, flip).start()
            load(zz, flip).start()

    if job is not None:
        for copy in arriving:
            copy.start()

    def corner(step):
        zz = p.order(step, True)
        joined(zz, 3)
        half0(zz).start()
        half1(zz).start()
        for flip in (1, 2, 0):
            joined(zz, flip)

    def plane(step):
        zz = p.order(step, True)
        half0(zz).wait_recv()
        here = (zz, 1)
        add_rows(
            0, half, put(theirs, here), get(theirs, here), get(half_in, (zz, 0))
        )
        side(zz).start()
        half1(zz).wait_recv()

        @pl.loop(0, half // 16)
        def _(i):
            low = pl.ds(pl.multiple_of(i * 16, 16), 16)
            high = pl.ds(pl.multiple_of(half + i * 16, 16), 16)
            total = theirs[zz, 2, high].astype(f32) + half_in[zz, 1, low].astype(f32)
            theirs[zz, 2, high] = total.astype(bf16)

        face(zz).start()

    def column(step):
        zz = p.order(step, True)
        side(zz).wait_recv()
        face(zz).wait_recv()
        base = (get(theirs, (zz, 0)), get(side_in, (zz,)), get(face_in, (zz,)))
        if step == line - 1:
            add_rows(0, count, put(out, ()), *base)

            @pl.when(z > 0)
            def _():
                up(zz).wait_recv()
                add_rows(0, count, put(out, ()), get(out, ()), get(up_in, (zz,)))

            @pl.when(z < line - 1)
            def _():
                down(zz).wait_recv()
                add_rows(0, count, put(out, ()), get(out, ()), get(down_in, (zz,)))

            return

        def onward(copy, source, more):
            @pl.when(more)
            def _():
                copy(zz).wait_recv()
                add_rows(0, count, put(theirs, (zz, 0)), *base, get(source, (zz,)))

            @pl.when(jnp.logical_not(more))
            def _():
                add_rows(0, count, put(theirs, (zz, 0)), *base)

            copy(zz).start()

        pl.when(zz > z)(lambda: onward(up, up_in, z > 0))
        pl.when(zz < z)(lambda: onward(down, down_in, z < line - 1))

    for step in range(line + 2):
        if step < line:
            corner(step)
        if 0 <= step - 1 < line:
            plane(step - 1)
        if 0 <= step - 2 < line:
            column(step - 2)
        if job is not None and step < 4:
            job(step, ready, held_in, held_out)
            if step == 3:
                for copy in leaving:
                    copy.start()

    for zz in range(line):
        for flip in range(4):
            core(zz, flip).wait_send()
        for one in (half0, half1, side, face):
            one(zz).wait_send()
        pl.when(zz > z)(lambda zz=zz: up(zz).wait_send())
        pl.when(zz < z)(lambda zz=zz: down(zz).wait_send())
    if job is not None:
        for copy in leaving:
            copy.wait()


def scatter_sum(part, number, job, plain, arrays):
    line = lax.axis_size("dp") // 2
    _, rows, width = part.shape
    results = jax.eval_shape(plain, *arrays)
    size = sum(a.size * a.dtype.itemsize for a in list(arrays) + list(results))
    extra = None
    if size + 13 * line * rows * width * 2 > 52 * 2**20:
        extra, job, arrays, results = plain(*arrays), None, (), ()
    anywhere = pl.BlockSpec(memory_space=pl.ANY)
    more = []
    if job is not None:
        more = [pltpu.VMEM(a.shape, a.dtype) for a in list(arrays) + list(results)] + [
            pltpu.SemaphoreType.DMA((len(arrays),)),
            pltpu.SemaphoreType.DMA((len(results),)),
        ]
    total, *done = pl.pallas_call(
        functools.partial(scatter_kernel, line, job, len(arrays), len(results)),
        out_shape=[jax.ShapeDtypeStruct((rows, width), f32)]
        + [jax.ShapeDtypeStruct(r.shape, r.dtype) for r in results],
        in_specs=[anywhere] * (1 + len(arrays)),
        out_specs=[pl.BlockSpec(memory_space=pltpu.VMEM)] + [anywhere] * len(results),
        scratch_shapes=[
            pltpu.VMEM((line, 4, rows, width), bf16),
            pltpu.VMEM((line, 4, rows, width), bf16),
            pltpu.VMEM((line, 2, rows // 2, width), bf16),
            pltpu.VMEM((line, rows, width), bf16),
            pltpu.VMEM((line, rows, width), bf16),
            pltpu.VMEM((line, rows, width), bf16),
            pltpu.VMEM((line, rows, width), bf16),
            pltpu.SemaphoreType.DMA((10, line)),
            pltpu.SemaphoreType.DMA((10, line)),
            pltpu.SemaphoreType.DMA((4, line)),
        ] + more,
        compiler_params=pltpu.CompilerParams(
            collective_id=number, has_side_effects=True, vmem_limit_bytes=62 * 2**20
        ),
        name=f"scatter{number}",
    )(part, *arrays)
    return total, tuple(done) if extra is None else extra


def last_kernel(line, small, grad, held, rows_out, send, recv, keep, tsend, trecv, tkeep):
    p = Place(line)
    p.greet()
    here = p.y * 2 + p.c
    other = (1 - p.y) * 2 + p.c

    def tremote(src, where, i, device):
        return pltpu.make_async_remote_copy(
            src_ref=src, dst_ref=rows_out.at[where], send_sem=tsend.at[i], recv_sem=trecv.at[i],
            device_id=device, device_id_type=MESH,
        )

    partner = p.device(p.z, 0, 1 - p.c)
    keeping = pltpu.make_async_copy(grad, rows_out.at[here], tkeep)
    keeping.start()
    across = tremote(grad, here, 0, p.device(p.z, 2, p.c))
    beside = tremote(grad, here, 1, partner)
    relay = tremote(rows_out.at[other], other, 2, partner)
    across.start()
    beside.start()
    one = Gather(p, small, held, send, recv, keep)
    for step in range(line + 2):
        one.slot(step)
        if step == 1:
            across.wait_recv()
            relay.start()
    one.finish()
    beside.wait_recv()
    relay.wait_recv()
    for copy in (across, beside, relay):
        copy.wait_send()
    keeping.wait()


def gather_last(small, grad, number):
    line = lax.axis_size("dp") // 2
    devices, quarters = lax.axis_size(AXES), lax.axis_size("tensor")
    anywhere = pl.BlockSpec(memory_space=pl.ANY)
    return pl.pallas_call(
        functools.partial(last_kernel, line),
        out_shape=[
            jax.ShapeDtypeStruct((devices,) + small.shape, small.dtype),
            jax.ShapeDtypeStruct((quarters,) + grad.shape, grad.dtype),
        ],
        in_specs=[pl.BlockSpec(memory_space=pltpu.VMEM)] * 2,
        out_specs=[anywhere, anywhere],
        scratch_shapes=[
            pltpu.SemaphoreType.DMA((10, line)),
            pltpu.SemaphoreType.DMA((10, line)),
            pltpu.SemaphoreType.DMA,
            pltpu.SemaphoreType.DMA((3,)),
            pltpu.SemaphoreType.DMA((3,)),
            pltpu.SemaphoreType.DMA,
        ],
        compiler_params=pltpu.CompilerParams(collective_id=number, has_side_effects=True),
        name=f"last{number}",
    )(small, grad)


def per_device(
    hidden, norm_gain, expert_ids, gate_probs, out_grad, gate_weight, up_weight, down_weight
):
    quarters = lax.axis_size("tensor")
    quarter = lax.axis_index("tensor")
    own_count = hidden.shape[0] // quarters
    width = hidden.shape[1]
    top_count = expert_ids.shape[1]
    devices = lax.axis_size(AXES)
    experts = gate_weight.shape[0] * devices
    capacity = 2 * own_count * top_count // experts
    tokens = own_count * devices
    blocks_in = min(4, devices)
    groups = devices // blocks_in
    gtok = own_count * blocks_in
    gslots = capacity * blocks_in
    slots = groups * gslots
    me = lax.axis_index(AXES)

    own_rows = lax.dynamic_slice_in_dim(hidden, quarter * own_count, own_count, 0)
    values = own_rows.astype(f32)
    inverse = lax.rsqrt(jnp.mean(values * values, axis=-1, keepdims=True) + epsilon)
    unit_rows = values * inverse
    normed = (unit_rows * norm_gain).astype(bf16)
    grad_rows = out_grad.astype(f32)

    meta = jnp.concatenate(
        [
            expert_ids.astype(f32),
            gate_probs,
            jnp.zeros((own_count, 128 - 2 * top_count), f32),
        ],
        axis=1,
    )
    meta_all, normed_all, grads_all = gather_all(
        [meta, normed, out_grad], (0, 0, lax.axis_size("dp") // 2 - 1), 0
    )
    meta_all = meta_all.reshape(tokens, 128)
    ids_all = meta_all[:, :top_count].astype(jnp.int32)
    probs_all = meta_all[:, top_count:2 * top_count]

    hits = ids_all == me
    member = jnp.any(hits, axis=1).reshape(devices, own_count)
    prob = jnp.sum(jnp.where(hits, probs_all, 0.0), axis=1)
    earlier = jnp.arange(own_count)[:, None] < jnp.arange(own_count)[None, :]
    place = jnp.dot(member.astype(bf16), earlier.astype(bf16), preferred_element_type=f32)
    place = place.astype(jnp.int32)
    block = jnp.arange(devices, dtype=jnp.int32)[:, None] % blocks_in
    slot = jnp.where(member, block * capacity + place, -1).reshape(groups, gtok)
    picks = slot[:, None, :] == jnp.arange(gslots, dtype=jnp.int32)[None, :, None]
    choose = picks.astype(bf16)
    slot_prob = jnp.sum(
        jnp.where(picks, prob.reshape(groups, 1, gtok), 0.0), axis=2
    ).reshape(slots, 1)

    def pack(rows):
        return jnp.einsum(
            "gst,gtd->gsd", choose, rows.reshape(groups, gtok, width), preferred_element_type=f32
        ).astype(bf16).reshape(slots, width)

    def spread(rows):
        return jnp.einsum(
            "gst,gsd->gtd", choose, rows.reshape(groups, gslots, width), preferred_element_type=f32
        ).astype(bf16).reshape(devices, own_count, width)

    w_gate, w_up, w_down = gate_weight[0], up_weight[0], down_weight[0]
    inputs = pack(normed_all)
    gate_pre = dot(inputs, w_gate, 1, 0)
    up_pre = dot(inputs, w_up, 1, 0)
    sigma = jax.nn.sigmoid(gate_pre)
    silu_vals = gate_pre * sigma
    act = (silu_vals * up_pre).astype(bf16)
    results = dot(act, w_down, 1, 0).astype(bf16)
    results_f = results.astype(f32)
    grads = pack(grads_all).astype(f32)
    cotan = (slot_prob * grads).astype(bf16)
    slot_gg = jnp.sum(grads * results_f, axis=1)
    layer_part, (gate_pgrad, up_pgrad, back) = scatter_sum(
        spread((slot_prob * results_f).astype(bf16)), 1, backward_tile, backward_plain,
        (cotan, gate_pre, up_pre, w_down, w_gate, w_up),
    )
    normed_total, (gate_wgrad, up_wgrad, down_grad) = scatter_sum(
        spread(back), 2, weights_tile, weights_plain,
        (inputs, gate_pgrad, up_pgrad, act, cotan),
    )
    gate_wgrad, up_wgrad, down_grad = gate_wgrad[None], up_wgrad[None], down_grad[None]
    token_gg = jnp.sum(jnp.where(picks, slot_gg.reshape(groups, gslots, 1), 0.0), axis=1)

    layer_out = (values + layer_part).astype(bf16)
    gain_part = jnp.sum(normed_total * unit_rows, axis=0)
    upstream = normed_total * norm_gain
    own_grad = grad_rows + inverse * (
        upstream - unit_rows * jnp.mean(upstream * unit_rows, axis=-1, keepdims=True)
    )
    small = jnp.concatenate([token_gg.reshape(-1, 128), gain_part.reshape(-1, 128)], axis=0)
    small_all, input_grad = gather_last(small, own_grad.astype(bf16), 3)
    input_grad = input_grad.reshape(hidden.shape)
    tiles = tokens // 128
    gain_grad = jnp.sum(small_all[:, tiles:, :], axis=0).reshape(width)
    mine = lax.dynamic_slice_in_dim(
        small_all[:, :tiles, :].reshape(devices, tokens), me * own_count, own_count, 1
    )
    named = expert_ids[:, :, None] == jnp.arange(devices, dtype=jnp.int32)[None, None, :]
    gate_grad = jnp.sum(jnp.where(named, mine.T[:, None, :], 0.0), axis=2)
    return (layer_out, input_grad, gate_grad, gain_grad, gate_wgrad, up_wgrad, down_grad)


CORNER_UP, CORNER_DOWN = 10, 11


def along_z(line, z, zz):
    apart = jnp.abs(jnp.int32(z) - zz)
    return (apart == 1) | ((apart == 2) & ((z == 0) | (z == line - 1)))


class Stream(Gather):
    def landing(self, kind):
        return (0, 0, 1, 2, 3, 4, 5, 6, 7, 8, 3, 3)[kind]

    def order(self, step):
        return self.p.order(step, False)

    def corner_up(self, zz):
        p = self.p
        return self.copy(CORNER_UP, zz, 3, None, p.device(p.z + 1, 0, p.c))

    def corner_down(self, zz):
        p = self.p
        return self.copy(CORNER_DOWN, zz, 3, None, p.device(p.z - 1, 0, p.c))

    def routes(self, zz):
        z, line = self.p.z, self.p.line
        up = (z < line - 1) & (zz <= z) & along_z(line, z + 1, zz)
        down = (z > 0) & (zz >= z) & along_z(line, z - 1, zz)
        return along_z(line, z, zz), up, down

    def plane(self, step):
        zz = self.order(step)
        flat = jnp.logical_not(self.routes(zz)[0])
        self.arrived(SIDE, zz, 1, None)
        pl.when(flat)(lambda: self.half0(zz).start())
        self.core(zz, 1).start()
        self.arrived(FACE, zz, 2, None)
        pl.when(flat)(lambda: self.half1(zz).start())
        self.core(zz, 2).start()

    def corner(self, step):
        zz, z = self.order(step), self.p.z
        via, up, down = self.routes(zz)

        @pl.when(jnp.logical_not(via))
        def _():
            self.arrived(HALF0, zz, 3, 0)
            self.arrived(HALF1, zz, 3, 1)

        pl.when(via & (zz < z))(lambda: self.arrived(CORNER_UP, zz, 3, None))
        pl.when(via & (zz > z))(lambda: self.arrived(CORNER_DOWN, zz, 3, None))
        pl.when(up)(lambda: self.corner_up(zz).start())
        pl.when(down)(lambda: self.corner_down(zz).start())
        self.core(zz, 3).start()

    def done(self, step):
        p, zz = self.p, self.order(step)
        if step == 0:
            pltpu.make_async_copy(
                self.own, self.held.at[p.index(p.z, 0, p.c)], self.keep
            ).wait()
        for flip in range(4):
            self.arrived(CORE + flip, zz, flip, None, 1 - p.c)

    def sent(self):
        p = self.p
        for zz in range(p.line):
            pl.when((zz <= p.z) & (p.z < p.line - 1))(lambda zz=zz: self.up(zz).wait_send())
            pl.when((zz >= p.z) & (p.z > 0))(lambda zz=zz: self.down(zz).wait_send())
            self.side(zz).wait_send()
            self.face(zz).wait_send()
            via, up, down = self.routes(jnp.int32(zz))

            @pl.when(jnp.logical_not(via))
            def _(zz=zz):
                self.half0(zz).wait_send()
                self.half1(zz).wait_send()

            pl.when(up)(lambda zz=zz: self.corner_up(zz).wait_send())
            pl.when(down)(lambda zz=zz: self.corner_down(zz).wait_send())
            for flip in range(4):
                self.core(zz, flip).wait_send()


def put(ref, index):
    def store(rows, value):
        ref[index + (rows,)] = value.astype(ref.dtype)
    return store


def get(ref, index):
    return lambda rows: ref[index + (rows,)]


class Scatter:
    def __init__(
        self, place, part, out, theirs, half_in, side_in, face_in, up_in, down_in, corner_up_in,
        corner_down_in, send, recv,
    ):
        self.p, self.part, self.out, self.theirs = place, part, out, theirs
        self.half_in, self.side_in, self.face_in = half_in, side_in, face_in
        self.up_in, self.down_in = up_in, down_in
        self.corner_up_in, self.corner_down_in = corner_up_in, corner_down_in
        self.sends, self.recvs = send, recv
        self.count = out.shape[0]
        self.half = self.count // 2

    def order(self, step):
        return self.p.order(step, True)

    def remote(self, src, dst, kind, zz, device):
        return pltpu.make_async_remote_copy(
            src_ref=src, dst_ref=dst, send_sem=self.sends.at[kind, zz],
            recv_sem=self.recvs.at[kind, zz], device_id=device, device_id_type=MESH,
        )

    def core(self, zz, flip):
        p = self.p
        return self.remote(
            self.part.at[p.index(zz, flip, 1 - p.c)], self.theirs.at[zz, flip], CORE + flip, zz,
            p.device(p.z, 0, 1 - p.c),
        )

    def half0(self, zz):
        p = self.p
        return self.remote(
            self.theirs.at[zz, 3, pl.ds(0, self.half)], self.half_in.at[self.flat(zz), 0], HALF0, zz,
            p.device(p.z, 2, p.c),
        )

    def half1(self, zz):
        p = self.p
        return self.remote(
            self.theirs.at[zz, 3, pl.ds(self.half, self.half)], self.half_in.at[self.flat(zz), 1], HALF1, zz,
            p.device(p.z, 1, p.c),
        )

    def side(self, zz):
        p = self.p
        return self.remote(
            self.theirs.at[zz, 1], self.side_in.at[zz], SIDE, zz, p.device(p.z, 1, p.c)
        )

    def face(self, zz):
        p = self.p
        return self.remote(
            self.theirs.at[zz, 2], self.face_in.at[zz], FACE, zz, p.device(p.z, 2, p.c)
        )

    def up(self, zz):
        p = self.p
        return self.remote(
            self.theirs.at[zz, 0], self.up_in.at[zz], UP, zz, p.device(p.z + 1, 0, p.c)
        )

    def down(self, zz):
        p = self.p
        return self.remote(
            self.theirs.at[zz, 0], self.down_in.at[zz], DOWN, zz, p.device(p.z - 1, 0, p.c)
        )

    def flat(self, zz):
        return jnp.where(zz == self.p.z, 0, 1)

    def corner_up(self, zz, slot):
        p = self.p
        return self.remote(
            self.theirs.at[zz, 3], self.corner_up_in.at[slot], CORNER_UP, zz,
            p.device(p.z + 1, 0, p.c),
        )

    def corner_down(self, zz, slot):
        p = self.p
        return self.remote(
            self.theirs.at[zz, 3], self.corner_down_in.at[slot], CORNER_DOWN, zz,
            p.device(p.z - 1, 0, p.c),
        )

    def give(self, step):
        zz = self.order(step)
        for flip in (3, 1, 2, 0):
            self.core(zz, flip).start()

    def joined(self, zz, flip):
        self.core(zz, flip).wait_recv()
        here = (zz, flip)
        add_rows(
            0, self.count, put(self.theirs, here), get(self.theirs, here),
            get(self.part, (self.p.index(zz, flip, self.p.c),)),
        )

    def corner(self, step):
        p, zz, here = self.p, self.order(step), (self.order(step), 3)
        z, line = p.z, p.line
        via = along_z(line, z, zz)
        below = (z > 0) & (zz >= z) & along_z(line, z - 1, zz)
        above = (z < line - 1) & (zz <= z) & along_z(line, z + 1, zz)

        def onward():
            pl.when(via & (zz > z))(lambda: self.corner_up(zz, zz - z - 1).start())
            pl.when(via & (zz < z))(lambda: self.corner_down(zz, z - 1 - zz).start())

            @pl.when(jnp.logical_not(via))
            def _():
                self.half0(zz).start()
                self.half1(zz).start()

        self.joined(zz, 3)
        pl.when(jnp.logical_not(below | above))(onward)
        for flip in (1, 2, 0):
            self.joined(zz, flip)

        @pl.when(below)
        def _():
            slot = zz - z
            self.corner_up(zz, slot).wait_recv()
            add_rows(
                0, self.count, put(self.theirs, here), get(self.theirs, here),
                get(self.corner_up_in, (slot,)),
            )

        @pl.when(above)
        def _():
            slot = z - zz
            self.corner_down(zz, slot).wait_recv()
            add_rows(
                0, self.count, put(self.theirs, here), get(self.theirs, here),
                get(self.corner_down_in, (slot,)),
            )

        pl.when(below | above)(onward)

    def plane(self, step):
        zz, half, theirs = self.order(step), self.half, self.theirs
        flat, slot = jnp.logical_not(along_z(self.p.line, self.p.z, zz)), self.flat(zz)
        here = (zz, 1)

        @pl.when(flat)
        def _():
            self.half0(zz).wait_recv()
            add_rows(0, half, put(theirs, here), get(theirs, here), get(self.half_in, (slot, 0)))

        self.side(zz).start()

        @pl.when(flat)
        def _():
            self.half1(zz).wait_recv()

            @pl.loop(0, half // 16)
            def _(i):
                low = pl.ds(pl.multiple_of(i * 16, 16), 16)
                high = pl.ds(pl.multiple_of(half + i * 16, 16), 16)
                total = theirs[zz, 2, high].astype(f32) + self.half_in[slot, 1, low].astype(f32)
                theirs[zz, 2, high] = total.astype(bf16)

        self.face(zz).start()

    def column(self, step):
        p, zz, count, out = self.p, self.order(step), self.count, self.out
        z, line = p.z, p.line
        self.side(zz).wait_recv()
        self.face(zz).wait_recv()
        base = (
            get(self.theirs, (zz, 0)), get(self.side_in, (zz,)), get(self.face_in, (zz,))
        )
        if step == line - 1:
            add_rows(0, count, put(out, ()), *base)

            @pl.when(z > 0)
            def _():
                self.up(zz).wait_recv()
                add_rows(0, count, put(out, ()), get(out, ()), get(self.up_in, (zz,)))

            @pl.when(z < line - 1)
            def _():
                self.down(zz).wait_recv()
                add_rows(0, count, put(out, ()), get(out, ()), get(self.down_in, (zz,)))

            return

        def onward(copy, source, more):
            @pl.when(more)
            def _():
                copy(zz).wait_recv()
                add_rows(0, count, put(self.theirs, (zz, 0)), *base, get(source, (zz,)))

            @pl.when(jnp.logical_not(more))
            def _():
                add_rows(0, count, put(self.theirs, (zz, 0)), *base)

            copy(zz).start()

        pl.when(zz > z)(lambda: onward(self.up, self.up_in, z > 0))
        pl.when(zz < z)(lambda: onward(self.down, self.down_in, z < line - 1))

    def given(self, step):
        zz = self.order(step)
        for flip in range(4):
            self.core(zz, flip).wait_send()

    def sent(self):
        z = self.p.z
        for zz in range(self.p.line):
            self.side(zz).wait_send()
            self.face(zz).wait_send()
            via = along_z(self.p.line, z, jnp.int32(zz))

            @pl.when(jnp.logical_not(via))
            def _(zz=zz):
                self.half0(zz).wait_send()
                self.half1(zz).wait_send()

            pl.when(via & (zz > z))(lambda zz=zz: self.corner_up(zz, 0).wait_send())
            pl.when(via & (zz < z))(lambda zz=zz: self.corner_down(zz, 0).wait_send())
            pl.when(zz > z)(lambda zz=zz: self.up(zz).wait_send())
            pl.when(zz < z)(lambda zz=zz: self.down(zz).wait_send())


class Both:
    def __init__(self, first, second, whole):
        self.parts, self.whole = (first, second), whole
        self.order = first.order

    def each(self, name, *args):
        for part in self.parts:
            getattr(part, name)(*args)

    def slot(self, step):
        line = self.parts[0].p.line
        if step == 0:
            self.each("first")
        elif 0 < step < line:
            self.each("column", step)
        if 0 <= step - 1 < line:
            self.each("plane", step - 1)
        if 0 <= step - 2 < line:
            self.each("corner", step - 2)

    def done(self, step):
        self.each("done", step)

    def sent(self):
        self.whole.sent()

    def give(self, step):
        self.each("give", step)

    def given(self, step):
        self.whole.given(step)

    def corner(self, step):
        self.each("corner", step)

    def plane(self, step):
        self.each("plane", step)

    def column(self, step):
        self.each("column", step)


def layer_kernel(
    line, tops, capacity,
    ids, probs, hidden, gain, out_grad, w_gate_in, w_up_in, w_down_in,
    layer_out, rows_out, gg_out, gain_out, w_gate, w_up, w_down, grads_all,
    turn, meta, meta_all, normed_all, hid, normed, inputs, cotan, stage, choose,
    gate_pre, up_pre, act, gate_pgrad, up_pgrad, ggs, gacc, small, small_all, total, own_grad,
    theirs1, half1, side1, face1, up1, down1, cup1, cdown1,
    theirs2, half2, side2, face2, up2, down2, cup2, cdown2,
    gsend, grecv, gkeep, srecv, load, stage_sem, tsend, trecv, tkeep,
):
    p = Place(line)
    own, width = hid.shape
    inner = act.shape[1]
    me = p.index(p.z, 0, p.c)
    gtok, gslots = choose.shape[1:]
    pslots = 2 * gslots
    barrier = pltpu.get_barrier_semaphore()

    def tell(device):
        pl.semaphore_signal(barrier, inc=1, device_id=device, device_id_type=MESH)

    for flip, c in ((1, p.c), (2, p.c), (0, 1 - p.c)):
        tell(p.device(p.z, flip, c))
    below, above = p.z > 0, p.z < line - 1
    pl.when(below)(lambda: tell(p.device(p.z - 1, 0, p.c)))
    pl.when(above)(lambda: tell(p.device(p.z + 1, 0, p.c)))

    quarter = p.y * 2 + p.c
    mine = pltpu.make_async_copy(
        hidden.at[pl.ds(pl.multiple_of(quarter * own, own), own)], hid, load.at[0]
    )
    mine.start()
    loads = [
        pltpu.make_async_copy(a, b, load.at[1 + i])
        for i, (a, b) in enumerate(((w_gate_in, w_gate), (w_up_in, w_up), (w_down_in, w_down)))
    ]
    turn[...] = jnp.zeros_like(turn)
    turn[0:tops, 0:own] = ids[...].astype(f32)
    turn[tops:2 * tops, 0:own] = probs[...]
    meta[...] = turn[...].T[0:own]
    mine.wait()

    def unit_of(rows):
        values = hid[rows].astype(f32)
        inverse = lax.rsqrt(jnp.mean(values * values, axis=-1, keepdims=True) + epsilon)
        return values, inverse

    @pl.loop(0, own // 16)
    def _(i):
        rows = pl.ds(pl.multiple_of(i * 16, 16), 16)
        values, inverse = unit_of(rows)
        normed[rows] = (values * inverse * gain[...]).astype(bf16)

    pl.semaphore_wait(barrier, 3 + below.astype(jnp.int32) + above.astype(jnp.int32))

    def stream(i, j, source, held):
        return Stream(p, source, held, gsend.at[i], grecv.at[j], gkeep.at[j])

    upper = own // 2

    def streams(i, j, source, held):
        halves = [
            stream(i, j + k, source.at[pl.ds(k * upper, upper)], held.at[:, pl.ds(k * upper, upper)])
            for k in range(2)
        ]
        return Both(*halves, stream(i, j, source, held))

    g_meta, g_small = stream(0, 0, meta, meta_all), stream(0, 1, small, small_all)
    g_norm, g_grad = streams(1, 2, normed, normed_all), streams(2, 4, out_grad, grads_all)
    def scatter(i, theirs, half_in, side_in, face_in, up_in, down_in, cup_in, cdown_in):
        def one(k):
            rows, quarter_rows = pl.ds(k * upper, upper), pl.ds(k * upper // 2, upper // 2)
            return Scatter(
                p, normed_all.at[:, rows], total.at[rows], theirs.at[:, :, rows],
                half_in.at[:, :, quarter_rows], side_in.at[:, rows], face_in.at[:, rows],
                up_in.at[:, rows], down_in.at[:, rows], cup_in.at[:, rows], cdown_in.at[:, rows],
                gsend.at[1 + i], srecv.at[2 * i + k],
            )
        whole = Scatter(
            p, normed_all, total, theirs, half_in, side_in, face_in, up_in, down_in, cup_in,
            cdown_in, gsend.at[1 + i], srecv.at[2 * i],
        )
        return Both(one(0), one(1), whole)

    s_out = scatter(0, theirs1, half1, side1, face1, up1, down1, cup1, cdown1)
    s_back = scatter(1, theirs2, half2, side2, face2, up2, down2, cup2, cdown2)
    me_f = me.astype(f32)
    wide = 512

    def columns(body, size=wide, full=width):
        @pl.loop(0, full // size)
        def _(i):
            body(pl.ds(pl.multiple_of(i * size, size), size))

    def hits_of(zz, h):
        got = meta_all[pl.ds(8 * zz + 4 * h, 4)].reshape(gtok, 128)
        lane = lax.broadcasted_iota(jnp.int32, (gtok, 128), 1)
        return got, lane, jnp.where((got == me_f) & (lane < tops), 1.0, 0.0)

    def prob_of(zz, h):
        got, _, hit = hits_of(zz, h)
        return jnp.sum(pltpu.roll(hit, tops, 1) * got, axis=1, keepdims=True)

    def route(zz):
        for h in range(2):
            _, lane, hit = hits_of(zz, h)
            member = jnp.sum(hit, axis=1, keepdims=True)
            a = lax.broadcasted_iota(jnp.int32, (gtok, gtok), 0)
            b = lax.broadcasted_iota(jnp.int32, (gtok, gtok), 1)
            earlier = jnp.where((a > b) & (a // own == b // own), 1.0, 0.0).astype(bf16)
            spot = dot(earlier, jnp.broadcast_to(member, (gtok, 128)).astype(bf16), 1, 0)
            block = lax.broadcasted_iota(jnp.int32, (gtok, 128), 0) // own
            spot = spot + (block * capacity).astype(f32)
            picked = (spot == lane.astype(f32)) & (member > 0.0)
            choose[2 * zz + h] = jnp.where(picked, 1.0, 0.0).astype(bf16)

    def slots(zz, h=None):
        if h is None:
            return pl.ds(pl.multiple_of(zz * pslots, pslots), pslots)
        return pl.ds(pl.multiple_of(zz * pslots + h * gslots, gslots), gslots)

    def forward(zz):
        route(zz)
        for h in range(2):
            pick = choose[2 * zz + h]

            def pack(cols, pick=pick, h=h):
                rows = normed_all[pl.ds(8 * zz + 4 * h, 4), :, cols].reshape(gtok, wide)
                inputs[slots(zz, h), cols] = dot(pick, rows, 0, 0).astype(bf16)

            columns(pack)
        rows = slots(zz)

        def products(cols):
            gate = dot(inputs[rows], w_gate[:, cols], 1, 0)
            up = dot(inputs[rows], w_up[:, cols], 1, 0)
            gate_pre[rows, cols] = gate
            up_pre[rows, cols] = up
            act[rows, cols] = (gate * jax.nn.sigmoid(gate) * up).astype(bf16)

        columns(products, 256, inner)

    def result(zz):
        rows = slots(zz)
        probs = [prob_of(zz, h) for h in range(2)]

        def expand(cols):
            done = dot(act[rows], w_down[:, cols], 1, 0).astype(bf16)
            for h in range(2):
                got = dot(choose[2 * zz + h], done[h * gslots:(h + 1) * gslots], 1, 0)
                normed_all[pl.ds(8 * zz + 4 * h, 4), :, cols] = (
                    (got * probs[h]).astype(bf16).reshape(4, own, wide)
                )

        columns(expand)

    def fetch(step):
        zz = s_back.order(step)
        return pltpu.make_async_copy(grads_all.at[pl.ds(8 * zz, 8)], stage, stage_sem)

    def cotangent(step):
        zz = s_back.order(step)
        fetch(step).wait()
        for h in range(2):
            pick, prob = choose[2 * zz + h], prob_of(zz, h)
            which = lax.broadcasted_iota(jnp.int32, (gtok, 128), 1)
            high = prob.astype(bf16).astype(f32)
            middle = (prob - high).astype(bf16).astype(f32)
            low = prob - high - middle
            parts = jnp.where(
                which == 0, high, jnp.where(which == 1, middle, jnp.where(which == 2, low, 0.0))
            )
            factor = jnp.sum(dot(pick, parts.astype(bf16), 0, 0), axis=1, keepdims=True)

            def pack(cols, pick=pick, factor=factor, h=h):
                rows = stage[4 * h:4 * h + 4, :, cols].reshape(gtok, wide)
                cotan[slots(zz, h), cols] = (dot(pick, rows, 0, 0) * factor).astype(bf16)

            columns(pack)
        if step < line - 1:
            fetch(step + 1).start()

    def hidden_grads(zz):
        rows = slots(zz)
        ggs[...] = jnp.zeros_like(ggs)

        def chunk(cols):
            act_grad = dot(cotan[rows], w_down[cols], 1, 1)
            one, two = row_grads(act_grad, gate_pre[rows, cols], up_pre[rows, cols])
            gate_pgrad[rows, cols] = one
            up_pgrad[rows, cols] = two
            both = act_grad * act[rows, cols].astype(f32)
            ggs[...] += both[:, :128] + both[:, 128:]

        columns(chunk, 256, inner)
        for h in range(2):
            line_sum = jnp.sum(ggs[h * gslots:(h + 1) * gslots].T, axis=0, keepdims=True)
            high = line_sum.astype(bf16).astype(f32)
            which = lax.broadcasted_iota(jnp.int32, (16, gslots), 0)
            parts = jnp.where(which == 0, high, jnp.where(which == 1, line_sum - high, 0.0))
            spread = dot(parts.astype(bf16), choose[2 * zz + h], 1, 1)
            row = jnp.sum(spread, axis=0, keepdims=True)
            for k in range(gtok // 128):
                small[pl.ds(4 * zz + 2 * h + k, 1)] = row[:, 128 * k:128 * k + 128]

    def backs(zz):
        rows = slots(zz)

        def chunk(cols):
            back = dot(gate_pgrad[rows], w_gate[cols], 1, 1)
            back = (back + dot(up_pgrad[rows], w_up[cols], 1, 1)).astype(bf16)
            terms = back.astype(f32) * inputs[rows, cols].astype(f32)
            gacc[:, cols] += jnp.sum(terms.reshape(pslots // 8, 8, wide), axis=0)
            for h in range(2):
                got = dot(choose[2 * zz + h], back[h * gslots:(h + 1) * gslots], 1, 0)
                normed_all[pl.ds(8 * zz + 4 * h, 4), :, cols] = (
                    got.astype(bf16).reshape(4, own, wide)
                )

        columns(chunk)

    def weight_grads(step):
        deep = 256
        share = width // deep // 4

        @pl.loop(step * share, (step + 1) * share)
        def _(i):
            cols = pl.ds(pl.multiple_of(i * deep, deep), deep)
            block = inputs[:, cols]
            w_gate[cols] = dot(block, gate_pgrad[...], 0, 0).astype(bf16)
            w_up[cols] = dot(block, up_pgrad[...], 0, 0).astype(bf16)

        if step * deep < inner:
            rows = pl.ds(step * deep, deep)

            def chunk(cols):
                w_down[rows, cols] = dot(act[:, rows], cotan[:, cols], 0, 0).astype(bf16)

            columns(chunk)

    g_meta.slot(0)
    g_norm.slot(0)
    for copy in loads:
        copy.start()
    gacc[...] = jnp.zeros_like(gacc)

    def arrived(step):
        g_meta.done(step)
        g_norm.done(step)

    def relay_norm(step):
        g_meta.slot(step)
        g_norm.slot(step)

    def loaded():
        for copy in loads:
            copy.wait()

    def expand_results(step):
        result(s_out.order(step))
        s_out.give(step)

    def grads_here():
        for step in range(line):
            g_grad.done(step)
        fetch(0).start()

    def input_grads(step):
        s_out.given(step)
        backs(s_back.order(step))
        s_back.give(step)

    def add_hidden():
        @pl.loop(0, own // 16)
        def _(i):
            rows = pl.ds(pl.multiple_of(i * 16, 16), 16)
            layer_out[rows] = (hid[rows].astype(f32) + total[rows]).astype(bf16)

    first = small.shape[0] - width // 128

    def small_start():
        gsum = jnp.sum(gacc[...], axis=0, keepdims=True)
        for k in range(width // 128):
            small[first + k:first + k + 1] = gsum[:, 128 * k:128 * k + 128]
        g_small.slot(0)

    relay_norm(1)
    relay_norm(2)
    relay_norm(3)
    g_grad.slot(0)
    arrived(0)
    loaded()
    forward(g_norm.order(0))
    relay_norm(4)
    g_grad.slot(1)
    arrived(1)
    forward(g_norm.order(1))
    relay_norm(5)
    g_grad.slot(2)
    arrived(2)
    forward(g_norm.order(2))
    g_grad.slot(3)
    arrived(3)
    forward(g_norm.order(3))
    g_norm.sent()
    g_meta.sent()
    expand_results(0)
    g_grad.slot(4)
    expand_results(1)
    s_out.corner(0)
    g_grad.slot(5)
    expand_results(2)
    s_out.corner(1)
    s_out.plane(0)
    expand_results(3)
    s_out.corner(2)
    s_out.plane(1)
    s_out.column(0)
    grads_here()
    s_out.corner(3)
    s_out.plane(2)
    s_out.column(1)
    cotangent(0)
    hidden_grads(s_back.order(0))
    g_grad.sent()
    input_grads(0)
    s_out.plane(3)
    s_out.column(2)
    cotangent(1)
    hidden_grads(s_back.order(1))
    input_grads(1)
    s_back.corner(0)
    cotangent(2)
    hidden_grads(s_back.order(2))
    input_grads(2)
    s_out.column(3)
    add_hidden()
    s_back.corner(1)
    s_back.plane(0)
    cotangent(3)
    hidden_grads(s_back.order(3))
    input_grads(3)
    small_start()
    s_back.corner(2)
    s_back.plane(1)
    s_back.column(0)
    weight_grads(0)
    g_small.slot(1)
    s_back.corner(3)
    s_back.plane(2)
    s_back.column(1)
    weight_grads(1)
    g_small.slot(2)
    s_back.plane(3)
    s_back.column(2)
    weight_grads(2)
    g_small.slot(3)
    weight_grads(3)

    g_small.slot(4)
    other = (1 - p.y) * 2 + p.c
    partner = p.device(p.z, 0, 1 - p.c)
    keeping = pltpu.make_async_copy(own_grad, rows_out.at[quarter], tkeep)

    def tremote(k, i, src, where, device):
        rows = pl.ds(k * upper, upper)
        return pltpu.make_async_remote_copy(
            src_ref=src.at[rows], dst_ref=rows_out.at[where, rows], send_sem=tsend.at[k, i],
            recv_sem=trecv.at[k, i], device_id=device, device_id_type=MESH,
        )

    across = [tremote(k, 0, own_grad, quarter, p.device(p.z, 2, p.c)) for k in range(2)]
    beside = [tremote(k, 1, own_grad, quarter, partner) for k in range(2)]
    relay = [tremote(k, 2, rows_out.at[other], other, partner) for k in range(2)]
    for k in range(2):
        s_back.parts[k].column(line - 1)

        @pl.loop(k * upper // 16, (k + 1) * upper // 16)
        def _(i):
            rows = pl.ds(pl.multiple_of(i * 16, 16), 16)
            values, inverse = unit_of(rows)
            unit = values * inverse
            upstream = total[rows] * gain[...]
            mean = jnp.mean(upstream * unit, axis=-1, keepdims=True)
            grad = out_grad[rows].astype(f32) + inverse * (upstream - unit * mean)
            own_grad[rows] = grad.astype(bf16)

        across[k].start()
        beside[k].start()
    keeping.start()
    g_small.slot(5)
    for step in range(line):
        g_small.done(step)
    gain_out[...] = jnp.sum(small_all[:, first:], axis=0)
    gg_out[...] = small_all[:, pl.ds(me // 2, 1)].reshape(gg_out.shape)
    for k in range(2):
        across[k].wait_recv()
        relay[k].start()
    g_small.sent()
    s_out.sent()
    for step in range(line):
        s_back.given(step)
    s_back.sent()
    for k in range(2):
        beside[k].wait_recv()
        relay[k].wait_recv()
        for copy in (across[k], beside[k], relay[k]):
            copy.wait_send()
    keeping.wait()


def whole_layer(ids, probs, hidden, gain, out_grad, w_gate, w_up, w_down, capacity):
    line = lax.axis_size("dp") // 2
    devices, quarters = lax.axis_size(AXES), lax.axis_size("tensor")
    own, width = out_grad.shape
    inner = w_gate.shape[1]
    groups, gtok, gslots = devices // 4, own * 4, capacity * 4
    slots = groups * gslots
    small_rows = devices * own // 128 + width // 128
    anywhere, vmem = pl.BlockSpec(memory_space=pl.ANY), pl.BlockSpec(memory_space=pltpu.VMEM)
    shape = jax.ShapeDtypeStruct
    dma = pltpu.SemaphoreType.DMA
    passing = [
        pltpu.VMEM((line, 4, own, width), bf16),
        pltpu.VMEM((2, 2, own // 2, width), bf16),
        pltpu.VMEM((line, own, width), bf16),
        pltpu.VMEM((line, own, width), bf16),
        pltpu.VMEM((line, own, width), bf16),
        pltpu.VMEM((line, own, width), bf16),
        pltpu.VMEM((2, own, width), bf16),
        pltpu.VMEM((2, own, width), bf16),
    ]
    return pl.pallas_call(
        functools.partial(layer_kernel, line, ids.shape[0], capacity),
        out_shape=[
            pltpu.VMEM((own, width), bf16),
            pltpu.VMEM((quarters, own, width), bf16),
            pltpu.VMEM((devices, 128), f32),
            pltpu.VMEM((width // 128, 128), f32),
            pltpu.VMEM(w_gate.shape, bf16),
            pltpu.VMEM(w_up.shape, bf16),
            pltpu.VMEM(w_down.shape, bf16),
            shape((devices, own, width), bf16),
        ],
        in_specs=[vmem, vmem, anywhere, vmem, vmem, anywhere, anywhere, anywhere],
        out_specs=[vmem] * 7 + [anywhere],
        scratch_shapes=[
            pltpu.VMEM((128, 128), f32),
            pltpu.VMEM((own, 128), f32),
            pltpu.VMEM((devices, own, 128), f32),
            pltpu.VMEM((devices, own, width), bf16),
            pltpu.VMEM((own, width), bf16),
            pltpu.VMEM((own, width), bf16),
            pltpu.VMEM((slots, width), bf16),
            pltpu.VMEM((slots, width), bf16),
            pltpu.VMEM((8, own, width), bf16),
            pltpu.VMEM((groups, gtok, gslots), bf16),
            pltpu.VMEM((slots, inner), f32),
            pltpu.VMEM((slots, inner), f32),
            pltpu.VMEM((slots, inner), bf16),
            pltpu.VMEM((slots, inner), bf16),
            pltpu.VMEM((slots, inner), bf16),
            pltpu.VMEM((2 * gslots, 128), f32),
            pltpu.VMEM((8, width), f32),
            pltpu.VMEM((small_rows, 128), f32),
            pltpu.VMEM((devices, small_rows, 128), f32),
            pltpu.VMEM((own, width), f32),
            pltpu.VMEM((own, width), bf16),
        ] + passing + passing + [
            dma((3, 12, line)),
            dma((6, 9, line)),
            dma((6,)),
            dma((4, 12, line)),
            dma((4,)),
            dma,
            dma((2, 3)),
            dma((2, 3)),
            dma,
        ],
        compiler_params=pltpu.CompilerParams(
            collective_id=0, has_side_effects=True, vmem_limit_bytes=53 * 2**20
        ),
        name="layer",
    )(ids, probs, hidden, gain, out_grad, w_gate, w_up, w_down)


def finish_kernel(
    layer, rows, gg, gain_sum, gate_wgrad, up_wgrad, down_wgrad, ids, probs, gain,
    layer_out, rows_out, gate_grad, gain_grad, gate_out, up_out, down_out, sems,
):
    pairs = [
        (layer, layer_out), (rows, rows_out), (gate_wgrad, gate_out), (up_wgrad, up_out),
        (down_wgrad, down_out),
    ]
    copies = []
    for a, b in pairs:
        count = a.shape[0] // 4
        for i in range(4):
            part = pl.ds(i * count, count)
            copies.append(pltpu.make_async_copy(a.at[part], b.at[part], sems.at[len(copies)]))
    for copy in copies:
        copy.start()
    own = ids.shape[1]
    tensor, dp = lax.axis_index("tensor"), lax.axis_index("dp")
    odd = (dp * 4 + tensor) % 2 == 1
    found = jnp.where(odd, gg[:, own:2 * own], gg[:, 0:own])
    device = lax.broadcasted_iota(jnp.int32, found.shape, 0)
    for k in range(ids.shape[0]):
        hit = device == ids[k:k + 1]
        value = jnp.sum(jnp.where(hit, found, 0.0), axis=0, keepdims=True)
        gate_grad[k:k + 1] = value / probs[k:k + 1]
    gain_grad[...] = gain_sum[...] / gain[...]
    for copy in copies:
        copy.wait()


def finish(*arrays):
    layer, rows, gg, gain_sum, gate_wgrad, up_wgrad, down_wgrad, ids, probs, gain = arrays
    anywhere, vmem = pl.BlockSpec(memory_space=pl.ANY), pl.BlockSpec(memory_space=pltpu.VMEM)
    return pl.pallas_call(
        finish_kernel,
        out_shape=[
            jax.ShapeDtypeStruct(a.shape, a.dtype)
            for a in (layer, rows, probs, gain, gate_wgrad, up_wgrad, down_wgrad)
        ],
        in_specs=[anywhere, anywhere, vmem, vmem, anywhere, anywhere, anywhere, vmem, vmem, vmem],
        out_specs=[anywhere, anywhere, vmem, vmem, anywhere, anywhere, anywhere],
        scratch_shapes=[pltpu.SemaphoreType.DMA((20,))],
        compiler_params=pltpu.CompilerParams(vmem_limit_bytes=4 * 2**20),
        name="finish",
    )(*arrays)


def per_device_whole(
    hidden, norm_gain, expert_ids, gate_probs, out_grad, gate_weight, up_weight, down_weight
):
    own_count, width = out_grad.shape
    top_count = expert_ids.shape[1]
    capacity = 2 * own_count * top_count // lax.axis_size(AXES)
    ids, probs = expert_ids.T, gate_probs.T
    *results, _ = whole_layer(
        ids, probs, hidden, norm_gain[None], out_grad, gate_weight[0], up_weight[0],
        down_weight[0], capacity,
    )
    layer_out, input_grad, gate_grad, gain_grad, gate_wgrad, up_wgrad, down_grad = finish(
        *results, ids, probs, norm_gain.reshape(-1, 128)
    )
    return (
        layer_out, input_grad.reshape(hidden.shape), gate_grad.T, gain_grad.reshape(width),
        gate_wgrad[None], up_wgrad[None], down_grad[None],
    )


def choose_form(*arrays):
    hidden, _, expert_ids, _, out_grad = arrays[:5]
    devices = lax.axis_size(AXES)
    capacity = 2 * out_grad.shape[0] * expert_ids.shape[1] // devices
    fits = devices <= 32 and capacity * 4 == 128 and out_grad.shape[0] == 64
    return (per_device_whole if fits else per_device)(*arrays)


def solution(mesh):
    rows, wide = P(AXES, None), P(AXES, None, None)
    in_specs = (P("dp", None), P(), rows, rows, rows, wide, wide, wide)
    out_specs = (rows, P("dp", None), rows, P(), wide, wide, wide)
    return jax.shard_map(
        choose_form, mesh=mesh, in_specs=in_specs, out_specs=out_specs, check_vma=False
    )
```
